128 devices in a mesh: dom: 16 (over z, y), tile: 8 (over x, core).
Axes of the slice: x: 4, y: 4, z: 4, core: 2. Of those that a mesh axis runs over, the one named last changes fastest.
Arguments:
- dof_values: float32 [20, 9, 65536], P(None, None, ('dom', 'tile')), may hold values from -6 to 6
- density: float32 [65536], P(('dom', 'tile')), may hold values from 1 to 3
- lame_lambda: float32 [65536], P(('dom', 'tile')), may hold values from 0.5 to 2
- shear_modulus: float32 [65536], P(('dom', 'tile')), may hold values from 0 to 3, as said below
- jacobian: float32 [3, 3, 65536], P(None, None, ('dom', 'tile')), may hold values from -4 to 4
- normals: float32 [4, 3, 65536], P(None, None, ('dom', 'tile')), may hold values from -4 to 4
- face_scale: float32 [4, 65536], P(None, ('dom', 'tile')), may hold values from 0.5 to 2
- derivative: float32 [3, 20, 20], replicated, may hold values from -1.25 to 1.25
- face_proj: float32 [4, 10, 20], replicated, may hold values from -1.25 to 1.25
- lift_matrix: float32 [4, 20, 10], replicated, may hold values from -2 to 2
- neighbour: int32 [4, 65536], P(None, ('dom', 'tile')), may hold values from 0 to 2399, as said below
- send_face: int32 [1408, 32], P(('dom', 'tile')), may hold values from 0 to 2047
- cluster: int32 [65536], P(('dom', 'tile')), may hold values 0 or 1
- sea_face: int32 [16384, 64], P(('dom', 'tile')), may hold values from -1 to 511, as said below
- sea_cell: int32 [16384, 64], P(('dom', 'tile')), may hold values from 0 to 32767
- height: float32 [1024, 4096], P('dom', 'tile'), may hold values from -4 to 4
- momentum: float32 [2, 1024, 4096], P(None, 'dom', 'tile'), may hold values from -4 to 4
- ocean_depth: float32 [1024, 4096], P('dom', 'tile'), may hold values from 0.5 to 2
Outputs:
- dof_out: float32 [20, 9, 65536], P(None, None, ('dom', 'tile'))
- height_out: float32 [1024, 4096], P('dom', 'tile')
- momentum_out: float32 [2, 1024, 4096], P(None, 'dom', 'tile')
The draws below stay inside these ranges and needn't reach their ends.
Inputs may be any that keep to these rules, and one draw needn't show every extreme that they name: `neighbour`: an entry below 2048 names local face f * 512 + e of the same device; an entry 2048 + n * 32 + c names slot c of what partner n sends to this device. `send_face`: row s * 11 + n lists local faces f * 512 + e of device s sent to its partner n. `sea_face`: row s * 128 + d lists local elements of device s whose bottom face lies under tile d; rows are live only where (d - s) mod 128 is 0, 1, 8 or 64; live entries come first, the rest are -1; each device's own row is full. `sea_cell`: row d * 128 + s gives, for each slot of device s, the cell i * 512 + j of tile d. `shear_modulus`: zero in a tenth of the elements or so, else positive.
All inputs are finite; a program needn't handle non-finite values. No bound on the sum of `cluster` on one device may be relied on, other than what follows from the above.
Results may differ from the reference program's by a relative error of at most 0.0003.
Values sent between devices are 32-bit elements; how exact they have to be, the bound alone decides.
A program may use at most 64 MiB of HBM per device.

```python
import math
import jax
import jax.numpy as jnp
from jax import lax

BASIS = 20
FACE_BASIS = 10
QUANT = 9
NBR = 11
E_DEV = 512
CAP = 32
UCAP = 64
GX = 64
GY = 512
STEPS = 4
ELEMS = 65536
NGX = 1024
NGY = 4096
N_DOM = 16
N_TILE = 8
DEVICES = 128


def draw_shear_modulus(key, part):
    key_size, key_solid = jax.random.split(jax.random.fold_in(key, 11))
    magnitude = jnp.exp(jax.random.uniform(key_size, (ELEMS,), jnp.float32, jnp.log(0.3), jnp.log(3.0)))
    is_solid = jax.random.uniform(key_solid, (ELEMS,), jnp.float32) >= 0.1
    return jnp.where(is_solid, magnitude, 0.0).astype(jnp.float32)


def draw_neighbour(key, part):
    key_kind, key_local, key_remote = jax.random.split(jax.random.fold_in(key, 23), 3)
    local_faces = 4 * E_DEV
    remote_slots = NBR * CAP
    choose_remote = jax.random.randint(key_kind, (4, ELEMS), 0, 8) == 0
    local_pick = jax.random.randint(key_local, (4, ELEMS), 0, local_faces)
    remote_pick = local_faces + jax.random.randint(key_remote, (4, ELEMS), 0, remote_slots)
    picked = jnp.where(choose_remote, remote_pick, local_pick)
    return picked.at[0, 0].set(local_faces + remote_slots - 1).at[1, 0].set(0).astype(jnp.int32)


def draw_sea_face(key, part):
    key_count, key_element = jax.random.split(jax.random.fold_in(key, 37))
    device_count = N_DOM * N_TILE
    row_count = device_count * device_count
    rows = jnp.arange(row_count)
    relative = (rows % device_count - rows // device_count) % device_count
    live_row = (relative == 1) | (relative == N_TILE) | (relative == device_count // 2)
    raw_count = jax.random.randint(key_count, (row_count,), 0, UCAP + 1)
    counts = jnp.where(live_row, raw_count * raw_count // UCAP, 0)
    counts = jnp.where(relative == 0, UCAP, counts)[:, None]
    slot_index = jnp.arange(UCAP)[None, :]
    element_pick = jax.random.randint(key_element, (row_count, UCAP), 0, E_DEV)
    return jnp.where(slot_index < counts, element_pick, -1).astype(jnp.int32)


def with_ends(drawn, own_key, least, top_value):
    extent = drawn.shape
    place = [jax.random.randint(jax.random.fold_in(own_key, axis), (), 0, extent[axis]) for axis in range(len(extent))]
    drawn = drawn.at[tuple(place)].set(least)
    longest = extent.index(max(extent))
    place[longest] = (place[longest] + 1) % extent[longest]
    return drawn.at[tuple(place)].set(top_value)


def steps_of(rng, extent, cuts, low, high):
    loudness, own = 1.0, jax.random.fold_in(rng, 6)
    for axis_at, shards_of in cuts:
        steps = jnp.exp(jax.random.uniform(jax.random.fold_in(own, axis_at), (shards_of,), jnp.float32, low / len(cuts), high / len(cuts)))
        loudness = loudness * jnp.repeat(steps, extent[axis_at] // shards_of).reshape([-1 if axis == axis_at else 1 for axis in range(len(extent))])
    return loudness


def scatter_about(own_key, dims, scale, bound, shards=(), kind=jnp.bfloat16):
    factor_of = steps_of(own_key, dims, shards, -0.22, 0.18) if shards else 1.0
    entries = jax.random.normal(own_key, dims, jnp.float32) * scale * factor_of
    return jnp.minimum(jnp.maximum(entries, -bound), bound).astype(kind)


def setup_inputs(seed: int = 0) -> dict:
    streams_of = jax.random.split(jax.random.key(seed), 19)
    dof_values = scatter_about(streams_of[0], (BASIS, QUANT, ELEMS), 1.0, 6.0, ((2, 128),), jnp.float32)
    density = jnp.clip(jnp.exp(math.log(3.0) - 1.0986123 * jax.random.uniform(streams_of[1], (ELEMS,), jnp.float32) ** steps_of(streams_of[1], (ELEMS,), ((0, 128),), -0.2, 0.2)), 1.0, 3.0)
    lame_lambda = jnp.clip(jnp.exp(math.log(2.0) - 1.3862944 * jax.random.uniform(streams_of[2], (ELEMS,), jnp.float32) ** steps_of(streams_of[2], (ELEMS,), ((0, 128),), -0.2, 0.2)), 0.5, 2.0)
    shear_modulus = draw_shear_modulus(jax.random.fold_in(streams_of[18], 71), 0)
    jacobian = scatter_about(streams_of[4], (3, 3, ELEMS), 0.7, 4.0, ((2, 128),), jnp.float32)
    normals = scatter_about(streams_of[5], (4, 3, ELEMS), 0.6, 4.0, ((2, 128),), jnp.float32)
    face_scale = jnp.clip(jnp.exp(math.log(2.0) - 1.3862944 * jax.random.uniform(streams_of[6], (4, ELEMS), jnp.float32) ** steps_of(streams_of[6], (4, ELEMS), ((1, 128),), -0.2, 0.2)), 0.5, 2.0)
    derivative = scatter_about(streams_of[7], (3, BASIS, BASIS), BASIS ** -0.5, 1.25, (), jnp.float32)
    face_proj = scatter_about(streams_of[8], (4, FACE_BASIS, BASIS), BASIS ** -0.5, 1.25, (), jnp.float32)
    lift_matrix = scatter_about(streams_of[9], (4, BASIS, FACE_BASIS), FACE_BASIS ** -0.5, 2.0, (), jnp.float32)
    neighbour = draw_neighbour(jax.random.fold_in(streams_of[18], 71), 0)
    send_face = with_ends(jax.random.randint(streams_of[11], (DEVICES * NBR, CAP), 0, 4 * E_DEV), jax.random.fold_in(streams_of[11], 1), 0, (4 * E_DEV) - 1).astype(jnp.int32)
    cluster = with_ends((jax.random.randint(streams_of[12], (ELEMS,), 0, 2) < 1).astype(jnp.int32), jax.random.fold_in(streams_of[12], 1), 0, 1)
    sea_face = draw_sea_face(jax.random.fold_in(streams_of[18], 71), 0)
    sea_cell = with_ends(jax.random.randint(streams_of[14], (DEVICES * DEVICES, UCAP), 0, GX * GY), jax.random.fold_in(streams_of[14], 1), 0, (GX * GY) - 1).astype(jnp.int32)
    height = scatter_about(streams_of[15], (NGX, NGY), 0.3, 4.0, ((0, 16), (1, 8)), jnp.float32)
    momentum = scatter_about(streams_of[16], (2, NGX, NGY), 0.3, 4.0, ((1, 16), (2, 8)), jnp.float32)
    ocean_depth = jnp.clip(jnp.exp(math.log(2.0) - 1.3862944 * jax.random.uniform(streams_of[17], (NGX, NGY), jnp.float32) ** steps_of(streams_of[17], (NGX, NGY), ((0, 16), (1, 8)), -0.2, 0.2)), 0.5, 2.0)
    return dict(dof_values=dof_values, density=density, lame_lambda=lame_lambda, shear_modulus=shear_modulus, jacobian=jacobian, normals=normals, face_scale=face_scale, derivative=derivative, face_proj=face_proj, lift_matrix=lift_matrix, neighbour=neighbour, send_face=send_face, cluster=cluster, sea_face=sea_face, sea_cell=sea_cell, height=height, momentum=momentum, ocean_depth=ocean_depth)


STRESS_PAIRS = ((0, 3, 5), (3, 1, 4), (5, 4, 2))
highest = lax.Precision.HIGHEST
step_size = 0.3
wave_rate = 0.45

def partner_offsets(tile_count, device_count):
    return [1, -1, 2, -2, tile_count, -tile_count, tile_count + 1, -(tile_count + 1), 2 * tile_count, -2 * tile_count, device_count // 2]

def time_derivative(values, derivative, jacobian, inv_density, lame_lambda, shear_modulus):
    gradient = jnp.einsum('dkb,bve->dkve', derivative, values, precision=highest)
    physical = jnp.einsum('dxe,dkve->xkve', jacobian, gradient, precision=highest)
    velocity_grad = [[physical[j, :, 6 + i] for j in range(3)] for i in range(3)]
    divergence = velocity_grad[0][0] + velocity_grad[1][1] + velocity_grad[2][2]

    def stress(i, j):
        mixed = shear_modulus * (velocity_grad[i][j] + velocity_grad[j][i])
        return lame_lambda * divergence + mixed if i == j else mixed
    acceleration = [inv_density * (physical[0, :, STRESS_PAIRS[i][0]] + physical[1, :, STRESS_PAIRS[i][1]] + physical[2, :, STRESS_PAIRS[i][2]]) for i in range(3)]
    return jnp.stack([stress(0, 0), stress(1, 1), stress(2, 2), stress(0, 1), stress(1, 2), stress(0, 2)] + acceleration, axis=1)

def predict(dof_values, derivative, jacobian, inv_density, lame_lambda, shear_modulus):
    integral = step_size * dof_values
    taylor_term = dof_values
    factor = step_size
    for k in range(1, 4):
        taylor_term = time_derivative(taylor_term, derivative, jacobian, inv_density, lame_lambda, shear_modulus)
        factor = factor * step_size / (k + 1)
        integral = integral + factor * taylor_term
    return integral

def face_traces(integral, face_proj):
    return jnp.einsum('fck,kve->cvfe', face_proj, integral, precision=highest)

def normal_operator(jump_value, normals, inv_density, lame_lambda, shear_modulus):
    direction = [normals[:, d, :] for d in range(3)]
    velocity_jump = [jump_value[:, 6 + d] for d in range(3)]
    normal_flow = velocity_jump[0] * direction[0] + velocity_jump[1] * direction[1] + velocity_jump[2] * direction[2]
    traction = [inv_density * (jump_value[:, STRESS_PAIRS[i][0]] * direction[0] + jump_value[:, STRESS_PAIRS[i][1]] * direction[1] + jump_value[:, STRESS_PAIRS[i][2]] * direction[2]) for i in range(3)]

    def stress(i, j):
        mixed = shear_modulus * (velocity_jump[i] * direction[j] + velocity_jump[j] * direction[i])
        return lame_lambda * normal_flow + mixed if i == j else mixed
    return jnp.stack([stress(0, 0), stress(1, 1), stress(2, 2), stress(0, 1), stress(1, 2), stress(0, 2)] + traction, axis=1)

def shallow_step(level, flow_x, flow_y, ocean_depth):
    padded_x = jnp.pad(flow_x, 1)
    padded_y = jnp.pad(flow_y, 1)
    spread = padded_x[2:, 1:-1] - padded_x[:-2, 1:-1] + (padded_y[1:-1, 2:] - padded_y[1:-1, :-2])
    level = level - 0.5 * wave_rate * spread
    padded_h = jnp.pad(level, 1)
    flow_x = flow_x - 0.5 * wave_rate * ocean_depth * (padded_h[2:, 1:-1] - padded_h[:-2, 1:-1])
    flow_y = flow_y - 0.5 * wave_rate * ocean_depth * (padded_h[1:-1, 2:] - padded_h[1:-1, :-2])
    return (level, flow_x, flow_y)

def split_blocks(array, device_count):
    shaped = array.reshape(array.shape[:-1] + (device_count, array.shape[-1] // device_count))
    return jnp.moveaxis(shaped, -2, 0)

def reference(dof_values, density, lame_lambda, shear_modulus, jacobian, normals, face_scale, derivative, face_proj, lift_matrix, neighbour, send_face, cluster, sea_face, sea_cell, height, momentum, ocean_depth):
    device_count = N_DOM * N_TILE
    offsets = jnp.array(partner_offsets(N_TILE, device_count), jnp.int32)
    partner_count = offsets.shape[0]
    element_blocks = (split_blocks(dof_values, device_count), split_blocks(density, device_count), split_blocks(lame_lambda, device_count), split_blocks(shear_modulus, device_count), split_blocks(jacobian, device_count))
    send_blocks = send_face.reshape(device_count, partner_count, CAP)
    sea_blocks = sea_face.reshape(device_count, device_count, UCAP)
    cell_blocks = sea_cell.reshape(device_count, device_count, UCAP)

    def first_pass(inputs):
        block_dofs, block_density, block_lame, block_shear, block_jacobian, block_send, block_sea = inputs
        inv_density = 1.0 / block_density
        integral = predict(block_dofs, derivative, block_jacobian, inv_density, block_lame, block_shear)
        traces = face_traces(integral, face_proj)
        face_table = traces.reshape(traces.shape[0] * traces.shape[1], -1)
        outgoing = jnp.take(face_table, block_send, axis=1)
        upward = traces[0, 8, 0]
        handed = jnp.where(block_sea >= 0, jnp.take(upward, jnp.maximum(block_sea, 0)), 0.0)
        return (outgoing, handed)
    outgoing_all, handed_all = lax.map(first_pass, element_blocks + (send_blocks, sea_blocks))
    receiver = jnp.arange(device_count, dtype=jnp.int32)
    source_index = (receiver[:, None] - offsets[None, :]) % device_count
    partner_index = jnp.broadcast_to(jnp.arange(partner_count, dtype=jnp.int32)[None, :], source_index.shape)
    picked = outgoing_all[source_index, :, partner_index, :]
    incoming_all = jnp.transpose(picked, (0, 2, 1, 3)).reshape(device_count, outgoing_all.shape[1], partner_count * CAP)
    arrived_all = jnp.transpose(handed_all, (1, 0, 2))

    def second_pass(inputs):
        block_dofs, block_density, block_lame, block_shear, block_jacobian, block_normals, block_scale, block_neighbour, block_cluster, incoming, arrived, block_cells = inputs
        inv_density = 1.0 / block_density
        integral = predict(block_dofs, derivative, block_jacobian, inv_density, block_lame, block_shear)
        traces = face_traces(integral, face_proj)
        face_table = traces.reshape(traces.shape[0] * traces.shape[1], -1)
        lookup = jnp.concatenate([face_table, incoming], axis=1)
        neighbour_trace = jnp.take(lookup, block_neighbour, axis=1).reshape(traces.shape)
        jump_value = neighbour_trace - traces
        wave_speed = jnp.sqrt((block_lame + 2.0 * block_shear) * inv_density)
        correction = 0.5 * block_scale * (normal_operator(jump_value, block_normals, inv_density, block_lame, block_shear) + wave_speed * jump_value)
        lifted = jnp.einsum('fkc,cvfe->kve', lift_matrix, correction, precision=highest)
        volume = time_derivative(integral, derivative, block_jacobian, inv_density, block_lame, block_shear)
        updated = block_dofs + volume + lifted
        block_out = jnp.where(block_cluster[None, None, :] == 1, updated, block_dofs)
        uplift = jnp.zeros((GX * GY,), jnp.float32).at[block_cells.reshape(-1)].add(arrived.reshape(-1)).reshape(GX, GY)
        return (block_out, uplift)
    second_inputs = element_blocks + (split_blocks(normals, device_count), split_blocks(face_scale, device_count), split_blocks(neighbour, device_count), split_blocks(cluster, device_count), incoming_all, arrived_all, cell_blocks)
    out_blocks, uplift_tiles = lax.map(second_pass, second_inputs)
    dof_out = jnp.moveaxis(out_blocks, 0, -2).reshape(dof_values.shape)
    uplift = uplift_tiles.reshape(N_DOM, N_TILE, GX, GY).transpose(0, 2, 1, 3).reshape(height.shape)
    level = height + uplift
    flow_x, flow_y = (momentum[0], momentum[1])
    for k in range(STEPS):
        level, flow_x, flow_y = shallow_step(level, flow_x, flow_y, ocean_depth)
    return (dof_out, level, jnp.stack([flow_x, flow_y]))
```

```python
import functools

import jax
import jax.numpy as jnp
from jax import lax
from jax.experimental import pallas as pl
from jax.experimental.pallas import tpu as pltpu
from jax.sharding import PartitionSpec as P

STEPS = 4
STRESS_PAIRS = ((0, 3, 5), (3, 1, 4), (5, 4, 2))
STRESS_ORDER = ((0, 0), (1, 1), (2, 2), (0, 1), (1, 2), (0, 2))
STEP_SIZE = 0.3
WAVE_RATE = 0.45
MESH = pl.DeviceIdType.MESH
F32 = jnp.float32
BF16 = jnp.bfloat16

B = 20
BP = 24
Q = 9
E = 512
CH = 256
LANES = 128
TILES = 16
RTILES = 3
SLOTS = 32
ROW0 = 16
ROWS = 96


def partner_offsets(tile_count, device_count):
    t = tile_count
    return [1, -1, 2, -2, t, -t, t + 1, -(t + 1), 2 * t, -2 * t, device_count // 2]


def split(x):
    high = x.astype(BF16).astype(F32)
    return high, x - high


def stacked(x):
    high, low = split(x)
    pad = jnp.zeros((8,) + x.shape[1:], F32)
    parts = [high, low, high]
    if (3 * x.shape[0]) % 16:
        parts.append(pad)
    return jnp.concatenate(parts, axis=0).astype(BF16)


def kernel(
    n_dom,
    n_tile,
    dof,
    density,
    lame,
    shear,
    jac,
    nrm,
    fscale,
    deriv,
    fproj,
    lift,
    nbr,
    send,
    cluster,
    sea_face,
    sea_cell,
    height,
    momentum,
    depth,
    dof_out,
    height_out,
    momentum_out,
    x_ref,
    base,
    out,
    tab,
    tab2,
    otail,
    acc,
    amat,
    lmat,
    sidx,
    nbr8,
    coef,
    msg,
    msg_in,
    tails,
    hand,
    hand_in,
    flow,
    flow_l,
    flow_r,
    level,
    level_l,
    level_r,
    local_sem,
    send_sem,
    recv_sem,
):
    devices = n_dom * n_tile
    dom, tile = lax.axis_index("dom"), lax.axis_index("tile")
    me = dom * n_tile + tile
    offsets = partner_offsets(n_tile, devices)
    greet = offsets + [n_tile - 1, -(n_tile - 1)]

    def device(offset):
        target = lax.rem(me + (offset + devices), devices)
        return (target // n_tile, lax.rem(target, n_tile))

    barrier = pltpu.get_barrier_semaphore()
    for o in greet:
        pl.semaphore_signal(barrier, inc=1, device_id=device(o), device_id_type=MESH)

    x_copy = pltpu.make_async_copy(dof, x_ref, local_sem.at[0])
    x_copy.start()
    grid_copies = []
    for t in range(4):
        lanes = slice(t * LANES, (t + 1) * LANES)
        rows = slice(ROW0, ROW0 + 64)
        grid_copies += [
            pltpu.make_async_copy(
                momentum.at[:, :, lanes], flow.at[0:2, t, rows, :], local_sem.at[1 + t]
            ),
            pltpu.make_async_copy(depth.at[:, lanes], flow.at[2, t, rows, :], local_sem.at[5 + t]),
            pltpu.make_async_copy(height.at[:, lanes], level.at[t, rows, :], local_sem.at[9 + t]),
        ]
    for c in grid_copies:
        c.start()

    lane = lax.broadcasted_iota(jnp.int32, (8, LANES), 1)
    sub = lax.broadcasted_iota(jnp.int32, (8, LANES), 0)

    amat[...] = jnp.zeros_like(amat)
    lmat[...] = jnp.zeros_like(lmat)
    for d in range(3):
        amat[d * BP : d * BP + B, 0:B] = deriv[d]
    for f in range(4):
        for c in range(10):
            row = fproj[c, f : f + 1, :]
            lrow = lift[c, f : f + 1, :]
            if c < 8:
                amat[72 + f * 8 + c : 73 + f * 8 + c, 0:B] = row
                lmat[f * 8 + c : f * 8 + c + 1, 0:B] = lrow
            else:
                k = 32 + f * 2 + c - 8
                amat[72 + k : 73 + k, 0:B] = row
                lmat[k : k + 1, 0:B] = lrow
                for r in range(4):
                    k = 112 + f * 8 + r * 2 + c - 8
                    amat[k : k + 1, 0:B] = row
    a_high, a_low = split(amat[...])
    a_all = a_high + pltpu.roll(a_high, BP, 1) + pltpu.roll(a_low, 2 * BP, 1)
    a_all = a_all.astype(BF16)[:, 0:80]
    l_high, l_low = split(jnp.transpose(lmat[...]))
    l_high, l_low = l_high[0:BP], l_low[0:BP]
    l_all = l_high + pltpu.roll(l_high, 40, 1) + pltpu.roll(l_low, 80, 1)
    l_all = l_all.astype(BF16)[:, 0:120]

    inv_den = 1.0 / density[...]
    speed = jnp.sqrt((lame[...] + 2.0 * shear[...]) * inv_den)
    half = 0.5 * fscale[...]
    scaled = [half * nrm[j] for j in range(3)]
    coefs = (
        scaled
        + [shear[...] * s for s in scaled]
        + [inv_den * s for s in scaled]
        + [half * speed]
    )
    for k, c in enumerate(coefs):
        for f in range(4):
            coef[k, 2 * f : 2 * f + 2, :] = jnp.broadcast_to(c[f : f + 1, :], (2, E))
    for f in range(4):
        nbr8[2 * f : 2 * f + 2, :] = jnp.broadcast_to(nbr[f : f + 1, :], (2, E))
    sidx[...] = jnp.zeros_like(sidx)
    sidx[0:11, 0:SLOTS] = send[...]

    x_copy.wait()

    def predictor(i, _):
        off = pl.multiple_of(i * CH, CH)
        cut = pl.ds(off, CH)
        rho = 1.0 / density[:, cut]
        lam = lame[:, cut]
        mu = shear[:, cut]
        mu2 = mu + mu
        jc = [[jac[d, x : x + 1, cut] for x in range(3)] for d in range(3)]

        def combine(g):
            def phys(x, v):
                return (
                    jc[0][x] * g[0:BP, v * CH : (v + 1) * CH]
                    + jc[1][x] * g[BP : 2 * BP, v * CH : (v + 1) * CH]
                    + jc[2][x] * g[2 * BP : 3 * BP, v * CH : (v + 1) * CH]
                )

            vg = [[phys(j, 6 + i) for j in range(3)] for i in range(3)]
            div = lam * (vg[0][0] + vg[1][1] + vg[2][2])
            res = [div + mu2 * vg[i][i] for i in range(3)]
            res += [mu * (vg[i][j] + vg[j][i]) for i, j in STRESS_ORDER[3:]]
            for i in range(3):
                s = STRESS_PAIRS[i]
                res.append(rho * (phys(0, s[0]) + phys(1, s[1]) + phys(2, s[2])))
            return res

        pad = jnp.zeros((BP - B, CH), F32)
        start = [jnp.concatenate([x_ref[v, :, cut], pad], axis=0) for v in range(Q)]
        term = start
        integral = [STEP_SIZE * w for w in term]
        factor = STEP_SIZE
        for k in range(1, 4):
            right = stacked(jnp.concatenate(term, axis=1))
            term = combine(jnp.dot(a_all[0:72], right, preferred_element_type=F32))
            factor = factor * STEP_SIZE / (k + 1)
            integral = [s + factor * w for s, w in zip(integral, term)]
        right = stacked(jnp.concatenate(integral, axis=1))
        g = jnp.dot(a_all, right, preferred_element_type=F32)
        volume = combine(g)
        for v in range(Q):
            cols = slice(v * CH, (v + 1) * CH)
            base[v, :, cut] = start[v] + volume[v]
            for f in range(4):
                here = pl.ds(pl.multiple_of(f * E + off, LANES), CH)
                tab[v, :, here] = g[72 + f * 8 : 80 + f * 8, cols]
                tab[Q + v, :, here] = g[112 + f * 8 : 120 + f * 8, cols]
            otail[v, :, cut] = g[104:112, cols]
        for f in range(4):
            here = pl.ds(pl.multiple_of(f * E + off, LANES), CH)
            pair = lax.broadcasted_iota(jnp.int32, (8, CH), 0) // 2
            for j in range(3):
                packed = g[112 + f * 8 : 120 + f * 8, 4 * j * CH : (4 * j + 1) * CH]
                for q in range(1, 4):
                    if 4 * j + q < Q:
                        v = 4 * j + q
                        more = g[112 + f * 8 : 120 + f * 8, v * CH : (v + 1) * CH]
                        packed = jnp.where(pair == q, more, packed)
                tab2[j, :, here] = packed
        return 0

    lax.fori_loop(0, E // CH, predictor, 0)

    shift = lax.rem(devices - me, devices)
    ups = [jnp.broadcast_to(tab[8, 0:1, t * LANES : (t + 1) * LANES], (8, LANES)) for t in range(4)]
    slots = []
    for r in range(8):
        idx = sea_face[r * 8 : r * 8 + 8, :]
        at, which = idx & (LANES - 1), idx >> 7
        val = jnp.zeros((8, LANES), F32)
        for t in range(4):
            val = jnp.where(which == t, jnp.take_along_axis(ups[t], at, axis=1), val)
        slots.append(val)
    handed = pltpu.roll(jnp.concatenate(slots, axis=0), shift, 1)
    zeros64 = jnp.zeros((64, LANES), F32)
    hand[...] = jnp.transpose(jnp.concatenate([handed, zeros64], axis=0))

    pl.semaphore_wait(barrier, len(greet))

    copies = []

    def push(src, dst, offset):
        k = len(copies)
        copy = pltpu.make_async_remote_copy(
            src_ref=src,
            dst_ref=dst,
            send_sem=send_sem.at[k],
            recv_sem=recv_sem.at[k],
            device_id=device(offset),
            device_id_type=MESH,
        )
        copy.start()
        copies.append(copy)
        return copy

    hand_offsets = (1, n_tile, devices // 2)
    hand_copies = []
    for k, o in enumerate(hand_offsets):
        row = o // 8 * 8
        hand_copies.append(push(hand.at[row : row + 8, :], hand_in.at[k], o))

    def gather(sources, idx, tiles, start):
        at, which = idx & (LANES - 1), idx >> 7
        res = list(start)
        for t in tiles:
            mask = which == t
            for k, source in enumerate(sources):
                val = jnp.take_along_axis(source[:, t * LANES : (t + 1) * LANES], at, axis=1)
                res[k] = val if res[k] is None else jnp.where(mask, val, res[k])
        return res

    block = lane // SLOTS
    places = [(v // 4, v % 4) for v in range(Q)] + [(2, 1 + j) for j in range(3)]
    dg_copies = []
    for p in range(RTILES):
        members = [n for n in range(4 * p, 4 * p + 4) if n < len(offsets)]
        idx = jnp.zeros((8, LANES), jnp.int32)
        for n in members:
            row = jnp.broadcast_to(sidx[n : n + 1, :], (8, LANES))
            idx = jnp.where(block == n % 4, pltpu.roll(row, SLOTS * (n % 4), 1), idx)
        sources = [tab.at[v] for v in range(Q)] + [tab2.at[j] for j in range(3)]
        got = gather(sources, idx, range(TILES), [None] * 12)
        for n in members:
            for r in range(3):
                packed = None
                for k, (pr, pb) in enumerate(places):
                    if pr != r:
                        continue
                    turn = (SLOTS * (pb - n % 4)) % LANES
                    val = pltpu.roll(got[k], turn, 1) if turn else got[k]
                    packed = val if packed is None else jnp.where(block == pb, val, packed)
                msg[n, r * 8 : r * 8 + 8, :] = packed
        for n in members:
            dg_copies.append(push(msg.at[n], msg_in.at[n], offsets[n]))

    for c in grid_copies:
        c.wait()

    def halos(ring, left, right):
        lead = (slice(None),) * (len(ring.shape) - 3)
        top, low = slice(ROW0, ROW0 + 8), slice(ROW0 + 56, ROW0 + 64)
        above, below = slice(ROW0 - 8, ROW0), slice(ROW0 + 64, ROW0 + 72)
        body = slice(ROW0, ROW0 + 64)
        cols = slice(0, 4)
        res = []
        for offset, src, dst in (
            (-n_tile, ring.at[lead + (cols, top)], ring.at[lead + (cols, below)]),
            (n_tile, ring.at[lead + (cols, low)], ring.at[lead + (cols, above)]),
            (-1, ring.at[lead + (0, body)], right.at[lead + (body,)]),
            (1, ring.at[lead + (3, body)], left.at[lead + (body,)]),
            (-n_tile - 1, ring.at[lead + (0, top)], right.at[lead + (below,)]),
            (-n_tile + 1, ring.at[lead + (3, top)], left.at[lead + (below,)]),
            (n_tile - 1, ring.at[lead + (0, low)], right.at[lead + (above,)]),
            (n_tile + 1, ring.at[lead + (3, low)], left.at[lead + (above,)]),
        ):
            res.append(push(src, dst, offset))
        return res

    flow_copies = halos(flow, flow_l, flow_r)

    def local_gather(et, _):
        off = pl.multiple_of(et * LANES, LANES)
        for f in range(4):
            idx = jnp.broadcast_to(nbr8[2 * f : 2 * f + 1, pl.ds(off, LANES)], (8, LANES))
            got = gather([tab.at[v] for v in range(Q)], idx, range(TILES), [None] * Q)
            for v in range(Q):
                acc[v, :, pl.ds(pl.multiple_of(f * E + off, LANES), LANES)] = got[v]
        idx = nbr8[:, pl.ds(off, LANES)]
        got = gather([tab.at[Q + v] for v in range(Q)], idx, range(TILES), [None] * Q)
        for v in range(Q):
            acc[v, :, pl.ds(pl.multiple_of(4 * E + off, LANES), LANES)] = got[v]
        return 0

    lax.fori_loop(0, 2, local_gather, 0)

    for c in hand_copies:
        c.wait_recv()
    back = (0, devices - 1, devices - n_tile, devices // 2)
    cells = pltpu.roll(sea_cell[...], shift, 1)
    cells_t = jnp.transpose(
        jnp.concatenate([cells, jnp.zeros((64, LANES), jnp.int32)], axis=0).astype(F32)
    ).astype(jnp.int32)
    values = [hand[0:1, :]]
    for k, o in enumerate(hand_offsets):
        values.append(hand_in[k, o % 8 : o % 8 + 1, :])
    row_ids = lax.broadcasted_iota(jnp.int32, (64, LANES), 0)
    highs, lows = [], []
    for k in range(0, 4, 2):
        pair_v = values[k] + pltpu.roll(values[k + 1], 64, 1)
        pair_c = cells_t[back[k] : back[k] + 1, :] + pltpu.roll(
            cells_t[back[k + 1] : back[k + 1] + 1, :], 64, 1
        )
        v_high, v_low = split(pair_v)
        here = row_ids == jnp.broadcast_to(pair_c >> 9, (64, LANES))
        highs.append(jnp.where(here, v_high, 0.0))
        lows.append(jnp.where(here, v_low, 0.0))
    left = jnp.concatenate(
        [jnp.concatenate(highs, axis=1), jnp.concatenate(lows, axis=1)], axis=0
    ).astype(BF16)
    col_ids = lax.broadcasted_iota(jnp.int32, (64, E), 1)
    picks = []
    for k in range(4):
        column = jnp.broadcast_to(cells[:, back[k] : back[k] + 1] & (E - 1), (64, E))
        picks.append(jnp.where(col_ids == column, 1.0, 0.0).astype(BF16))
    lifted = jnp.dot(left, jnp.concatenate(picks, axis=0), preferred_element_type=F32)
    for t in range(4):
        lanes = slice(t * LANES, (t + 1) * LANES)
        level[t, ROW0 : ROW0 + 64, :] += lifted[0:64, lanes] + lifted[64:128, lanes]
    level_copies = halos(level, level_l, level_r)

    lax.fori_loop(2, 4, local_gather, 0)

    for c in flow_copies:
        c.wait()
    above_ok = jnp.where(dom > 0, 1.0, 0.0)
    below_ok = jnp.where(dom < n_dom - 1, 1.0, 0.0)
    right_ok = jnp.where(tile < n_tile - 1, 1.0, 0.0)
    left_ok = jnp.where(tile > 0, 1.0, 0.0)
    span = slice(ROW0 - 8, ROW0 + 72)
    lane80 = lax.broadcasted_iota(jnp.int32, (80, LANES), 1)
    row80 = lax.broadcasted_iota(jnp.int32, (80, LANES), 0)
    row_ok = jnp.where(row80 < 8, above_ok, jnp.where(row80 >= 72, below_ok, 1.0))
    side_ok = row_ok * jnp.where(lane80 < 64, right_ok, left_ok)

    def close(ring, left, right, scale):
        for t in range(4):
            ring[t, ROW0 - 8 : ROW0, :] = ring[t, ROW0 - 8 : ROW0, :] * above_ok
            ring[t, ROW0 + 64 : ROW0 + 72, :] = ring[t, ROW0 + 64 : ROW0 + 72, :] * below_ok
        ring[4, span, :] = jnp.where(lane80 < 64, right[span, :], left[span, :]) * side_ok
        if scale is not None:
            for t in range(5):
                ring[t, span, :] = ring[t, span, :] * scale

    c0 = 0.5 * WAVE_RATE
    for k in range(3):
        close(flow.at[k], flow_l.at[k], flow_r.at[k], c0 if k == 2 else None)
    for c in level_copies:
        c.wait()
    close(level, level_l, level_r, None)
    for ring in (flow.at[0], level):
        for t in range(5):
            ring[t, 0:8, :] = jnp.zeros((8, LANES), F32)
            ring[t, ROWS - 8 : ROWS, :] = jnp.zeros((8, LANES), F32)
    up, down = slice(ROW0 - 9, ROW0 + 71), slice(ROW0 - 7, ROW0 + 73)

    def across(ring):
        vals = [ring[t, span, :] for t in range(5)]
        fwd = [pltpu.roll(x, LANES - 1, 1) for x in vals]
        bwd = [pltpu.roll(x, 1, 1) for x in vals]
        res = []
        for t in range(5):
            nxt = jnp.where(lane80 == LANES - 1, fwd[(t + 1) % 5], fwd[t])
            prv = jnp.where(lane80 == 0, bwd[(t + 4) % 5], bwd[t])
            res.append(nxt - prv)
        return res

    def wave(_, carry):
        diff = across(flow.at[1])
        for t in range(5):
            spread = (flow[0, t, down, :] - flow[0, t, up, :]) + diff[t]
            ok = side_ok if t == 4 else row_ok
            level[t, span, :] = level[t, span, :] - (c0 * ok) * spread
        diff = across(level)
        for t in range(5):
            g = flow[2, t, span, :]
            flow[0, t, span, :] = flow[0, t, span, :] - g * (level[t, down, :] - level[t, up, :])
            flow[1, t, span, :] = flow[1, t, span, :] - g * diff[t]
        return carry

    lax.fori_loop(0, STEPS, wave, 0)
    out_copies = []
    for t in range(4):
        lanes = slice(t * LANES, (t + 1) * LANES)
        rows = slice(ROW0, ROW0 + 64)
        out_copies += [
            pltpu.make_async_copy(
                flow.at[0:2, t, rows, :], momentum_out.at[:, :, lanes], local_sem.at[1 + t]
            ),
            pltpu.make_async_copy(
                level.at[t, rows, :], height_out.at[:, lanes], local_sem.at[9 + t]
            ),
        ]
    for c in out_copies:
        c.start()

    for c in dg_copies:
        c.wait_recv()
    for p in range(RTILES):
        members = [n for n in range(4 * p, 4 * p + 4) if n < len(offsets)]
        cols = slice((TILES + p) * LANES, (TILES + p + 1) * LANES)
        for k, (pr, pb) in enumerate(places):
            res = None
            for n in members:
                val = msg_in[n, pr * 8 : pr * 8 + 8, :]
                turn = (SLOTS * (n % 4 - pb)) % LANES
                val = pltpu.roll(val, turn, 1) if turn else val
                res = val if res is None else jnp.where(block == n % 4, val, res)
            if k < Q:
                tab[k, :, cols] = res
            else:
                tails[p * 3 + k - Q] = res
        for v in range(Q):
            r = 2 * (v % 4)
            first = jnp.broadcast_to(tails[p * 3 + v // 4, r : r + 1, :], (8, LANES))
            second = jnp.broadcast_to(tails[p * 3 + v // 4, r + 1 : r + 2, :], (8, LANES))
            tab[Q + v, :, cols] = jnp.where(sub % 2 == 0, first, second)

    def finish(et, _):
        off = pl.multiple_of(et * LANES, LANES)
        cut = pl.ds(off, LANES)
        lam = lame[:, cut]
        remote = range(TILES, TILES + RTILES)
        parts = [[] for _ in range(Q)]
        for f in range(5):
            here = pl.ds(pl.multiple_of(f * E + off, LANES), LANES)
            start = [acc[v, :, here] for v in range(Q)]
            if f < 4:
                idx = jnp.broadcast_to(nbr8[2 * f : 2 * f + 1, cut], (8, LANES))
                sources = [tab.at[v] for v in range(Q)]
                own = [tab[v, :, here] for v in range(Q)]
                c = [coef[k, 2 * f : 2 * f + 1, cut] for k in range(10)]
            else:
                idx = nbr8[:, cut]
                sources = [tab.at[Q + v] for v in range(Q)]
                own = [otail[v, :, cut] for v in range(Q)]
                c = [coef[k, :, cut] for k in range(10)]
            got = gather(sources, idx, remote, start)
            jump = [a - b for a, b in zip(got, own)]
            u = jump[6:9]
            n, mun, rhn, ws = c[0:3], c[3:6], c[6:9], c[9]
            flux = lam * (u[0] * n[0] + u[1] * n[1] + u[2] * n[2])
            res = []
            for i in range(3):
                push_i = u[i] * mun[i]
                res.append(flux + (push_i + push_i) + ws * jump[i])
            for k, (i, j) in enumerate(STRESS_ORDER[3:]):
                res.append(u[i] * mun[j] + u[j] * mun[i] + ws * jump[3 + k])
            for i in range(3):
                s = STRESS_PAIRS[i]
                res.append(
                    jump[s[0]] * rhn[0] + jump[s[1]] * rhn[1] + jump[s[2]] * rhn[2] + ws * u[i]
                )
            for v in range(Q):
                parts[v].append(res[v])
        right = jnp.concatenate([jnp.concatenate(x, axis=0) for x in parts], axis=1)
        high, low = split(right)
        right = jnp.concatenate([high, low, high], axis=0).astype(BF16)
        lifts = jnp.dot(l_all, right, preferred_element_type=F32)
        chosen = jnp.broadcast_to(cluster[:, cut], (B, LANES)) == 1
        for v in range(Q):
            new = base[v, 0:B, cut] + lifts[0:B, v * LANES : (v + 1) * LANES]
            out[v, :, cut] = jnp.where(chosen, new, x_ref[v, :, cut])
        return 0

    lax.fori_loop(0, E // LANES, finish, 0)
    done = pltpu.make_async_copy(out, dof_out, local_sem.at[0])
    done.start()
    for c in hand_copies + dg_copies:
        c.wait_send()
    for c in out_copies:
        c.wait()
    done.wait()


def shards(
    dof_values,
    density,
    lame_lambda,
    shear_modulus,
    jacobian,
    normals,
    face_scale,
    derivative,
    face_proj,
    lift_matrix,
    neighbour,
    send_face,
    cluster,
    sea_face,
    sea_cell,
    height,
    momentum,
    ocean_depth,
):
    n_dom, n_tile = lax.axis_size("dom"), lax.axis_size("tile")
    row = lambda x: x.reshape(1, x.shape[0])
    vmem = pl.BlockSpec(memory_space=pltpu.VMEM)
    far = pl.BlockSpec(memory_space=pl.ANY)
    table = (TILES + RTILES) * LANES
    dof_out, height_out, momentum_out = pl.pallas_call(
        functools.partial(kernel, n_dom, n_tile),
        out_shape=(
            jax.ShapeDtypeStruct((Q, B, E), F32),
            jax.ShapeDtypeStruct(height.shape, F32),
            jax.ShapeDtypeStruct(momentum.shape, F32),
        ),
        in_specs=[far] + [vmem] * 14 + [far] * 3,
        out_specs=(far, far, far),
        scratch_shapes=[
            pltpu.VMEM((Q, B, E), F32),
            pltpu.VMEM((Q, BP, E), F32),
            pltpu.VMEM((Q, B, E), F32),
            pltpu.VMEM((2 * Q, 8, table), F32),
            pltpu.VMEM((3, 8, TILES * LANES), F32),
            pltpu.VMEM((Q, 8, E), F32),
            pltpu.VMEM((Q, 8, 5 * E), F32),
            pltpu.VMEM((144, LANES), F32),
            pltpu.VMEM((LANES, LANES), F32),
            pltpu.VMEM((16, LANES), jnp.int32),
            pltpu.VMEM((8, E), jnp.int32),
            pltpu.VMEM((10, 8, E), F32),
            pltpu.VMEM((11, 24, LANES), F32),
            pltpu.VMEM((11, 24, LANES), F32),
            pltpu.VMEM((9, 8, LANES), F32),
            pltpu.VMEM((LANES, LANES), F32),
            pltpu.VMEM((3, 8, LANES), F32),
            pltpu.VMEM((3, 5, ROWS, LANES), F32),
            pltpu.VMEM((3, ROWS, LANES), F32),
            pltpu.VMEM((3, ROWS, LANES), F32),
            pltpu.VMEM((5, ROWS, LANES), F32),
            pltpu.VMEM((ROWS, LANES), F32),
            pltpu.VMEM((ROWS, LANES), F32),
            pltpu.SemaphoreType.DMA((13,)),
            pltpu.SemaphoreType.DMA((30,)),
            pltpu.SemaphoreType.DMA((30,)),
        ],
        compiler_params=pltpu.CompilerParams(collective_id=0, has_side_effects=True),
    )(
        jnp.transpose(dof_values, (1, 0, 2)),
        row(density),
        row(lame_lambda),
        row(shear_modulus),
        jacobian,
        jnp.transpose(normals, (1, 0, 2)),
        face_scale,
        derivative,
        jnp.transpose(face_proj, (1, 0, 2)),
        jnp.transpose(lift_matrix, (2, 0, 1)),
        neighbour,
        send_face,
        row(cluster),
        jnp.transpose(sea_face),
        jnp.transpose(sea_cell),
        height,
        momentum,
        ocean_depth,
    )
    return jnp.transpose(dof_out, (1, 0, 2)), height_out, momentum_out


def solution(mesh):
    both = ("dom", "tile")
    return jax.shard_map(
        shards,
        mesh=mesh,
        in_specs=(
            P(None, None, both),
            P(both),
            P(both),
            P(both),
            P(None, None, both),
            P(None, None, both),
            P(None, both),
            P(),
            P(),
            P(),
            P(None, both),
            P(both, None),
            P(both),
            P(both, None),
            P(both, None),
            P("dom", "tile"),
            P(None, "dom", "tile"),
            P("dom", "tile"),
        ),
        out_specs=(P(None, None, both), P("dom", "tile"), P(None, "dom", "tile")),
        check_vma=False,
    )
```

```python
import functools

import jax
import jax.numpy as jnp
from jax import lax
from jax.experimental import pallas as pl
from jax.experimental.pallas import tpu as pltpu
from jax.sharding import PartitionSpec as P

STEPS = 4
STRESS_PAIRS = ((0, 3, 5), (3, 1, 4), (5, 4, 2))
STRESS_ORDER = ((0, 0), (1, 1), (2, 2), (0, 1), (1, 2), (0, 2))
STEP_SIZE = 0.3
WAVE_RATE = 0.45
FLAT = pl.DeviceIdType.LOGICAL
F32 = jnp.float32
BF16 = jnp.bfloat16

B = 20
BP = 24
Q = 9
E = 512
CH = 256
LANES = 128
VMEM = 58 << 20
TILES = 16
RTILES = 3
SLOTS = 32
ROW0 = 16
ROWS = 96


def partner_offsets(tile_count, device_count):
    t = tile_count
    return [1, -1, 2, -2, t, -t, t + 1, -(t + 1), 2 * t, -2 * t, device_count // 2]


def split(x):
    high = x.astype(BF16).astype(F32)
    return high, x - high


def stacked(x):
    high, low = split(x)
    pad = jnp.zeros((8,) + x.shape[1:], F32)
    parts = [high, low, high]
    if (3 * x.shape[0]) % 16:
        parts.append(pad)
    return jnp.concatenate(parts, axis=0).astype(BF16)


def kernel(n_dom, n_tile, *refs):
    (
        dof_in,
        density_in,
        lame_in,
        shear_in,
        jac_in,
        nrm_in,
        fscale_in,
        deriv_in,
        fproj_in,
        lift_in,
        nbr_in,
        send_in,
        cluster_in,
        sea_face_in,
        sea_cell_in,
        height,
        momentum,
        depth,
    ) = refs[:18]
    out, flow_out, level_out = refs[18:21]
    (
        x_ref,
        density,
        lame,
        shear,
        jac,
        nrm,
        fscale,
        deriv,
        fproj,
        lift,
        nbr,
        send,
        cluster,
        sea_face,
        sea_cell,
    ) = refs[21:36]
    (
        base,
        tab,
        tab2,
        otail,
        acc,
        amat,
        lmat,
        sidx,
        nbr8,
        coef,
        msg,
        msg_in,
        tails,
        hand,
        hand_in,
        flow,
        level,
        flow_side,
        flow_side_in,
        flow_corner,
        flow_corner_in,
        level_side,
        level_side_in,
        level_corner_in,
        local_sem,
        send_sem,
        recv_sem,
    ) = refs[36:]
    devices = n_dom * n_tile
    dom, tile = lax.axis_index("dom"), lax.axis_index("tile")
    me = dom * n_tile + tile
    offsets = partner_offsets(n_tile, devices)
    greet = offsets + [n_tile - 1, -(n_tile - 1)]

    def device(offset):
        target = me + offset % devices
        return jnp.where(target >= devices, target - devices, target)

    barrier = pltpu.get_barrier_semaphore()
    for o in greet:
        pl.semaphore_signal(barrier, inc=1, device_id=device(o), device_id_type=FLAT)

    near = {}

    def fetch(name, src, dst):
        near[name] = pltpu.make_async_copy(src, dst, local_sem.at[len(near)])
        near[name].start()

    fetch("deriv", deriv_in, deriv)
    fetch("fproj", fproj_in, fproj)
    fetch("lift", lift_in, lift)
    for i in range(E // CH):
        cut = slice(i * CH, (i + 1) * CH)
        fetch(f"dof{i}", dof_in.at[:, :, cut], x_ref.at[:, :, cut])
        if i == 0:
            fetch("density", density_in, density)
            fetch("lame", lame_in, lame)
            fetch("shear", shear_in, shear)
            fetch("jac", jac_in, jac)
    fetch("sea_face", sea_face_in, sea_face)
    fetch("send", send_in, send)
    fetch("nbr", nbr_in, nbr)
    fetch("nrm", nrm_in, nrm)
    fetch("fscale", fscale_in, fscale)
    fetch("cluster", cluster_in, cluster)
    fetch("sea_cell", sea_cell_in, sea_cell)
    grid_rows = slice(ROW0, ROW0 + 64)
    for t in range(4):
        lanes = slice(t * LANES, (t + 1) * LANES)
        fetch(f"momentum{t}", momentum.at[:, :, lanes], flow.at[0:2, t, grid_rows, :])
        fetch(f"depth{t}", depth.at[:, lanes], flow.at[2, t, grid_rows, :])
        fetch(f"height{t}", height.at[:, lanes], level.at[t, grid_rows, :])

    lane = lax.broadcasted_iota(jnp.int32, (8, LANES), 1)
    sub = lax.broadcasted_iota(jnp.int32, (8, LANES), 0)

    for name in ("deriv", "fproj", "lift"):
        near[name].wait()
    amat[...] = jnp.zeros_like(amat)
    lmat[...] = jnp.zeros_like(lmat)
    for d in range(3):
        amat[d * BP : d * BP + B, 0:B] = deriv[d]
    for f in range(4):
        for c in range(10):
            row = fproj[c, f : f + 1, :]
            lrow = lift[c, f : f + 1, :]
            if c < 8:
                amat[72 + f * 8 + c : 73 + f * 8 + c, 0:B] = row
                lmat[f * 8 + c : f * 8 + c + 1, 0:B] = lrow
            else:
                k = 32 + f * 2 + c - 8
                amat[72 + k : 73 + k, 0:B] = row
                lmat[k : k + 1, 0:B] = lrow
                for r in range(4):
                    k = 112 + f * 8 + r * 2 + c - 8
                    amat[k : k + 1, 0:B] = row
    a_high, a_low = split(amat[...])
    a_all = a_high + pltpu.roll(a_high, BP, 1) + pltpu.roll(a_low, 2 * BP, 1)
    a_all = a_all.astype(BF16)[:, 0:80]
    l_high, l_low = split(jnp.transpose(lmat[...]))
    l_high, l_low = l_high[0:BP], l_low[0:BP]
    l_all = l_high + pltpu.roll(l_high, 40, 1) + pltpu.roll(l_low, 80, 1)
    l_all = l_all.astype(BF16)[:, 0:120]

    for name in ("density", "lame", "shear", "jac"):
        near[name].wait()

    def predictor(i, _):
        off = pl.multiple_of(i * CH, CH)
        cut = pl.ds(off, CH)
        rho = 1.0 / density[:, cut]
        lam = lame[:, cut]
        mu = shear[:, cut]
        mu2 = mu + mu
        jc = [[jac[d, x : x + 1, cut] for x in range(3)] for d in range(3)]

        def combine(g):
            def phys(x, v):
                return (
                    jc[0][x] * g[0:BP, v * CH : (v + 1) * CH]
                    + jc[1][x] * g[BP : 2 * BP, v * CH : (v + 1) * CH]
                    + jc[2][x] * g[2 * BP : 3 * BP, v * CH : (v + 1) * CH]
                )

            vg = [[phys(j, 6 + i) for j in range(3)] for i in range(3)]
            div = lam * (vg[0][0] + vg[1][1] + vg[2][2])
            res = [div + mu2 * vg[i][i] for i in range(3)]
            res += [mu * (vg[i][j] + vg[j][i]) for i, j in STRESS_ORDER[3:]]
            for i in range(3):
                s = STRESS_PAIRS[i]
                res.append(rho * (phys(0, s[0]) + phys(1, s[1]) + phys(2, s[2])))
            return res

        pad = jnp.zeros((BP - B, CH), F32)
        start = [jnp.concatenate([x_ref[v, :, cut], pad], axis=0) for v in range(Q)]
        term = start
        integral = [STEP_SIZE * w for w in term]
        factor = STEP_SIZE
        for k in range(1, 4):
            right = stacked(jnp.concatenate(term, axis=1))
            term = combine(jnp.dot(a_all[0:72], right, preferred_element_type=F32))
            factor = factor * STEP_SIZE / (k + 1)
            integral = [s + factor * w for s, w in zip(integral, term)]
        right = stacked(jnp.concatenate(integral, axis=1))
        g = jnp.dot(a_all, right, preferred_element_type=F32)
        volume = combine(g)
        for v in range(Q):
            cols = slice(v * CH, (v + 1) * CH)
            base[v, :, cut] = start[v] + volume[v]
            for f in range(4):
                here = pl.ds(pl.multiple_of(f * E + off, LANES), CH)
                tab[v, :, here] = g[72 + f * 8 : 80 + f * 8, cols]
                tab[Q + v, :, here] = g[112 + f * 8 : 120 + f * 8, cols]
            otail[v, :, cut] = g[104:112, cols]
        for f in range(4):
            here = pl.ds(pl.multiple_of(f * E + off, LANES), CH)
            pair = lax.broadcasted_iota(jnp.int32, (8, CH), 0) // 2
            for j in range(3):
                packed = g[112 + f * 8 : 120 + f * 8, 4 * j * CH : (4 * j + 1) * CH]
                for q in range(1, 4):
                    if 4 * j + q < Q:
                        v = 4 * j + q
                        more = g[112 + f * 8 : 120 + f * 8, v * CH : (v + 1) * CH]
                        packed = jnp.where(pair == q, more, packed)
                tab2[j, :, here] = packed
        return 0

    for i in range(E // CH):
        near[f"dof{i}"].wait()
        lax.fori_loop(i, i + 1, predictor, 0)
    near["sea_face"].wait()

    shift = lax.rem(devices - me, devices)
    ups = [jnp.broadcast_to(tab[8, 0:1, t * LANES : (t + 1) * LANES], (8, LANES)) for t in range(4)]
    slots = []
    for r in range(8):
        idx = sea_face[r * 8 : r * 8 + 8, :]
        at, which = idx & (LANES - 1), idx >> 7
        val = jnp.zeros((8, LANES), F32)
        for t in range(4):
            val = jnp.where(which == t, jnp.take_along_axis(ups[t], at, axis=1), val)
        slots.append(val)
    handed = pltpu.roll(jnp.concatenate(slots, axis=0), shift, 1)
    zeros64 = jnp.zeros((64, LANES), F32)
    hand[...] = jnp.transpose(jnp.concatenate([handed, zeros64], axis=0))

    pl.semaphore_wait(barrier, len(greet))

    copies = []

    def push(src, dst, offset):
        k = len(copies)
        copy = pltpu.make_async_remote_copy(
            src_ref=src,
            dst_ref=dst,
            send_sem=send_sem.at[k],
            recv_sem=recv_sem.at[k],
            device_id=device(offset),
            device_id_type=FLAT,
        )
        copy.start()
        copies.append(copy)
        return copy

    hand_offsets = (1, n_tile, devices // 2)
    hand_copies = []
    for k, o in enumerate(hand_offsets):
        row = o // 8 * 8
        hand_copies.append(push(hand.at[row : row + 8, :], hand_in.at[k], o))

    near["send"].wait()
    sidx[...] = jnp.zeros_like(sidx)
    sidx[0:11, 0:SLOTS] = send[...]
    def gather(sources, idx, tiles, start):
        at, which = idx & (LANES - 1), idx >> 7
        res = list(start)
        for t in tiles:
            mask = which == t
            for k, source in enumerate(sources):
                val = jnp.take_along_axis(source[:, t * LANES : (t + 1) * LANES], at, axis=1)
                res[k] = val if res[k] is None else jnp.where(mask, val, res[k])
        return res

    block = lane // SLOTS
    places = [(v // 4, v % 4) for v in range(Q)] + [(2, 1 + j) for j in range(3)]
    dg_copies = []
    for p in range(RTILES):
        members = [n for n in range(4 * p, 4 * p + 4) if n < len(offsets)]
        idx = jnp.zeros((8, LANES), jnp.int32)
        for n in members:
            row = jnp.broadcast_to(sidx[n : n + 1, :], (8, LANES))
            idx = jnp.where(block == n % 4, pltpu.roll(row, SLOTS * (n % 4), 1), idx)
        sources = [tab.at[v] for v in range(Q)] + [tab2.at[j] for j in range(3)]
        got = gather(sources, idx, range(TILES), [None] * 12)
        for n in members:
            for r in range(3):
                packed = None
                for k, (pr, pb) in enumerate(places):
                    if pr != r:
                        continue
                    turn = (SLOTS * (pb - n % 4)) % LANES
                    val = pltpu.roll(got[k], turn, 1) if turn else got[k]
                    packed = val if packed is None else jnp.where(block == pb, val, packed)
                msg[n, r * 8 : r * 8 + 8, :] = packed
        for n in members:
            dg_copies.append(push(msg.at[n], msg_in.at[n], offsets[n]))

    for t in range(4):
        near[f"momentum{t}"].wait()
        near[f"depth{t}"].wait()
        near[f"height{t}"].wait()
    top, low = slice(ROW0, ROW0 + 8), slice(ROW0 + 56, ROW0 + 64)
    above, below = slice(ROW0 - 8, ROW0), slice(ROW0 + 64, ROW0 + 72)
    group = lane // 8

    def column(ring, t):
        res = None
        for r in range(8):
            val = ring[t, ROW0 + 8 * r : ROW0 + 8 * r + 8, :]
            turn = (8 * r + (8 if t else 0)) % LANES
            val = pltpu.roll(val, turn, 1) if turn else val
            res = val if res is None else jnp.where(group == r, val, res)
        return res

    corners = ((0, top), (3, top), (0, low), (3, low))
    for side, t in ((0, 0), (1, 3)):
        fx, fy, dp = (column(flow.at[k], t) for k in range(3))
        flow_side[side, 0] = jnp.where(lane < 64, fx, pltpu.roll(fy, 64, 1))
        flow_side[side, 1] = dp
    for k, (t, rows) in enumerate(corners):
        turns = (0, 8, 16) if t == 0 else (0, LANES - 8, LANES - 16)
        fx, fy, dp = (
            pltpu.roll(flow[i, t, rows, :], turns[i], 1) if i else flow[i, t, rows, :]
            for i in range(3)
        )
        spot = group if t == 0 else 15 - group
        flow_corner[k] = jnp.where(spot == 0, fx, jnp.where(spot == 1, fy, dp))
    corner_offsets = (-n_tile - 1, -n_tile + 1, n_tile - 1, n_tile + 1)
    cols = slice(0, 4)
    flow_copies = [
        push(flow.at[:, cols, top, :], flow.at[:, cols, below, :], -n_tile),
        push(flow.at[:, cols, low, :], flow.at[:, cols, above, :], n_tile),
        push(flow_side.at[0], flow_side_in.at[0], -1),
        push(flow_side.at[1], flow_side_in.at[1], 1),
    ]
    for k, o in enumerate(corner_offsets):
        flow_copies.append(push(flow_corner.at[k], flow_corner_in.at[k], o))

    for name in ("nbr", "nrm", "fscale", "cluster", "sea_cell"):
        near[name].wait()
    inv_den = 1.0 / density[...]
    speed = jnp.sqrt((lame[...] + 2.0 * shear[...]) * inv_den)
    half = 0.5 * fscale[...]
    scaled = [half * nrm[j] for j in range(3)]
    coefs = (
        scaled
        + [shear[...] * s for s in scaled]
        + [inv_den * s for s in scaled]
        + [half * speed]
    )
    for k, c in enumerate(coefs):
        for f in range(4):
            coef[k, 2 * f : 2 * f + 2, :] = jnp.broadcast_to(c[f : f + 1, :], (2, E))
    for f in range(4):
        nbr8[2 * f : 2 * f + 2, :] = jnp.broadcast_to(nbr[f : f + 1, :], (2, E))
    def local_gather(et, _):
        off = pl.multiple_of(et * LANES, LANES)
        for f in range(4):
            idx = jnp.broadcast_to(nbr8[2 * f : 2 * f + 1, pl.ds(off, LANES)], (8, LANES))
            got = gather([tab.at[v] for v in range(Q)], idx, range(TILES), [None] * Q)
            for v in range(Q):
                acc[v, :, pl.ds(pl.multiple_of(f * E + off, LANES), LANES)] = got[v]
        idx = nbr8[:, pl.ds(off, LANES)]
        got = gather([tab.at[Q + v] for v in range(Q)], idx, range(TILES), [None] * Q)
        for v in range(Q):
            acc[v, :, pl.ds(pl.multiple_of(4 * E + off, LANES), LANES)] = got[v]
        return 0

    lax.fori_loop(0, 2, local_gather, 0)

    for c in hand_copies:
        c.wait_recv()
    back = (0, devices - 1, devices - n_tile, devices // 2)
    cells = pltpu.roll(sea_cell[...], shift, 1)
    cells_t = jnp.transpose(
        jnp.concatenate([cells, jnp.zeros((64, LANES), jnp.int32)], axis=0).astype(F32)
    ).astype(jnp.int32)
    values = [hand[0:1, :]]
    for k, o in enumerate(hand_offsets):
        values.append(hand_in[k, o % 8 : o % 8 + 1, :])
    row_ids = lax.broadcasted_iota(jnp.int32, (64, LANES), 0)
    highs, lows = [], []
    for k in range(0, 4, 2):
        pair_v = values[k] + pltpu.roll(values[k + 1], 64, 1)
        pair_c = cells_t[back[k] : back[k] + 1, :] + pltpu.roll(
            cells_t[back[k + 1] : back[k + 1] + 1, :], 64, 1
        )
        v_high, v_low = split(pair_v)
        here = row_ids == jnp.broadcast_to(pair_c >> 9, (64, LANES))
        highs.append(jnp.where(here, v_high, 0.0))
        lows.append(jnp.where(here, v_low, 0.0))
    left = jnp.concatenate(
        [jnp.concatenate(highs, axis=1), jnp.concatenate(lows, axis=1)], axis=0
    ).astype(BF16)
    col_ids = lax.broadcasted_iota(jnp.int32, (64, E), 1)
    picks = []
    for k in range(4):
        chosen = jnp.broadcast_to(cells[:, back[k] : back[k] + 1] & (E - 1), (64, E))
        picks.append(jnp.where(col_ids == chosen, 1.0, 0.0).astype(BF16))
    lifted = jnp.dot(left, jnp.concatenate(picks, axis=0), preferred_element_type=F32)
    for t in range(4):
        lanes = slice(t * LANES, (t + 1) * LANES)
        level[t, ROW0 : ROW0 + 64, :] += lifted[0:64, lanes] + lifted[64:128, lanes]
    for side, t in ((0, 0), (1, 3)):
        level_side[side] = column(level, t)
    level_copies = [
        push(level.at[cols, top, :], level.at[cols, below, :], -n_tile),
        push(level.at[cols, low, :], level.at[cols, above, :], n_tile),
        push(level_side.at[0], level_side_in.at[0], -1),
        push(level_side.at[1], level_side_in.at[1], 1),
    ]
    for k, (o, (t, rows)) in enumerate(zip(corner_offsets, corners)):
        level_copies.append(push(level.at[t, rows, :], level_corner_in.at[k], o))

    lax.fori_loop(2, 4, local_gather, 0)

    for c in dg_copies:
        c.wait_recv()
    for p in range(RTILES):
        members = [n for n in range(4 * p, 4 * p + 4) if n < len(offsets)]
        cols = slice((TILES + p) * LANES, (TILES + p + 1) * LANES)
        for k, (pr, pb) in enumerate(places):
            res = None
            for n in members:
                val = msg_in[n, pr * 8 : pr * 8 + 8, :]
                turn = (SLOTS * (n % 4 - pb)) % LANES
                val = pltpu.roll(val, turn, 1) if turn else val
                res = val if res is None else jnp.where(block == n % 4, val, res)
            if k < Q:
                tab[k, :, cols] = res
            else:
                tails[p * 3 + k - Q] = res
        for v in range(Q):
            r = 2 * (v % 4)
            first = jnp.broadcast_to(tails[p * 3 + v // 4, r : r + 1, :], (8, LANES))
            second = jnp.broadcast_to(tails[p * 3 + v // 4, r + 1 : r + 2, :], (8, LANES))
            tab[Q + v, :, cols] = jnp.where(sub % 2 == 0, first, second)

    def finish(et, _):
        off = pl.multiple_of(et * LANES, LANES)
        cut = pl.ds(off, LANES)
        lam = lame[:, cut]
        remote = range(TILES, TILES + RTILES)
        parts = [[] for _ in range(Q)]
        for f in range(5):
            here = pl.ds(pl.multiple_of(f * E + off, LANES), LANES)
            start = [acc[v, :, here] for v in range(Q)]
            if f < 4:
                idx = jnp.broadcast_to(nbr8[2 * f : 2 * f + 1, cut], (8, LANES))
                sources = [tab.at[v] for v in range(Q)]
                own = [tab[v, :, here] for v in range(Q)]
                c = [coef[k, 2 * f : 2 * f + 1, cut] for k in range(10)]
            else:
                idx = nbr8[:, cut]
                sources = [tab.at[Q + v] for v in range(Q)]
                own = [otail[v, :, cut] for v in range(Q)]
                c = [coef[k, :, cut] for k in range(10)]
            got = gather(sources, idx, remote, start)
            jump = [a - b for a, b in zip(got, own)]
            u = jump[6:9]
            n, mun, rhn, ws = c[0:3], c[3:6], c[6:9], c[9]
            flux = lam * (u[0] * n[0] + u[1] * n[1] + u[2] * n[2])
            res = []
            for i in range(3):
                push_i = u[i] * mun[i]
                res.append(flux + (push_i + push_i) + ws * jump[i])
            for k, (i, j) in enumerate(STRESS_ORDER[3:]):
                res.append(u[i] * mun[j] + u[j] * mun[i] + ws * jump[3 + k])
            for i in range(3):
                s = STRESS_PAIRS[i]
                res.append(
                    jump[s[0]] * rhn[0] + jump[s[1]] * rhn[1] + jump[s[2]] * rhn[2] + ws * u[i]
                )
            for v in range(Q):
                parts[v].append(res[v])
        right = jnp.concatenate([jnp.concatenate(x, axis=0) for x in parts], axis=1)
        high, low = split(right)
        right = jnp.concatenate([high, low, high], axis=0).astype(BF16)
        lifts = jnp.dot(l_all, right, preferred_element_type=F32)
        chosen = jnp.broadcast_to(cluster[:, cut], (B, LANES)) == 1
        for v in range(Q):
            new = base[v, 0:B, cut] + lifts[0:B, v * LANES : (v + 1) * LANES]
            out[v, :, cut] = jnp.where(chosen, new, x_ref[v, :, cut])
        return 0

    lax.fori_loop(0, E // LANES, finish, 0)
    for c in hand_copies + dg_copies:
        c.wait_send()
    for c in flow_copies:
        c.wait()
    above_ok, below_ok, right_ok, left_ok = inside(n_dom, n_tile)

    def close(ring, side, corner, res, scale):
        for t in range(4):
            res[t, ROW0 - 8 : ROW0, :] = ring[t, ROW0 - 8 : ROW0, :] * (above_ok * scale)
            res[t, ROW0 + 64 : ROW0 + 72, :] = ring[t, ROW0 + 64 : ROW0 + 72, :] * (below_ok * scale)
            val = ring[t, grid_rows, :]
            res[t, grid_rows, :] = val * scale if scale != 1.0 else val
        side_ok = jnp.where(lane < 64, right_ok, left_ok) * scale
        for r in range(8):
            right, left = side(r)
            res[4, ROW0 + 8 * r : ROW0 + 8 * r + 8, :] = jnp.where(lane < 64, right, left) * side_ok
        res[4, below, :] = jnp.where(lane < 64, corner(0), corner(1)) * (side_ok * below_ok)
        res[4, above, :] = jnp.where(lane < 64, corner(2), corner(3)) * (side_ok * above_ok)
        for t in range(5):
            res[t, 0:8, :] = jnp.zeros((8, LANES), F32)
            res[t, ROWS - 8 : ROWS, :] = jnp.zeros((8, LANES), F32)

    def turned(val, turn):
        return pltpu.roll(val, turn % LANES, 1) if turn % LANES else val

    for k in range(3):
        start = 64 if k == 1 else 0
        from_right, from_left = flow_side_in[0, k // 2], flow_side_in[1, k // 2]

        def side(r):
            at = start + 8 * r
            return turned(from_right, -at), turned(from_left, LANES - 8 - at)

        def corner(j):
            return turned(flow_corner_in[j], (-8 if j % 2 == 0 else 8) * k)

        close(flow.at[k], side, corner, flow_out.at[k], 0.5 * WAVE_RATE if k == 2 else 1.0)
    for c in level_copies:
        c.wait()
    from_right, from_left = level_side_in[0], level_side_in[1]

    def level_sides(r):
        return turned(from_right, -8 * r), turned(from_left, LANES - 8 - 8 * r)

    close(level, level_sides, lambda j: level_corner_in[j], level_out, 1.0)


def inside(n_dom, n_tile):
    dom, tile = lax.axis_index("dom"), lax.axis_index("tile")
    return (
        jnp.where(dom > 0, 1.0, 0.0),
        jnp.where(dom < n_dom - 1, 1.0, 0.0),
        jnp.where(tile < n_tile - 1, 1.0, 0.0),
        jnp.where(tile > 0, 1.0, 0.0),
    )


def grid_kernel(n_dom, n_tile, dof, flow_in, level_in, dof_out, height_out, momentum_out, *rest):
    flow, level, sem = rest
    dof_copy = pltpu.make_async_copy(dof, dof_out, sem.at[0])
    dof_copy.start()
    above_ok, below_ok, right_ok, left_ok = inside(n_dom, n_tile)
    c0 = 0.5 * WAVE_RATE
    lane = lax.broadcasted_iota(jnp.int32, (8, LANES), 1)
    side_ok = jnp.where(lane < 64, right_ok, left_ok)
    for ring in (flow.at[0], level):
        for t in range(5):
            ring[t, 0:8, :] = jnp.zeros((8, LANES), F32)
            ring[t, ROWS - 8 : ROWS, :] = jnp.zeros((8, LANES), F32)

    def across(vals):
        fwd = [pltpu.roll(x, LANES - 1, 1) for x in vals]
        bwd = [pltpu.roll(x, 1, 1) for x in vals]
        res = []
        for t in range(5):
            nxt = jnp.where(lane == LANES - 1, fwd[(t + 1) % 5], fwd[t])
            prv = jnp.where(lane == 0, bwd[(t + 4) % 5], bwd[t])
            res.append(nxt - prv)
        return res

    def wave(flow_old, level_old):
        for r in range(10):
            at = ROW0 - 8 + 8 * r
            rows = slice(at, at + 8)
            row_ok = above_ok if r == 0 else below_ok if r == 9 else 1.0
            diff = across([flow_old[1, t, rows, :] for t in range(5)])
            for t in range(5):
                spread = flow_old[0, t, at + 1 : at + 9, :] - flow_old[0, t, at - 1 : at + 7, :]
                rate = c0 * row_ok * side_ok if t == 4 else c0 * row_ok
                level[t, rows, :] = level_old[t, rows, :] - rate * (spread + diff[t])
        for r in range(10):
            at = ROW0 - 8 + 8 * r
            rows = slice(at, at + 8)
            diff = across([level[t, rows, :] for t in range(5)])
            for t in range(5):
                g = flow_in[2, t, rows, :]
                slope = level[t, at + 1 : at + 9, :] - level[t, at - 1 : at + 7, :]
                flow[0, t, rows, :] = flow_old[0, t, rows, :] - g * slope
                flow[1, t, rows, :] = flow_old[1, t, rows, :] - g * diff[t]

    wave(flow_in, level_in)

    def again(_, carry):
        wave(flow, level)
        return carry

    lax.fori_loop(0, STEPS - 1, again, 0)
    copies = [dof_copy]
    rows = slice(ROW0, ROW0 + 64)
    for t in range(4):
        lanes = slice(t * LANES, (t + 1) * LANES)
        copies += [
            pltpu.make_async_copy(
                flow.at[:, t, rows, :], momentum_out.at[:, :, lanes], sem.at[1 + t]
            ),
            pltpu.make_async_copy(level.at[t, rows, :], height_out.at[:, lanes], sem.at[5 + t]),
        ]
    for c in copies[1:]:
        c.start()
    for c in copies:
        c.wait()


def shards(
    dof_values,
    density,
    lame_lambda,
    shear_modulus,
    jacobian,
    normals,
    face_scale,
    derivative,
    face_proj,
    lift_matrix,
    neighbour,
    send_face,
    cluster,
    sea_face,
    sea_cell,
    height,
    momentum,
    ocean_depth,
):
    n_dom, n_tile = lax.axis_size("dom"), lax.axis_size("tile")
    row = lambda x: x.reshape(1, x.shape[0])
    vmem = pl.BlockSpec(memory_space=pltpu.VMEM)
    far = pl.BlockSpec(memory_space=pltpu.HBM)
    table = (TILES + RTILES) * LANES
    args = (
        jnp.transpose(dof_values, (1, 0, 2)),
        row(density),
        row(lame_lambda),
        row(shear_modulus),
        jacobian,
        jnp.transpose(normals, (1, 0, 2)),
        face_scale,
        derivative,
        jnp.transpose(face_proj, (1, 0, 2)),
        jnp.transpose(lift_matrix, (2, 0, 1)),
        neighbour,
        send_face,
        row(cluster),
        jnp.transpose(sea_face),
        jnp.transpose(sea_cell),
        height,
        momentum,
        ocean_depth,
    )
    dof_new, flow, level = pl.pallas_call(
        functools.partial(kernel, n_dom, n_tile),
        out_shape=(
            pltpu.VMEM((Q, B, E), F32),
            pltpu.VMEM((3, 5, ROWS, LANES), F32),
            pltpu.VMEM((5, ROWS, LANES), F32),
        ),
        in_specs=[far] * 18,
        out_specs=(vmem,) * 3,
        scratch_shapes=[pltpu.VMEM(x.shape, x.dtype) for x in args[:15]]
        + [
            pltpu.VMEM((Q, BP, E), F32),
            pltpu.VMEM((2 * Q, 8, table), F32),
            pltpu.VMEM((3, 8, TILES * LANES), F32),
            pltpu.VMEM((Q, 8, E), F32),
            pltpu.VMEM((Q, 8, 5 * E), F32),
            pltpu.VMEM((144, LANES), F32),
            pltpu.VMEM((LANES, LANES), F32),
            pltpu.VMEM((16, LANES), jnp.int32),
            pltpu.VMEM((8, E), jnp.int32),
            pltpu.VMEM((10, 8, E), F32),
            pltpu.VMEM((11, 24, LANES), F32),
            pltpu.VMEM((11, 24, LANES), F32),
            pltpu.VMEM((9, 8, LANES), F32),
            pltpu.VMEM((LANES, LANES), F32),
            pltpu.VMEM((3, 8, LANES), F32),
            pltpu.VMEM((3, 5, ROWS, LANES), F32),
            pltpu.VMEM((5, ROWS, LANES), F32),
            pltpu.VMEM((2, 2, 8, LANES), F32),
            pltpu.VMEM((2, 2, 8, LANES), F32),
            pltpu.VMEM((4, 8, LANES), F32),
            pltpu.VMEM((4, 8, LANES), F32),
            pltpu.VMEM((2, 8, LANES), F32),
            pltpu.VMEM((2, 8, LANES), F32),
            pltpu.VMEM((4, 8, LANES), F32),
            pltpu.SemaphoreType.DMA((32,)),
            pltpu.SemaphoreType.DMA((30,)),
            pltpu.SemaphoreType.DMA((30,)),
        ],
        compiler_params=pltpu.CompilerParams(
            collective_id=0, has_side_effects=True, vmem_limit_bytes=VMEM
        ),
    )(*args)
    dof_out, height_out, momentum_out = pl.pallas_call(
        functools.partial(grid_kernel, n_dom, n_tile),
        out_shape=(
            jax.ShapeDtypeStruct((Q, B, E), F32),
            jax.ShapeDtypeStruct(height.shape, F32),
            jax.ShapeDtypeStruct(momentum.shape, F32),
        ),
        in_specs=[vmem] * 3,
        out_specs=(far,) * 3,
        scratch_shapes=[
            pltpu.VMEM((2, 5, ROWS, LANES), F32),
            pltpu.VMEM((5, ROWS, LANES), F32),
            pltpu.SemaphoreType.DMA((9,)),
        ],
        compiler_params=pltpu.CompilerParams(vmem_limit_bytes=16 << 20),
    )(dof_new, flow, level)
    return jnp.transpose(dof_out, (1, 0, 2)), height_out, momentum_out


def solution(mesh):
    both = ("dom", "tile")
    return jax.shard_map(
        shards,
        mesh=mesh,
        in_specs=(
            P(None, None, both),
            P(both),
            P(both),
            P(both),
            P(None, None, both),
            P(None, None, both),
            P(None, both),
            P(),
            P(),
            P(),
            P(None, both),
            P(both, None),
            P(both),
            P(both, None),
            P(both, None),
            P("dom", "tile"),
            P(None, "dom", "tile"),
            P("dom", "tile"),
        ),
        out_specs=(P(None, None, both), P("dom", "tile"), P(None, "dom", "tile")),
        check_vma=False,
    )
```

```python
import functools

import jax
import jax.numpy as jnp
from jax import lax
from jax.experimental import pallas as pl
from jax.experimental.pallas import tpu as pltpu
from jax.sharding import PartitionSpec as P

STEPS = 4
STRESS_PAIRS = ((0, 3, 5), (3, 1, 4), (5, 4, 2))
STRESS_ORDER = ((0, 0), (1, 1), (2, 2), (0, 1), (1, 2), (0, 2))
STEP_SIZE = 0.3
WAVE_RATE = 0.45
FLAT = pl.DeviceIdType.LOGICAL
F32 = jnp.float32
BF16 = jnp.bfloat16

B = 20
BP = 24
Q = 9
E = 512
CH = 256
GROUP = 2
DOFS = 1
LANES = 128
VMEM = 58 << 20
AHEAD = 1
SIDE = 2
TILES = 16
RTILES = 3
SLOTS = 32
ROW0 = 16
ROWS = 96


def partner_offsets(tile_count, device_count):
    t = tile_count
    return [1, -1, 2, -2, t, -t, t + 1, -(t + 1), 2 * t, -2 * t, device_count // 2]


def split(x):
    high = x.astype(BF16).astype(F32)
    return high, x - high


def stacked(x):
    high, low = split(x)
    pad = jnp.zeros((8,) + x.shape[1:], F32)
    parts = [high, low, high]
    if (3 * x.shape[0]) % 16:
        parts.append(pad)
    return jnp.concatenate(parts, axis=0).astype(BF16)


def kernel(n_dom, n_tile, *refs):
    (
        dof_in,
        density_in,
        lame_in,
        shear_in,
        jac_in,
        nrm_in,
        fscale_in,
        deriv_in,
        fproj_in,
        lift_in,
        nbr_in,
        send_in,
        cluster_in,
        sea_face_in,
        sea_cell_in,
        height,
        momentum,
        depth,
    ) = refs[:18]
    out, flow_out, level_out = refs[18:21]
    (
        x_ref,
        density,
        lame,
        shear,
        jac,
        nrm,
        fscale,
        deriv,
        fproj,
        lift,
        nbr,
        send,
        cluster,
        sea_face,
        sea_cell,
    ) = refs[21:36]
    (
        base,
        tab,
        tab2,
        otail,
        acc,
        amat,
        lmat,
        sidx,
        nbr8,
        coef,
        msg,
        msg_in,
        tails,
        hand,
        hand_in,
        flow,
        level,
        flow_side,
        flow_side_in,
        flow_corner,
        flow_corner_in,
        level_side,
        level_side_in,
        level_corner_in,
        local_sem,
        send_sem,
        recv_sem,
    ) = refs[36:]
    devices = n_dom * n_tile
    dom, tile = lax.axis_index("dom"), lax.axis_index("tile")
    me = dom * n_tile + tile
    offsets = partner_offsets(n_tile, devices)
    greet = offsets + [n_tile - 1, -(n_tile - 1)]

    def device(offset):
        target = me + offset % devices
        return jnp.where(target >= devices, target - devices, target)

    barrier = pltpu.get_barrier_semaphore()
    for o in greet:
        pl.semaphore_signal(barrier, inc=1, device_id=device(o), device_id_type=FLAT)

    near = {}

    def fetch(name, src, dst):
        near[name] = pltpu.make_async_copy(src, dst, local_sem.at[len(near)])
        near[name].start()

    fetch("deriv", deriv_in, deriv)
    fetch("fproj", fproj_in, fproj)
    fetch("lift", lift_in, lift)
    for i in range(DOFS):
        cut = slice(i * E // DOFS, (i + 1) * E // DOFS)
        fetch(f"dof{i}", dof_in.at[:, :, cut], x_ref.at[:, :, cut])
        if i == 0:
            fetch("density", density_in, density)
            fetch("lame", lame_in, lame)
            fetch("shear", shear_in, shear)
            fetch("jac", jac_in, jac)
    fetch("sea_face", sea_face_in, sea_face)
    fetch("send", send_in, send)
    fetch("nbr", nbr_in, nbr)
    fetch("nrm", nrm_in, nrm)
    fetch("fscale", fscale_in, fscale)
    fetch("cluster", cluster_in, cluster)
    fetch("sea_cell", sea_cell_in, sea_cell)
    grid_rows = slice(ROW0, ROW0 + 64)
    for t in range(4):
        lanes = slice(t * LANES, (t + 1) * LANES)
        fetch(f"momentum{t}", momentum.at[:, :, lanes], flow.at[0:2, t, grid_rows, :])
        fetch(f"depth{t}", depth.at[:, lanes], flow.at[2, t, grid_rows, :])
        fetch(f"height{t}", height.at[:, lanes], level.at[t, grid_rows, :])

    lane = lax.broadcasted_iota(jnp.int32, (8, LANES), 1)
    sub = lax.broadcasted_iota(jnp.int32, (8, LANES), 0)

    for name in ("deriv", "fproj", "lift"):
        near[name].wait()
    amat[...] = jnp.zeros_like(amat)
    lmat[...] = jnp.zeros_like(lmat)
    for d in range(3):
        amat[d * BP : d * BP + B, 0:B] = deriv[d]
    for f in range(4):
        for c in range(10):
            row = fproj[c, f : f + 1, :]
            lrow = lift[c, f : f + 1, :]
            if c < 8:
                amat[72 + f * 16 + c : 73 + f * 16 + c, 0:B] = row
                lmat[f * 8 + c : f * 8 + c + 1, 0:B] = lrow
            else:
                k = 32 + f * 2 + c - 8
                amat[104 + k : 105 + k, 0:B] = row
                lmat[k : k + 1, 0:B] = lrow
                for r in range(4):
                    k = 80 + f * 16 + r * 2 + c - 8
                    amat[k : k + 1, 0:B] = row
    a_high, a_low = split(amat[...])
    a_all = a_high + pltpu.roll(a_high, BP, 1) + pltpu.roll(a_low, 2 * BP, 1)
    a_all = a_all.astype(BF16)[:, 0:80]
    l_high, l_low = split(jnp.transpose(lmat[...]))
    l_high, l_low = l_high[0:BP], l_low[0:BP]
    l_all = l_high + pltpu.roll(l_high, 40, 1) + pltpu.roll(l_low, 80, 1)
    l_all = l_all.astype(BF16)[:, 0:120]

    for name in ("density", "lame", "shear", "jac"):
        near[name].wait()

    def predictor(i, _):
        chunks = []
        for h in range(GROUP):
            off = pl.multiple_of((i * GROUP + h) * CH, CH)
            chunks.append(Chunk(off))
        for k in range(1, 4):
            for c in chunks:
                c.advance(k)
        for c in chunks:
            c.finish()
        return 0

    class Chunk:
        def __init__(self, off):
            self.off = off
            self.cut = cut = pl.ds(off, CH)
            self.rho = 1.0 / density[:, cut]
            self.lam = lame[:, cut]
            self.mu = shear[:, cut]
            self.jc = [[jac[d, x : x + 1, cut] for x in range(3)] for d in range(3)]
            pad = jnp.zeros((BP - B, CH), F32)
            self.term = [
                STEP_SIZE * jnp.concatenate([x_ref[v, :, cut], pad], axis=0) for v in range(Q)
            ]
            self.integral = self.term

        def combine(self, g, scale):
            jc = [[x * scale for x in row] for row in self.jc] if scale != 1.0 else self.jc
            lam, mu, rho = self.lam, self.mu, self.rho

            def phys(x, v):
                return (
                    jc[0][x] * g[0:BP, v * CH : (v + 1) * CH]
                    + jc[1][x] * g[BP : 2 * BP, v * CH : (v + 1) * CH]
                    + jc[2][x] * g[2 * BP : 3 * BP, v * CH : (v + 1) * CH]
                )

            vg = [[phys(j, 6 + i) for j in range(3)] for i in range(3)]
            div = lam * (vg[0][0] + vg[1][1] + vg[2][2])
            res = [div + (mu + mu) * vg[i][i] for i in range(3)]
            res += [mu * (vg[i][j] + vg[j][i]) for i, j in STRESS_ORDER[3:]]
            for i in range(3):
                s = STRESS_PAIRS[i]
                res.append(rho * (phys(0, s[0]) + phys(1, s[1]) + phys(2, s[2])))
            return res

        def advance(self, k):
            right = stacked(jnp.concatenate(self.term, axis=1))
            g = jnp.dot(a_all[0:72], right, preferred_element_type=F32)
            self.term = self.combine(g, STEP_SIZE / (k + 1))
            self.integral = [s + w for s, w in zip(self.integral, self.term)]

        def finish(self):
            off, cut = self.off, self.cut
            right = stacked(jnp.concatenate(self.integral, axis=1))
            g = jnp.dot(a_all, right, preferred_element_type=F32)
            volume = self.combine(g, 1.0)
            for v in range(Q):
                cols = slice(v * CH, (v + 1) * CH)
                base[v, :, cut] = volume[v]
                for f in range(4):
                    here = pl.ds(pl.multiple_of(f * E + off, LANES), CH)
                    tab[v, :, here] = g[72 + f * 16 : 80 + f * 16, cols]
                    tab[Q + v, :, here] = g[80 + f * 16 : 88 + f * 16, cols]
                otail[v, :, cut] = g[136:144, cols]
            pair = lax.broadcasted_iota(jnp.int32, (8, CH), 0) // 2
            for f in range(4):
                here = pl.ds(pl.multiple_of(f * E + off, LANES), CH)
                for j in range(3):
                    packed = None
                    for v in range(4 * j, min(4 * j + 4, Q)):
                        val = g[80 + f * 16 : 88 + f * 16, v * CH : (v + 1) * CH]
                        packed = val if packed is None else jnp.where(pair == v % 4, val, packed)
                    tab2[j, :, here] = packed

    per = E // (CH * GROUP)
    for i in range(DOFS):
        near[f"dof{i}"].wait()
        lax.fori_loop(i * per // DOFS, (i + 1) * per // DOFS, predictor, 0)
    near["sea_face"].wait()

    shift = lax.rem(devices - me, devices)
    ups = [jnp.broadcast_to(tab[8, 0:1, t * LANES : (t + 1) * LANES], (8, LANES)) for t in range(4)]
    slots = []
    for r in range(8):
        idx = sea_face[r * 8 : r * 8 + 8, :]
        at, which = idx & (LANES - 1), idx >> 7
        val = jnp.zeros((8, LANES), F32)
        for t in range(4):
            val = jnp.where(which == t, jnp.take_along_axis(ups[t], at, axis=1), val)
        slots.append(val)
    handed = pltpu.roll(jnp.concatenate(slots, axis=0), shift, 1)
    zeros64 = jnp.zeros((64, LANES), F32)
    hand[...] = jnp.transpose(jnp.concatenate([handed, zeros64], axis=0))

    pl.semaphore_wait(barrier, len(greet))

    copies = []

    def push(src, dst, offset):
        k = len(copies)
        copy = pltpu.make_async_remote_copy(
            src_ref=src,
            dst_ref=dst,
            send_sem=send_sem.at[k],
            recv_sem=recv_sem.at[k],
            device_id=device(offset),
            device_id_type=FLAT,
        )
        copy.start()
        copies.append(copy)
        return copy

    hand_offsets = (1, n_tile, devices // 2)
    hand_copies = []
    for k, o in enumerate(hand_offsets):
        row = o // 8 * 8
        hand_copies.append(push(hand.at[row : row + 8, :], hand_in.at[k], o))

    near["send"].wait()
    sidx[...] = jnp.zeros_like(sidx)
    sidx[0:11, 0:SLOTS] = send[...]
    def gather(sources, idx, tiles):
        at, which = idx & (LANES - 1), idx >> 7
        res = [jnp.zeros((8, LANES), F32)] * len(sources)
        for t in tiles:
            mask = which == t
            for k, source in enumerate(sources):
                val = jnp.take_along_axis(source[:, t * LANES : (t + 1) * LANES], at, axis=1)
                res[k] = jnp.where(mask, val, res[k])
        return res

    direct = range(TILES)
    pair = sub // 2
    block = lane // SLOTS
    places = [(v // 4, v % 4) for v in range(Q)] + [(2, 1 + j) for j in range(3)]
    dg_copies = []
    rows = []
    for p in range(RTILES):
        idx = jnp.zeros((8, LANES), jnp.int32)
        for n in range(4 * p, min(4 * p + 4, len(offsets))):
            row = jnp.broadcast_to(sidx[n : n + 1, :], (8, LANES))
            idx = jnp.where(block == n % 4, pltpu.roll(row, SLOTS * (n % 4), 1), idx)
        rows.append(idx)
    for p in reversed(range(RTILES)):
        members = [n for n in range(4 * p, 4 * p + 4) if n < len(offsets)]
        sources = [tab.at[v] for v in range(Q)] + [tab2.at[j] for j in range(3)]
        got = gather(sources, rows[p], direct)
        for n in members:
            for r in range(3):
                packed = None
                for k, (pr, pb) in enumerate(places):
                    if pr != r:
                        continue
                    turn = (SLOTS * (pb - n % 4)) % LANES
                    val = pltpu.roll(got[k], turn, 1) if turn else got[k]
                    packed = val if packed is None else jnp.where(block == pb, val, packed)
                msg[n, r * 8 : r * 8 + 8, :] = packed
        for n in members:
            dg_copies.append(push(msg.at[n], msg_in.at[n], offsets[n]))

    for t in range(4):
        near[f"momentum{t}"].wait()
        near[f"depth{t}"].wait()
        near[f"height{t}"].wait()
    top, low = slice(ROW0, ROW0 + 8), slice(ROW0 + 56, ROW0 + 64)
    above, below = slice(ROW0 - 8, ROW0), slice(ROW0 + 64, ROW0 + 72)
    group = lane // 8

    def column(ring, t):
        res = None
        for r in range(8):
            val = ring[t, ROW0 + 8 * r : ROW0 + 8 * r + 8, :]
            turn = (8 * r + (8 if t else 0)) % LANES
            val = pltpu.roll(val, turn, 1) if turn else val
            res = val if res is None else jnp.where(group == r, val, res)
        return res

    corners = ((0, top), (3, top), (0, low), (3, low))
    for side, t in ((0, 0), (1, 3)):
        fx, fy, dp = (column(flow.at[k], t) for k in range(3))
        flow_side[side, 0] = jnp.where(lane < 64, fx, pltpu.roll(fy, 64, 1))
        flow_side[side, 1] = dp
    for k, (t, rows) in enumerate(corners):
        turns = (0, 8, 16) if t == 0 else (0, LANES - 8, LANES - 16)
        fx, fy, dp = (
            pltpu.roll(flow[i, t, rows, :], turns[i], 1) if i else flow[i, t, rows, :]
            for i in range(3)
        )
        spot = group if t == 0 else 15 - group
        flow_corner[k] = jnp.where(spot == 0, fx, jnp.where(spot == 1, fy, dp))
    corner_offsets = (-n_tile - 1, -n_tile + 1, n_tile - 1, n_tile + 1)
    cols = slice(0, 4)
    flow_copies = [
        push(flow.at[:, cols, top, :], flow.at[:, cols, below, :], -n_tile),
        push(flow.at[:, cols, low, :], flow.at[:, cols, above, :], n_tile),
        push(flow_side.at[0], flow_side_in.at[0], -1),
        push(flow_side.at[1], flow_side_in.at[1], 1),
    ]
    for k, o in enumerate(corner_offsets):
        flow_copies.append(push(flow_corner.at[k], flow_corner_in.at[k], o))

    for name in ("nbr", "nrm", "fscale", "cluster", "sea_cell"):
        near[name].wait()
    inv_den = 1.0 / density[...]
    speed = jnp.sqrt((lame[...] + 2.0 * shear[...]) * inv_den)
    half = 0.5 * fscale[...]
    scaled = [half * nrm[j] for j in range(3)]
    coefs = (
        scaled
        + [shear[...] * s for s in scaled]
        + [inv_den * s for s in scaled]
        + [half * speed]
    )
    for k, c in enumerate(coefs):
        for f in range(4):
            coef[k, 2 * f : 2 * f + 2, :] = jnp.broadcast_to(c[f : f + 1, :], (2, E))
    for f in range(4):
        nbr8[2 * f : 2 * f + 2, :] = jnp.broadcast_to(nbr[f : f + 1, :], (2, E))
    def index(f, cut):
        if f < 4:
            return jnp.broadcast_to(nbr[f : f + 1, cut], (8, LANES))
        return nbr8[:, cut]

    def local_gather(i, _):
        for et in range(AHEAD):
            off = pl.multiple_of((i * AHEAD + et) * LANES, LANES)
            cut = pl.ds(off, LANES)
            for f in range(5):
                here = pl.ds(pl.multiple_of(f * E + off, LANES), LANES)
                got = gather([tab.at[v + Q * (f // 4)] for v in range(Q)], index(f, cut), direct)
                for v in range(Q):
                    acc[v, :, here] = got[v] - (tab[v, :, here] if f < 4 else otail[v, :, cut])
        return 0

    lax.fori_loop(0, 2 // AHEAD, local_gather, 0)

    for c in hand_copies:
        c.wait_recv()
    back = (0, devices - 1, devices - n_tile, devices // 2)
    cells = pltpu.roll(sea_cell[...], shift, 1)
    cells_t = jnp.transpose(
        jnp.concatenate([cells, jnp.zeros((64, LANES), jnp.int32)], axis=0).astype(F32)
    ).astype(jnp.int32)
    values = [hand[0:1, :]]
    for k, o in enumerate(hand_offsets):
        values.append(hand_in[k, o % 8 : o % 8 + 1, :])
    row_ids = lax.broadcasted_iota(jnp.int32, (64, LANES), 0)
    highs, lows = [], []
    for k in range(0, 4, 2):
        pair_v = values[k] + pltpu.roll(values[k + 1], 64, 1)
        pair_c = cells_t[back[k] : back[k] + 1, :] + pltpu.roll(
            cells_t[back[k + 1] : back[k + 1] + 1, :], 64, 1
        )
        v_high, v_low = split(pair_v)
        here = row_ids == jnp.broadcast_to(pair_c >> 9, (64, LANES))
        highs.append(jnp.where(here, v_high, 0.0))
        lows.append(jnp.where(here, v_low, 0.0))
    left = jnp.concatenate(
        [jnp.concatenate(highs, axis=1), jnp.concatenate(lows, axis=1)], axis=0
    ).astype(BF16)
    col_ids = lax.broadcasted_iota(jnp.int32, (64, E), 1)
    picks = []
    for k in range(4):
        chosen = jnp.broadcast_to(cells[:, back[k] : back[k] + 1] & (E - 1), (64, E))
        picks.append(jnp.where(col_ids == chosen, 1.0, 0.0).astype(BF16))
    lifted = jnp.dot(left, jnp.concatenate(picks, axis=0), preferred_element_type=F32)
    for t in range(4):
        lanes = slice(t * LANES, (t + 1) * LANES)
        level[t, ROW0 : ROW0 + 64, :] += lifted[0:64, lanes] + lifted[64:128, lanes]
    for side, t in ((0, 0), (1, 3)):
        level_side[side] = column(level, t)
    level_copies = [
        push(level.at[cols, top, :], level.at[cols, below, :], -n_tile),
        push(level.at[cols, low, :], level.at[cols, above, :], n_tile),
        push(level_side.at[0], level_side_in.at[0], -1),
        push(level_side.at[1], level_side_in.at[1], 1),
    ]
    for k, (o, (t, rows)) in enumerate(zip(corner_offsets, corners)):
        level_copies.append(push(level.at[t, rows, :], level_corner_in.at[k], o))

    lax.fori_loop(2 // AHEAD, 4 // AHEAD, local_gather, 0)

    for c in dg_copies:
        c.wait_recv()
    for p in range(RTILES):
        members = [n for n in range(4 * p, 4 * p + 4) if n < len(offsets)]
        cols = slice((TILES + p) * LANES, (TILES + p + 1) * LANES)
        unpacked = []
        for k, (pr, pb) in enumerate(places):
            res = None
            for n in members:
                val = msg_in[n, pr * 8 : pr * 8 + 8, :]
                turn = (SLOTS * (n % 4 - pb)) % LANES
                val = pltpu.roll(val, turn, 1) if turn else val
                res = val if res is None else jnp.where(block == n % 4, val, res)
            unpacked.append(res)
        for j in range(3):
            tails[p * 3 + j] = unpacked[Q + j]
        for v in range(Q):
            r = 2 * (v % 4)
            first = jnp.broadcast_to(tails[p * 3 + v // 4, r : r + 1, :], (8, LANES))
            second = jnp.broadcast_to(tails[p * 3 + v // 4, r + 1 : r + 2, :], (8, LANES))
            tab[v, :, cols] = unpacked[v]
            tab[Q + v, :, cols] = jnp.where(sub % 2 == 0, first, second)
    def finish_one(off):
        cut = pl.ds(off, LANES)
        lam = lame[:, cut]
        remote = range(TILES, TILES + RTILES)
        parts = [[] for _ in range(Q)]
        for f in range(5):
            here = pl.ds(pl.multiple_of(f * E + off, LANES), LANES)
            if f < 4:
                c = [coef[k, 2 * f : 2 * f + 1, cut] for k in range(10)]
            else:
                c = [coef[k, :, cut] for k in range(10)]
            got = gather([tab.at[v + Q * (f // 4)] for v in range(Q)], index(f, cut), remote)
            jump = [acc[v, :, here] + got[v] for v in range(Q)]
            u = jump[6:9]
            n, mun, rhn, ws = c[0:3], c[3:6], c[6:9], c[9]
            flux = lam * (u[0] * n[0] + u[1] * n[1] + u[2] * n[2])
            res = []
            for i in range(3):
                push_i = u[i] * mun[i]
                res.append(flux + (push_i + push_i) + ws * jump[i])
            for k, (i, j) in enumerate(STRESS_ORDER[3:]):
                res.append(u[i] * mun[j] + u[j] * mun[i] + ws * jump[3 + k])
            for i in range(3):
                s = STRESS_PAIRS[i]
                res.append(
                    jump[s[0]] * rhn[0] + jump[s[1]] * rhn[1] + jump[s[2]] * rhn[2] + ws * u[i]
                )
            for v in range(Q):
                parts[v].append(res[v])
        right = jnp.concatenate([jnp.concatenate(x, axis=0) for x in parts], axis=1)
        high, low = split(right)
        right = jnp.concatenate([high, low, high], axis=0).astype(BF16)
        lifts = jnp.dot(l_all, right, preferred_element_type=F32)
        chosen = jnp.broadcast_to(cluster[:, cut], (B, LANES)) == 1
        for v in range(Q):
            x = x_ref[v, :, cut]
            new = x + (base[v, 0:B, cut] + lifts[0:B, v * LANES : (v + 1) * LANES])
            out[v, :, cut] = jnp.where(chosen, new, x)

    def finish(i, _):
        for et in range(SIDE):
            finish_one(pl.multiple_of((i * SIDE + et) * LANES, LANES))
        return 0

    lax.fori_loop(0, E // LANES // SIDE, finish, 0)
    for c in hand_copies + dg_copies:
        c.wait_send()
    for c in flow_copies:
        c.wait()
    above_ok, below_ok, right_ok, left_ok = inside(n_dom, n_tile)

    def close(ring, side, corner, res, scale):
        for t in range(4):
            res[t, ROW0 - 8 : ROW0, :] = ring[t, ROW0 - 8 : ROW0, :] * (above_ok * scale)
            res[t, ROW0 + 64 : ROW0 + 72, :] = ring[t, ROW0 + 64 : ROW0 + 72, :] * (below_ok * scale)
            val = ring[t, grid_rows, :]
            res[t, grid_rows, :] = val * scale if scale != 1.0 else val
        side_ok = jnp.where(lane < 64, right_ok, left_ok) * scale
        for r in range(8):
            right, left = side(r)
            res[4, ROW0 + 8 * r : ROW0 + 8 * r + 8, :] = jnp.where(lane < 64, right, left) * side_ok
        res[4, below, :] = jnp.where(lane < 64, corner(0), corner(1)) * (side_ok * below_ok)
        res[4, above, :] = jnp.where(lane < 64, corner(2), corner(3)) * (side_ok * above_ok)
        for t in range(5):
            res[t, 0:8, :] = jnp.zeros((8, LANES), F32)
            res[t, ROWS - 8 : ROWS, :] = jnp.zeros((8, LANES), F32)

    def turned(val, turn):
        return pltpu.roll(val, turn % LANES, 1) if turn % LANES else val

    for k in range(3):
        start = 64 if k == 1 else 0
        from_right, from_left = flow_side_in[0, k // 2], flow_side_in[1, k // 2]

        def side(r):
            at = start + 8 * r
            return turned(from_right, -at), turned(from_left, LANES - 8 - at)

        def corner(j):
            return turned(flow_corner_in[j], (-8 if j % 2 == 0 else 8) * k)

        close(flow.at[k], side, corner, flow_out.at[k], 0.5 * WAVE_RATE if k == 2 else 1.0)
    for c in level_copies:
        c.wait()
    from_right, from_left = level_side_in[0], level_side_in[1]

    def level_sides(r):
        return turned(from_right, -8 * r), turned(from_left, LANES - 8 - 8 * r)

    close(level, level_sides, lambda j: level_corner_in[j], level_out, 1.0)


def inside(n_dom, n_tile):
    dom, tile = lax.axis_index("dom"), lax.axis_index("tile")
    return (
        jnp.where(dom > 0, 1.0, 0.0),
        jnp.where(dom < n_dom - 1, 1.0, 0.0),
        jnp.where(tile < n_tile - 1, 1.0, 0.0),
        jnp.where(tile > 0, 1.0, 0.0),
    )


def grid_kernel(n_dom, n_tile, dof, flow_in, level_in, dof_out, height_out, momentum_out, *rest):
    flow, level, sem = rest
    dof_copy = pltpu.make_async_copy(dof, dof_out, sem.at[0])
    dof_copy.start()
    above_ok, below_ok, right_ok, left_ok = inside(n_dom, n_tile)
    c0 = 0.5 * WAVE_RATE
    lane = lax.broadcasted_iota(jnp.int32, (8, LANES), 1)
    side_ok = jnp.where(lane < 64, right_ok, left_ok)
    for ring in (flow.at[0], level):
        for t in range(5):
            ring[t, 0:8, :] = jnp.zeros((8, LANES), F32)
            ring[t, ROWS - 8 : ROWS, :] = jnp.zeros((8, LANES), F32)

    def across(vals):
        fwd = [pltpu.roll(x, LANES - 1, 1) for x in vals]
        bwd = [pltpu.roll(x, 1, 1) for x in vals]
        res = []
        for t in range(5):
            nxt = jnp.where(lane == LANES - 1, fwd[(t + 1) % 5], fwd[t])
            prv = jnp.where(lane == 0, bwd[(t + 4) % 5], bwd[t])
            res.append(nxt - prv)
        return res

    def rise(flow_old, level_old):
        for r in range(10):
            at = ROW0 - 8 + 8 * r
            rows = slice(at, at + 8)
            row_ok = above_ok if r == 0 else below_ok if r == 9 else 1.0
            diff = across([flow_old[1, t, rows, :] for t in range(5)])
            for t in range(5):
                spread = flow_old[0, t, at + 1 : at + 9, :] - flow_old[0, t, at - 1 : at + 7, :]
                rate = c0 * row_ok * side_ok if t == 4 else c0 * row_ok
                level[t, rows, :] = level_old[t, rows, :] - rate * (spread + diff[t])

    def push(flow_old, t, at, diff):
        rows = slice(at, at + 8)
        g = flow_in[2, t, rows, :]
        slope = level[t, at + 1 : at + 9, :] - level[t, at - 1 : at + 7, :]
        flow[0, t, rows, :] = flow_old[0, t, rows, :] - g * slope
        flow[1, t, rows, :] = flow_old[1, t, rows, :] - g * diff

    def wave(flow_old, level_old):
        rise(flow_old, level_old)
        for r in range(10):
            at = ROW0 - 8 + 8 * r
            diff = across([level[t, at : at + 8, :] for t in range(5)])
            for t in range(5):
                push(flow_old, t, at, diff[t])

    wave(flow_in, level_in)

    def again(_, carry):
        wave(flow, level)
        return carry

    lax.fori_loop(0, STEPS - 2, again, 0)
    rise(flow, level)
    copies = [dof_copy]
    rows = slice(ROW0, ROW0 + 64)

    def send(src, dst):
        copies.append(pltpu.make_async_copy(src, dst, sem.at[len(copies)]))
        copies[-1].start()

    for t in range(4):
        send(level.at[t, rows, :], height_out.at[:, t * LANES : (t + 1) * LANES])
    for t in range(4):
        for r in range(8):
            at = ROW0 + 8 * r
            here = level[t, at : at + 8, :]
            ahead = level[t + 1, at : at + 8, :]
            behind = level[(t + 4) % 5, at : at + 8, :]
            nxt = jnp.where(lane == LANES - 1, pltpu.roll(ahead, LANES - 1, 1), pltpu.roll(here, LANES - 1, 1))
            prv = jnp.where(lane == 0, pltpu.roll(behind, 1, 1), pltpu.roll(here, 1, 1))
            push(flow, t, at, nxt - prv)
        send(flow.at[:, t, rows, :], momentum_out.at[:, :, t * LANES : (t + 1) * LANES])
    for c in copies:
        c.wait()


def shards(
    dof_values,
    density,
    lame_lambda,
    shear_modulus,
    jacobian,
    normals,
    face_scale,
    derivative,
    face_proj,
    lift_matrix,
    neighbour,
    send_face,
    cluster,
    sea_face,
    sea_cell,
    height,
    momentum,
    ocean_depth,
):
    n_dom, n_tile = lax.axis_size("dom"), lax.axis_size("tile")
    row = lambda x: x.reshape(1, x.shape[0])
    vmem = pl.BlockSpec(memory_space=pltpu.VMEM)
    far = pl.BlockSpec(memory_space=pltpu.HBM)
    table = (TILES + RTILES) * LANES
    args = (
        jnp.transpose(dof_values, (1, 0, 2)),
        row(density),
        row(lame_lambda),
        row(shear_modulus),
        jacobian,
        jnp.transpose(normals, (1, 0, 2)),
        face_scale,
        derivative,
        jnp.transpose(face_proj, (1, 0, 2)),
        jnp.transpose(lift_matrix, (2, 0, 1)),
        neighbour,
        send_face,
        row(cluster),
        jnp.transpose(sea_face),
        jnp.transpose(sea_cell),
        height,
        momentum,
        ocean_depth,
    )
    dof_new, flow, level = pl.pallas_call(
        functools.partial(kernel, n_dom, n_tile),
        out_shape=(
            pltpu.VMEM((Q, B, E), F32),
            pltpu.VMEM((3, 5, ROWS, LANES), F32),
            pltpu.VMEM((5, ROWS, LANES), F32),
        ),
        in_specs=[far] * 18,
        out_specs=(vmem,) * 3,
        scratch_shapes=[pltpu.VMEM(x.shape, x.dtype) for x in args[:15]]
        + [
            pltpu.VMEM((Q, BP, E), F32),
            pltpu.VMEM((2 * Q, 8, table), F32),
            pltpu.VMEM((3, 8, TILES * LANES), F32),
            pltpu.VMEM((Q, 8, E), F32),
            pltpu.VMEM((Q, 8, 5 * E), F32),
            pltpu.VMEM((144, LANES), F32),
            pltpu.VMEM((LANES, LANES), F32),
            pltpu.VMEM((16, LANES), jnp.int32),
            pltpu.VMEM((8, E), jnp.int32),
            pltpu.VMEM((10, 8, E), F32),
            pltpu.VMEM((11, 24, LANES), F32),
            pltpu.VMEM((11, 24, LANES), F32),
            pltpu.VMEM((9, 8, LANES), F32),
            pltpu.VMEM((LANES, LANES), F32),
            pltpu.VMEM((3, 8, LANES), F32),
            pltpu.VMEM((3, 5, ROWS, LANES), F32),
            pltpu.VMEM((5, ROWS, LANES), F32),
            pltpu.VMEM((2, 2, 8, LANES), F32),
            pltpu.VMEM((2, 2, 8, LANES), F32),
            pltpu.VMEM((4, 8, LANES), F32),
            pltpu.VMEM((4, 8, LANES), F32),
            pltpu.VMEM((2, 8, LANES), F32),
            pltpu.VMEM((2, 8, LANES), F32),
            pltpu.VMEM((4, 8, LANES), F32),
            pltpu.SemaphoreType.DMA((32,)),
            pltpu.SemaphoreType.DMA((30,)),
            pltpu.SemaphoreType.DMA((30,)),
        ],
        compiler_params=pltpu.CompilerParams(
            collective_id=0, has_side_effects=True, vmem_limit_bytes=VMEM
        ),
    )(*args)
    dof_out, height_out, momentum_out = pl.pallas_call(
        functools.partial(grid_kernel, n_dom, n_tile),
        out_shape=(
            jax.ShapeDtypeStruct((Q, B, E), F32),
            jax.ShapeDtypeStruct(height.shape, F32),
            jax.ShapeDtypeStruct(momentum.shape, F32),
        ),
        in_specs=[vmem] * 3,
        out_specs=(far,) * 3,
        scratch_shapes=[
            pltpu.VMEM((2, 5, ROWS, LANES), F32),
            pltpu.VMEM((5, ROWS, LANES), F32),
            pltpu.SemaphoreType.DMA((9,)),
        ],
        compiler_params=pltpu.CompilerParams(vmem_limit_bytes=16 << 20),
    )(dof_new, flow, level)
    return jnp.transpose(dof_out, (1, 0, 2)), height_out, momentum_out


def solution(mesh):
    both = ("dom", "tile")
    return jax.shard_map(
        shards,
        mesh=mesh,
        in_specs=(
            P(None, None, both),
            P(both),
            P(both),
            P(both),
            P(None, None, both),
            P(None, None, both),
            P(None, both),
            P(),
            P(),
            P(),
            P(None, both),
            P(both, None),
            P(both),
            P(both, None),
            P(both, None),
            P("dom", "tile"),
            P(None, "dom", "tile"),
            P("dom", "tile"),
        ),
        out_specs=(P(None, None, both), P("dom", "tile"), P(None, "dom", "tile")),
        check_vma=False,
    )
```

```python
import functools

import jax
import jax.numpy as jnp
from jax import lax
from jax.experimental import pallas as pl
from jax.experimental.pallas import tpu as pltpu
from jax.sharding import PartitionSpec as P

STEPS = 4
STRESS_PAIRS = ((0, 3, 5), (3, 1, 4), (5, 4, 2))
STRESS_ORDER = ((0, 0), (1, 1), (2, 2), (0, 1), (1, 2), (0, 2))
STEP_SIZE = 0.3
WAVE_RATE = 0.45
FLAT = pl.DeviceIdType.LOGICAL
F32 = jnp.float32
BF16 = jnp.bfloat16

B = 20
BP = 24
Q = 9
E = 512
CH = 256
GROUP = 2
DOFS = 1
LANES = 128
VMEM = 58 << 20
AHEAD = 1
SIDE = 2
TILES = 16
RTILES = 3
SLOTS = 32
ROW0 = 16
ROWS = 96


def partner_offsets(tile_count, device_count):
    t = tile_count
    return [1, -1, 2, -2, t, -t, t + 1, -(t + 1), 2 * t, -2 * t, device_count // 2]


def split(x):
    high = x.astype(BF16).astype(F32)
    return high, x - high


def stacked(x):
    high, low = split(x)
    pad = jnp.zeros((8,) + x.shape[1:], F32)
    parts = [high, low, high]
    if (3 * x.shape[0]) % 16:
        parts.append(pad)
    return jnp.concatenate(parts, axis=0).astype(BF16)


def kernel(n_dom, n_tile, *refs):
    (
        dof_in,
        density_in,
        lame_in,
        shear_in,
        jac_in,
        nrm_in,
        fscale_in,
        deriv_in,
        fproj_in,
        lift_in,
        nbr_in,
        send_in,
        cluster_in,
        sea_face_in,
        sea_cell_in,
        height,
        momentum,
        depth,
    ) = refs[:18]
    out, flow_out, level_out = refs[18:21]
    (
        x_ref,
        density,
        lame,
        shear,
        jac,
        nrm,
        fscale,
        deriv,
        fproj,
        lift,
        nbr,
        send,
        cluster,
        sea_face,
        sea_cell,
    ) = refs[21:36]
    (
        base,
        tab,
        tab2,
        otail,
        acc,
        amat,
        lmat,
        sidx,
        nbr8,
        coef,
        msg,
        msg_in,
        tails,
        hand,
        hand_in,
        flow,
        level,
        flow_side,
        flow_side_in,
        flow_corner,
        flow_corner_in,
        level_side,
        level_side_in,
        level_corner_in,
        local_sem,
        send_sem,
        recv_sem,
    ) = refs[36:]
    devices = n_dom * n_tile
    dom, tile = lax.axis_index("dom"), lax.axis_index("tile")
    me = dom * n_tile + tile
    offsets = partner_offsets(n_tile, devices)
    greet = offsets + [n_tile - 1, -(n_tile - 1)]

    def device(offset):
        target = me + offset % devices
        return jnp.where(target >= devices, target - devices, target)

    barrier = pltpu.get_barrier_semaphore()
    for o in greet:
        pl.semaphore_signal(barrier, inc=1, device_id=device(o), device_id_type=FLAT)

    near = {}

    def fetch(name, src, dst):
        near[name] = pltpu.make_async_copy(src, dst, local_sem.at[len(near)])
        near[name].start()

    fetch("deriv", deriv_in, deriv)
    fetch("fproj", fproj_in, fproj)
    for i in range(DOFS):
        cut = slice(i * E // DOFS, (i + 1) * E // DOFS)
        fetch(f"dof{i}", dof_in.at[:, :, cut], x_ref.at[:, :, cut])
        if i == 0:
            fetch("density", density_in, density)
            fetch("lame", lame_in, lame)
            fetch("shear", shear_in, shear)
            fetch("jac", jac_in, jac)
    fetch("sea_face", sea_face_in, sea_face)
    fetch("send", send_in, send)
    fetch("nbr", nbr_in, nbr)
    fetch("nrm", nrm_in, nrm)
    fetch("fscale", fscale_in, fscale)
    fetch("cluster", cluster_in, cluster)
    fetch("lift", lift_in, lift)
    fetch("sea_cell", sea_cell_in, sea_cell)
    grid_rows = slice(ROW0, ROW0 + 64)
    first = len(near)
    for t in range(4):
        lanes = slice(t * LANES, (t + 1) * LANES)
        for k, (src, dst) in enumerate(
            (
                (momentum.at[:, :, lanes], flow.at[0:2, t, grid_rows, :]),
                (depth.at[:, lanes], flow.at[2, t, grid_rows, :]),
                (height.at[:, lanes], level.at[t, grid_rows, :]),
            )
        ):
            pltpu.make_async_copy(src, dst, local_sem.at[first + k]).start()

    def wait_all(ref, sem):
        pltpu.make_async_copy(ref, ref, sem).wait()

    lane = lax.broadcasted_iota(jnp.int32, (8, LANES), 1)
    sub = lax.broadcasted_iota(jnp.int32, (8, LANES), 0)

    for name in ("deriv", "fproj"):
        near[name].wait()
    amat[...] = jnp.zeros_like(amat)
    for d in range(3):
        amat[d * BP : d * BP + B, 0:B] = deriv[d]
    for f in range(4):
        for c in range(10):
            row = fproj[c, f : f + 1, :]
            if c < 8:
                amat[72 + f * 16 + c : 73 + f * 16 + c, 0:B] = row
            else:
                k = 32 + f * 2 + c - 8
                amat[104 + k : 105 + k, 0:B] = row
                for r in range(4):
                    k = 80 + f * 16 + r * 2 + c - 8
                    amat[k : k + 1, 0:B] = row
    a_high, a_low = split(amat[...])
    a_all = a_high + pltpu.roll(a_high, BP, 1) + pltpu.roll(a_low, 2 * BP, 1)
    a_all = a_all.astype(BF16)[:, 0:80]
    for name in ("density", "lame", "shear", "jac"):
        near[name].wait()

    def predictor(i, _):
        chunks = []
        for h in range(GROUP):
            off = pl.multiple_of((i * GROUP + h) * CH, CH)
            chunks.append(Chunk(off))
        for k in range(1, 4):
            for c in chunks:
                c.advance(k)
        for c in chunks:
            c.finish()
        return 0

    class Chunk:
        def __init__(self, off):
            self.off = off
            self.cut = cut = pl.ds(off, CH)
            self.rho = 1.0 / density[:, cut]
            self.lam = lame[:, cut]
            self.mu = shear[:, cut]
            self.jc = [[jac[d, x : x + 1, cut] for x in range(3)] for d in range(3)]
            pad = jnp.zeros((BP - B, CH), F32)
            self.term = [
                STEP_SIZE * jnp.concatenate([x_ref[v, :, cut], pad], axis=0) for v in range(Q)
            ]
            self.integral = self.term

        def combine(self, g, scale):
            jc = [[x * scale for x in row] for row in self.jc] if scale != 1.0 else self.jc
            lam, mu, rho = self.lam, self.mu, self.rho

            def phys(x, v):
                return (
                    jc[0][x] * g[0:BP, v * CH : (v + 1) * CH]
                    + jc[1][x] * g[BP : 2 * BP, v * CH : (v + 1) * CH]
                    + jc[2][x] * g[2 * BP : 3 * BP, v * CH : (v + 1) * CH]
                )

            vg = [[phys(j, 6 + i) for j in range(3)] for i in range(3)]
            div = lam * (vg[0][0] + vg[1][1] + vg[2][2])
            res = [div + (mu + mu) * vg[i][i] for i in range(3)]
            res += [mu * (vg[i][j] + vg[j][i]) for i, j in STRESS_ORDER[3:]]
            for i in range(3):
                s = STRESS_PAIRS[i]
                res.append(rho * (phys(0, s[0]) + phys(1, s[1]) + phys(2, s[2])))
            return res

        def advance(self, k):
            right = stacked(jnp.concatenate(self.term, axis=1))
            g = jnp.dot(a_all[0:72], right, preferred_element_type=F32)
            self.term = self.combine(g, STEP_SIZE / (k + 1))
            self.integral = [s + w for s, w in zip(self.integral, self.term)]

        def finish(self):
            off, cut = self.off, self.cut
            right = stacked(jnp.concatenate(self.integral, axis=1))
            g = jnp.dot(a_all, right, preferred_element_type=F32)
            volume = self.combine(g, 1.0)
            for v in range(Q):
                cols = slice(v * CH, (v + 1) * CH)
                base[v, :, cut] = volume[v]
                for f in range(4):
                    here = pl.ds(pl.multiple_of(f * E + off, LANES), CH)
                    tab[v, :, here] = g[72 + f * 16 : 80 + f * 16, cols]
                    tab[Q + v, :, here] = g[80 + f * 16 : 88 + f * 16, cols]
                otail[v, :, cut] = g[136:144, cols]
            pair = lax.broadcasted_iota(jnp.int32, (8, CH), 0) // 2
            for f in range(4):
                here = pl.ds(pl.multiple_of(f * E + off, LANES), CH)
                for j in range(3):
                    packed = None
                    for v in range(4 * j, min(4 * j + 4, Q)):
                        val = g[80 + f * 16 : 88 + f * 16, v * CH : (v + 1) * CH]
                        packed = val if packed is None else jnp.where(pair == v % 4, val, packed)
                    tab2[j, :, here] = packed

    per = E // (CH * GROUP)
    for i in range(DOFS):
        near[f"dof{i}"].wait()
        lax.fori_loop(i * per // DOFS, (i + 1) * per // DOFS, predictor, 0)
    near["sea_face"].wait()

    shift = lax.rem(devices - me, devices)
    ups = [jnp.broadcast_to(tab[8, 0:1, t * LANES : (t + 1) * LANES], (8, LANES)) for t in range(4)]
    slots = []
    for r in range(8):
        idx = sea_face[r * 8 : r * 8 + 8, :]
        at, which = idx & (LANES - 1), idx >> 7
        val = jnp.zeros((8, LANES), F32)
        for t in range(4):
            val = jnp.where(which == t, jnp.take_along_axis(ups[t], at, axis=1), val)
        slots.append(val)
    handed = pltpu.roll(jnp.concatenate(slots, axis=0), shift, 1)
    zeros64 = jnp.zeros((64, LANES), F32)
    hand[...] = jnp.transpose(jnp.concatenate([handed, zeros64], axis=0))

    pl.semaphore_wait(barrier, len(greet))

    def push(src, dst, offset, group):
        pltpu.make_async_remote_copy(
            src_ref=src,
            dst_ref=dst,
            send_sem=send_sem.at[group],
            recv_sem=recv_sem.at[group],
            device_id=device(offset),
            device_id_type=FLAT,
        ).start()

    hand_offsets = (1, n_tile, devices // 2)
    for k, o in enumerate(hand_offsets):
        row = o // 8 * 8
        push(hand.at[row : row + 8, :], hand_in.at[k], o, 0)

    near["send"].wait()
    sidx[...] = jnp.zeros_like(sidx)
    sidx[0:11, 0:SLOTS] = send[...]
    def gather(sources, idx, tiles):
        at, which = idx & (LANES - 1), idx >> 7
        res = [jnp.zeros((8, LANES), F32)] * len(sources)
        for t in tiles:
            mask = which == t
            for k, source in enumerate(sources):
                val = jnp.take_along_axis(source[:, t * LANES : (t + 1) * LANES], at, axis=1)
                res[k] = jnp.where(mask, val, res[k])
        return res

    direct = range(TILES)
    pair = sub // 2
    block = lane // SLOTS
    places = [(v // 4, v % 4) for v in range(Q)] + [(2, 1 + j) for j in range(3)]
    rows = []
    for p in range(RTILES):
        idx = jnp.zeros((8, LANES), jnp.int32)
        for n in range(4 * p, min(4 * p + 4, len(offsets))):
            row = jnp.broadcast_to(sidx[n : n + 1, :], (8, LANES))
            idx = jnp.where(block == n % 4, pltpu.roll(row, SLOTS * (n % 4), 1), idx)
        rows.append(idx)
    for p in reversed(range(RTILES)):
        members = [n for n in range(4 * p, 4 * p + 4) if n < len(offsets)]
        sources = [tab.at[v] for v in range(Q)] + [tab2.at[j] for j in range(3)]
        got = gather(sources, rows[p], direct)
        for n in members:
            for r in range(3):
                packed = None
                for k, (pr, pb) in enumerate(places):
                    if pr != r:
                        continue
                    turn = (SLOTS * (pb - n % 4)) % LANES
                    val = pltpu.roll(got[k], turn, 1) if turn else got[k]
                    packed = val if packed is None else jnp.where(block == pb, val, packed)
                msg[n, r * 8 : r * 8 + 8, :] = packed
        for n in members:
            push(msg.at[n], msg_in.at[n], offsets[n], 1)

    wait_all(flow.at[0:2, 0:4, grid_rows, :], local_sem.at[first])
    wait_all(flow.at[2, 0:4, grid_rows, :], local_sem.at[first + 1])
    wait_all(level.at[0:4, grid_rows, :], local_sem.at[first + 2])
    top, low = slice(ROW0, ROW0 + 8), slice(ROW0 + 56, ROW0 + 64)
    above, below = slice(ROW0 - 8, ROW0), slice(ROW0 + 64, ROW0 + 72)
    group = lane // 8

    def column(ring, t):
        res = None
        for r in range(8):
            val = ring[t, ROW0 + 8 * r : ROW0 + 8 * r + 8, :]
            turn = (8 * r + (8 if t else 0)) % LANES
            val = pltpu.roll(val, turn, 1) if turn else val
            res = val if res is None else jnp.where(group == r, val, res)
        return res

    corners = ((0, top), (3, top), (0, low), (3, low))
    for side, t in ((0, 0), (1, 3)):
        fx, fy, dp = (column(flow.at[k], t) for k in range(3))
        flow_side[side, 0] = jnp.where(lane < 64, fx, pltpu.roll(fy, 64, 1))
        flow_side[side, 1] = dp
    for k, (t, rows) in enumerate(corners):
        turns = (0, 8, 16) if t == 0 else (0, LANES - 8, LANES - 16)
        fx, fy, dp = (
            pltpu.roll(flow[i, t, rows, :], turns[i], 1) if i else flow[i, t, rows, :]
            for i in range(3)
        )
        spot = group if t == 0 else 15 - group
        flow_corner[k] = jnp.where(spot == 0, fx, jnp.where(spot == 1, fy, dp))
    corner_offsets = (-n_tile - 1, -n_tile + 1, n_tile - 1, n_tile + 1)
    cols = slice(0, 4)
    push(flow.at[:, cols, top, :], flow.at[:, cols, below, :], -n_tile, 2)
    push(flow.at[:, cols, low, :], flow.at[:, cols, above, :], n_tile, 2)
    push(flow_side.at[0], flow_side_in.at[0], -1, 2)
    push(flow_side.at[1], flow_side_in.at[1], 1, 2)
    for k, o in enumerate(corner_offsets):
        push(flow_corner.at[k], flow_corner_in.at[k], o, 2)

    for name in ("nbr", "nrm", "fscale", "cluster", "sea_cell", "lift"):
        near[name].wait()
    lmat[...] = jnp.zeros_like(lmat)
    for f in range(4):
        for c in range(10):
            k = f * 8 + c if c < 8 else 32 + f * 2 + c - 8
            lmat[k : k + 1, 0:B] = lift[c, f : f + 1, :]
    l_high, l_low = split(jnp.transpose(lmat[...]))
    l_high, l_low = l_high[0:BP], l_low[0:BP]
    l_all = l_high + pltpu.roll(l_high, 40, 1) + pltpu.roll(l_low, 80, 1)
    l_all = l_all.astype(BF16)[:, 0:120]
    inv_den = 1.0 / density[...]
    speed = jnp.sqrt((lame[...] + 2.0 * shear[...]) * inv_den)
    half = 0.5 * fscale[...]
    scaled = [half * nrm[j] for j in range(3)]
    coefs = (
        scaled
        + [shear[...] * s for s in scaled]
        + [inv_den * s for s in scaled]
        + [half * speed]
    )
    for k, c in enumerate(coefs):
        for f in range(4):
            coef[k, 2 * f : 2 * f + 2, :] = jnp.broadcast_to(c[f : f + 1, :], (2, E))
    for f in range(4):
        nbr8[2 * f : 2 * f + 2, :] = jnp.broadcast_to(nbr[f : f + 1, :], (2, E))
    def index(f, cut):
        if f < 4:
            return jnp.broadcast_to(nbr[f : f + 1, cut], (8, LANES))
        return nbr8[:, cut]

    def local_gather(i, _):
        for et in range(AHEAD):
            off = pl.multiple_of((i * AHEAD + et) * LANES, LANES)
            cut = pl.ds(off, LANES)
            for f in range(5):
                here = pl.ds(pl.multiple_of(f * E + off, LANES), LANES)
                got = gather([tab.at[v + Q * (f // 4)] for v in range(Q)], index(f, cut), direct)
                for v in range(Q):
                    acc[v, :, here] = got[v] - (tab[v, :, here] if f < 4 else otail[v, :, cut])
        return 0

    lax.fori_loop(0, 2 // AHEAD, local_gather, 0)

    wait_all(hand_in, recv_sem.at[0])
    back = (0, devices - 1, devices - n_tile, devices // 2)
    cells = pltpu.roll(sea_cell[...], shift, 1)
    cells_t = jnp.transpose(
        jnp.concatenate([cells, jnp.zeros((64, LANES), jnp.int32)], axis=0).astype(F32)
    ).astype(jnp.int32)
    values = [hand[0:1, :]]
    for k, o in enumerate(hand_offsets):
        values.append(hand_in[k, o % 8 : o % 8 + 1, :])
    row_ids = lax.broadcasted_iota(jnp.int32, (64, LANES), 0)
    highs, lows = [], []
    for k in range(0, 4, 2):
        pair_v = values[k] + pltpu.roll(values[k + 1], 64, 1)
        pair_c = cells_t[back[k] : back[k] + 1, :] + pltpu.roll(
            cells_t[back[k + 1] : back[k + 1] + 1, :], 64, 1
        )
        v_high, v_low = split(pair_v)
        here = row_ids == jnp.broadcast_to(pair_c >> 9, (64, LANES))
        highs.append(jnp.where(here, v_high, 0.0))
        lows.append(jnp.where(here, v_low, 0.0))
    left = jnp.concatenate(
        [jnp.concatenate(highs, axis=1), jnp.concatenate(lows, axis=1)], axis=0
    ).astype(BF16)
    col_ids = lax.broadcasted_iota(jnp.int32, (64, E), 1)
    picks = []
    for k in range(4):
        chosen = jnp.broadcast_to(cells[:, back[k] : back[k] + 1] & (E - 1), (64, E))
        picks.append(jnp.where(col_ids == chosen, 1.0, 0.0).astype(BF16))
    lifted = jnp.dot(left, jnp.concatenate(picks, axis=0), preferred_element_type=F32)
    for t in range(4):
        lanes = slice(t * LANES, (t + 1) * LANES)
        level[t, ROW0 : ROW0 + 64, :] += lifted[0:64, lanes] + lifted[64:128, lanes]
    for side, t in ((0, 0), (1, 3)):
        level_side[side] = column(level, t)
    push(level.at[cols, top, :], level.at[cols, below, :], -n_tile, 3)
    push(level.at[cols, low, :], level.at[cols, above, :], n_tile, 3)
    push(level_side.at[0], level_side_in.at[0], -1, 3)
    push(level_side.at[1], level_side_in.at[1], 1, 3)
    for k, (o, (t, rows)) in enumerate(zip(corner_offsets, corners)):
        push(level.at[t, rows, :], level_corner_in.at[k], o, 3)

    lax.fori_loop(2 // AHEAD, 4 // AHEAD, local_gather, 0)

    halo_bytes = flow.at[0, 0:4, 0:64, :]
    wait_all(halo_bytes, recv_sem.at[2])
    wait_all(halo_bytes, send_sem.at[2])
    above_ok, below_ok, right_ok, left_ok = inside(n_dom, n_tile)

    def close(ring, side, corner, res, scale):
        for t in range(4):
            res[t, ROW0 - 8 : ROW0, :] = ring[t, ROW0 - 8 : ROW0, :] * (above_ok * scale)
            res[t, ROW0 + 64 : ROW0 + 72, :] = ring[t, ROW0 + 64 : ROW0 + 72, :] * (below_ok * scale)
            val = ring[t, grid_rows, :]
            res[t, grid_rows, :] = val * scale if scale != 1.0 else val
        side_ok = jnp.where(lane < 64, right_ok, left_ok) * scale
        for r in range(8):
            right, left = side(r)
            res[4, ROW0 + 8 * r : ROW0 + 8 * r + 8, :] = jnp.where(lane < 64, right, left) * side_ok
        res[4, below, :] = jnp.where(lane < 64, corner(0), corner(1)) * (side_ok * below_ok)
        res[4, above, :] = jnp.where(lane < 64, corner(2), corner(3)) * (side_ok * above_ok)
        for t in range(5):
            res[t, 0:8, :] = jnp.zeros((8, LANES), F32)
            res[t, ROWS - 8 : ROWS, :] = jnp.zeros((8, LANES), F32)

    def turned(val, turn):
        return pltpu.roll(val, turn % LANES, 1) if turn % LANES else val

    for k in range(3):
        start = 64 if k == 1 else 0
        from_right, from_left = flow_side_in[0, k // 2], flow_side_in[1, k // 2]

        def side(r):
            at = start + 8 * r
            return turned(from_right, -at), turned(from_left, LANES - 8 - at)

        def corner(j):
            return turned(flow_corner_in[j], (-8 if j % 2 == 0 else 8) * k)

        close(flow.at[k], side, corner, flow_out.at[k], 0.5 * WAVE_RATE if k == 2 else 1.0)
    for k, to in ((1, 1), (2, 3)):
        for r in range(10):
            rows = slice(ROW0 - 8 + 8 * r, ROW0 + 8 * r)
            spun = [pltpu.roll(flow_out[k, t, rows, :], 1, 1) for t in range(5)]
            for t in range(5):
                flow_out[to, t, rows, :] = jnp.where(lane == 0, spun[(t + 4) % 5], spun[t])
    wait_all(msg_in, recv_sem.at[1])
    for p in range(RTILES):
        members = [n for n in range(4 * p, 4 * p + 4) if n < len(offsets)]
        cols = slice((TILES + p) * LANES, (TILES + p + 1) * LANES)
        unpacked = []
        for k, (pr, pb) in enumerate(places):
            res = None
            for n in members:
                val = msg_in[n, pr * 8 : pr * 8 + 8, :]
                turn = (SLOTS * (n % 4 - pb)) % LANES
                val = pltpu.roll(val, turn, 1) if turn else val
                res = val if res is None else jnp.where(block == n % 4, val, res)
            unpacked.append(res)
        for j in range(3):
            tails[p * 3 + j] = unpacked[Q + j]
        for v in range(Q):
            r = 2 * (v % 4)
            first = jnp.broadcast_to(tails[p * 3 + v // 4, r : r + 1, :], (8, LANES))
            second = jnp.broadcast_to(tails[p * 3 + v // 4, r + 1 : r + 2, :], (8, LANES))
            tab[v, :, cols] = unpacked[v]
            tab[Q + v, :, cols] = jnp.where(sub % 2 == 0, first, second)
    def finish_one(off):
        cut = pl.ds(off, LANES)
        lam = lame[:, cut]
        remote = range(TILES, TILES + RTILES)
        parts = [[] for _ in range(Q)]
        for f in range(5):
            here = pl.ds(pl.multiple_of(f * E + off, LANES), LANES)
            if f < 4:
                c = [coef[k, 2 * f : 2 * f + 1, cut] for k in range(10)]
            else:
                c = [coef[k, :, cut] for k in range(10)]
            got = gather([tab.at[v + Q * (f // 4)] for v in range(Q)], index(f, cut), remote)
            jump = [acc[v, :, here] + got[v] for v in range(Q)]
            u = jump[6:9]
            n, mun, rhn, ws = c[0:3], c[3:6], c[6:9], c[9]
            flux = lam * (u[0] * n[0] + u[1] * n[1] + u[2] * n[2])
            res = []
            for i in range(3):
                push_i = u[i] * mun[i]
                res.append(flux + (push_i + push_i) + ws * jump[i])
            for k, (i, j) in enumerate(STRESS_ORDER[3:]):
                res.append(u[i] * mun[j] + u[j] * mun[i] + ws * jump[3 + k])
            for i in range(3):
                s = STRESS_PAIRS[i]
                res.append(
                    jump[s[0]] * rhn[0] + jump[s[1]] * rhn[1] + jump[s[2]] * rhn[2] + ws * u[i]
                )
            for v in range(Q):
                parts[v].append(res[v])
        right = jnp.concatenate([jnp.concatenate(x, axis=0) for x in parts], axis=1)
        high, low = split(right)
        right = jnp.concatenate([high, low, high], axis=0).astype(BF16)
        lifts = jnp.dot(l_all, right, preferred_element_type=F32)
        chosen = jnp.broadcast_to(cluster[:, cut], (B, LANES)) == 1
        for v in range(Q):
            x = x_ref[v, :, cut]
            new = x + (base[v, 0:B, cut] + lifts[0:B, v * LANES : (v + 1) * LANES])
            out[v, :, cut] = jnp.where(chosen, new, x)

    def finish(i, _):
        for et in range(SIDE):
            finish_one(pl.multiple_of((i * SIDE + et) * LANES, LANES))
        return 0

    lax.fori_loop(0, E // LANES // SIDE, finish, 0)
    halo_bytes = level.at[0:2, 0:56, :]
    wait_all(halo_bytes, recv_sem.at[3])
    wait_all(halo_bytes, send_sem.at[3])
    wait_all(hand_in, send_sem.at[0])
    wait_all(msg, send_sem.at[1])
    from_right, from_left = level_side_in[0], level_side_in[1]

    def level_sides(r):
        return turned(from_right, -8 * r), turned(from_left, LANES - 8 - 8 * r)

    close(level, level_sides, lambda j: level_corner_in[j], level_out, 1.0)


def inside(n_dom, n_tile):
    dom, tile = lax.axis_index("dom"), lax.axis_index("tile")
    return (
        jnp.where(dom > 0, 1.0, 0.0),
        jnp.where(dom < n_dom - 1, 1.0, 0.0),
        jnp.where(tile < n_tile - 1, 1.0, 0.0),
        jnp.where(tile > 0, 1.0, 0.0),
    )


def grid_kernel(n_dom, n_tile, dof, flow_in, level_in, dof_out, height_out, momentum_out, *rest):
    flow, level, sem = rest
    dof_copy = pltpu.make_async_copy(dof, dof_out, sem.at[0])
    dof_copy.start()
    above_ok, below_ok, right_ok, left_ok = inside(n_dom, n_tile)
    c0 = 0.5 * WAVE_RATE
    lane = lax.broadcasted_iota(jnp.int32, (8, LANES), 1)
    side_ok = jnp.where(lane < 64, right_ok, left_ok)
    for ring in (flow.at[0], level):
        for t in range(5):
            ring[t, 0:8, :] = jnp.zeros((8, LANES), F32)
            ring[t, ROWS - 8 : ROWS, :] = jnp.zeros((8, LANES), F32)

    def turned(vals, turn):
        spun = [pltpu.roll(x, -turn % LANES, 1) for x in vals]
        edge = lane >= LANES - turn if turn > 0 else lane < -turn
        step = 1 if turn > 0 else 4
        return [jnp.where(edge, spun[(t + step) % 5], spun[t]) for t in range(5)]

    def block(r):
        at = ROW0 - 8 + 8 * r
        return at, slice(at, at + 8)

    def rise(r, flow_old, level_old):
        at, rows = block(r)
        row_ok = above_ok if r == 0 else below_ok if r == 9 else 1.0
        vals = [flow_old[1, t, rows, :] for t in range(5)]
        later = turned(vals, 2)
        for t in range(5):
            spread = flow_old[0, t, at + 1 : at + 9, :] - flow_old[0, t, at - 1 : at + 7, :]
            rate = c0 * row_ok * side_ok if t == 4 else c0 * row_ok
            level[t, rows, :] = level_old[t, rows, :] - rate * (spread + (later[t] - vals[t]))

    def push(r, flow_old, last=False):
        at, rows = block(r)
        vals = [level[t, rows, :] for t in range(5)]
        before = turned(vals, -2)
        res = []
        for t in range(5):
            if t < 4 or not last:
                slope = level[t, at + 1 : at + 9, :] - level[t, at - 1 : at + 7, :]
                flow[0, t, rows, :] = flow_old[0, t, rows, :] - flow_in[2, t, rows, :] * slope
            res.append(flow_old[1, t, rows, :] - flow_in[3, t, rows, :] * (vals[t] - before[t]))
        for t, val in enumerate(turned(res, 1) if last else res):
            flow[1, t, rows, :] = val

    def wave(flow_old, level_old):
        for r in range(10):
            rise(r, flow_old, level_old)
        for r in range(10):
            push(r, flow_old)

    wave(flow_in, level_in)

    def again(_, carry):
        wave(flow, level)
        return carry

    lax.fori_loop(0, STEPS - 2, again, 0)
    for r in range(10):
        rise(r, flow, level)
    copies = [dof_copy]

    def send(src, dst):
        copies.append(pltpu.make_async_copy(src, dst, sem.at[len(copies)]))
        copies[-1].start()

    for t in range(4):
        lanes = slice(t * LANES, (t + 1) * LANES)
        send(level.at[t, ROW0 : ROW0 + 64, :], height_out.at[:, lanes])
    for part in range(2):
        for r in range(4 * part, 4 * part + 4):
            push(r + 1, flow, last=True)
        rows = slice(32 * part, 32 * part + 32)
        for t in range(4):
            lanes = slice(t * LANES, (t + 1) * LANES)
            ring = slice(ROW0 + 32 * part, ROW0 + 32 * part + 32)
            send(flow.at[:, t, ring, :], momentum_out.at[:, rows, lanes])
    for c in copies:
        c.wait()


def shards(
    dof_values,
    density,
    lame_lambda,
    shear_modulus,
    jacobian,
    normals,
    face_scale,
    derivative,
    face_proj,
    lift_matrix,
    neighbour,
    send_face,
    cluster,
    sea_face,
    sea_cell,
    height,
    momentum,
    ocean_depth,
):
    n_dom, n_tile = lax.axis_size("dom"), lax.axis_size("tile")
    row = lambda x: x.reshape(1, x.shape[0])
    vmem = pl.BlockSpec(memory_space=pltpu.VMEM)
    far = pl.BlockSpec(memory_space=pltpu.HBM)
    table = (TILES + RTILES) * LANES
    args = (
        jnp.transpose(dof_values, (1, 0, 2)),
        row(density),
        row(lame_lambda),
        row(shear_modulus),
        jacobian,
        jnp.transpose(normals, (1, 0, 2)),
        face_scale,
        derivative,
        jnp.transpose(face_proj, (1, 0, 2)),
        jnp.transpose(lift_matrix, (2, 0, 1)),
        neighbour,
        send_face,
        row(cluster),
        jnp.transpose(sea_face),
        jnp.transpose(sea_cell),
        height,
        momentum,
        ocean_depth,
    )
    dof_new, flow, level = pl.pallas_call(
        functools.partial(kernel, n_dom, n_tile),
        out_shape=(
            pltpu.VMEM((Q, B, E), F32),
            pltpu.VMEM((4, 5, ROWS, LANES), F32),
            pltpu.VMEM((5, ROWS, LANES), F32),
        ),
        in_specs=[far] * 18,
        out_specs=(vmem,) * 3,
        scratch_shapes=[pltpu.VMEM(x.shape, x.dtype) for x in args[:15]]
        + [
            pltpu.VMEM((Q, BP, E), F32),
            pltpu.VMEM((2 * Q, 8, table), F32),
            pltpu.VMEM((3, 8, TILES * LANES), F32),
            pltpu.VMEM((Q, 8, E), F32),
            pltpu.VMEM((Q, 8, 5 * E), F32),
            pltpu.VMEM((144, LANES), F32),
            pltpu.VMEM((LANES, LANES), F32),
            pltpu.VMEM((16, LANES), jnp.int32),
            pltpu.VMEM((8, E), jnp.int32),
            pltpu.VMEM((10, 8, E), F32),
            pltpu.VMEM((11, 24, LANES), F32),
            pltpu.VMEM((11, 24, LANES), F32),
            pltpu.VMEM((9, 8, LANES), F32),
            pltpu.VMEM((LANES, LANES), F32),
            pltpu.VMEM((3, 8, LANES), F32),
            pltpu.VMEM((3, 5, ROWS, LANES), F32),
            pltpu.VMEM((5, ROWS, LANES), F32),
            pltpu.VMEM((2, 2, 8, LANES), F32),
            pltpu.VMEM((2, 2, 8, LANES), F32),
            pltpu.VMEM((4, 8, LANES), F32),
            pltpu.VMEM((4, 8, LANES), F32),
            pltpu.VMEM((2, 8, LANES), F32),
            pltpu.VMEM((2, 8, LANES), F32),
            pltpu.VMEM((4, 8, LANES), F32),
            pltpu.SemaphoreType.DMA((18,)),
            pltpu.SemaphoreType.DMA((4,)),
            pltpu.SemaphoreType.DMA((4,)),
        ],
        compiler_params=pltpu.CompilerParams(
            collective_id=0, has_side_effects=True, vmem_limit_bytes=VMEM
        ),
    )(*args)
    dof_out, height_out, momentum_out = pl.pallas_call(
        functools.partial(grid_kernel, n_dom, n_tile),
        out_shape=(
            jax.ShapeDtypeStruct((Q, B, E), F32),
            jax.ShapeDtypeStruct(height.shape, F32),
            jax.ShapeDtypeStruct(momentum.shape, F32),
        ),
        in_specs=[vmem] * 3,
        out_specs=(far,) * 3,
        scratch_shapes=[
            pltpu.VMEM((2, 5, ROWS, LANES), F32),
            pltpu.VMEM((5, ROWS, LANES), F32),
            pltpu.SemaphoreType.DMA((13,)),
        ],
        compiler_params=pltpu.CompilerParams(vmem_limit_bytes=16 << 20),
    )(dof_new, flow, level)
    return jnp.transpose(dof_out, (1, 0, 2)), height_out, momentum_out


def solution(mesh):
    both = ("dom", "tile")
    return jax.shard_map(
        shards,
        mesh=mesh,
        in_specs=(
            P(None, None, both),
            P(both),
            P(both),
            P(both),
            P(None, None, both),
            P(None, None, both),
            P(None, both),
            P(),
            P(),
            P(),
            P(None, both),
            P(both, None),
            P(both),
            P(both, None),
            P(both, None),
            P("dom", "tile"),
            P(None, "dom", "tile"),
            P("dom", "tile"),
        ),
        out_specs=(P(None, None, both), P("dom", "tile"), P(None, "dom", "tile")),
        check_vma=False,
    )
```

```python
import functools

import jax
import jax.numpy as jnp
from jax import lax
from jax.experimental import pallas as pl
from jax.experimental.pallas import tpu as pltpu
from jax.sharding import PartitionSpec as P

STEPS = 4
STRESS_PAIRS = ((0, 3, 5), (3, 1, 4), (5, 4, 2))
STRESS_ORDER = ((0, 0), (1, 1), (2, 2), (0, 1), (1, 2), (0, 2))
STEP_SIZE = 0.3
WAVE_RATE = 0.45
FLAT = pl.DeviceIdType.LOGICAL
F32 = jnp.float32
BF16 = jnp.bfloat16

B = 20
BP = 24
Q = 9
E = 512
CH = 256
GROUP = 2
DOFS = 1
LANES = 128
VMEM = 58 << 20
SIDE = 4
TILES = 16
RTILES = 3
SLOTS = 32
ROW0 = 16
ROWS = 96


def partner_offsets(tile_count, device_count):
    t = tile_count
    return [1, -1, 2, -2, t, -t, t + 1, -(t + 1), 2 * t, -2 * t, device_count // 2]


def split(x):
    high = x.astype(BF16).astype(F32)
    return high, x - high


def stacked(x):
    high, low = split(x)
    pad = jnp.zeros((8,) + x.shape[1:], F32)
    parts = [high, low, high]
    if (3 * x.shape[0]) % 16:
        parts.append(pad)
    return jnp.concatenate(parts, axis=0).astype(BF16)


def kernel(n_dom, n_tile, *refs):
    (
        dof_in,
        density_in,
        lame_in,
        shear_in,
        jac_in,
        nrm_in,
        fscale_in,
        deriv_in,
        fproj_in,
        lift_in,
        nbr_in,
        send_in,
        cluster_in,
        sea_face_in,
        sea_cell_in,
        height,
        momentum,
        depth,
    ) = refs[:18]
    out, flow_out, level_out = refs[18:21]
    (
        x_ref,
        density,
        lame,
        shear,
        jac,
        nrm,
        fscale,
        deriv,
        fproj,
        lift,
        nbr,
        send,
        cluster,
        sea_face,
        sea_cell,
    ) = refs[21:36]
    (
        base,
        tab,
        tab2,
        otail,
        acc,
        amat,
        lmat,
        sidx,
        nbr8,
        coef,
        msg,
        msg_in,
        tails,
        hand,
        hand_in,
        flow,
        level,
        flow_side,
        flow_side_in,
        flow_corner,
        flow_corner_in,
        level_side,
        level_side_in,
        level_corner_in,
        local_sem,
        send_sem,
        recv_sem,
    ) = refs[36:]
    devices = n_dom * n_tile
    dom, tile = lax.axis_index("dom"), lax.axis_index("tile")
    me = dom * n_tile + tile
    offsets = partner_offsets(n_tile, devices)
    greet = offsets + [n_tile - 1, -(n_tile - 1)]

    def device(offset):
        target = me + offset % devices
        return jnp.where(target >= devices, target - devices, target)

    near = {}

    def fetch(name, src, dst):
        near[name] = pltpu.make_async_copy(src, dst, local_sem.at[len(near)])
        near[name].start()

    fetch("deriv", deriv_in, deriv)
    fetch("fproj", fproj_in, fproj)
    for i in range(DOFS):
        cut = slice(i * E // DOFS, (i + 1) * E // DOFS)
        fetch(f"dof{i}", dof_in.at[:, :, cut], x_ref.at[:, :, cut])
        if i == 0:
            fetch("density", density_in, density)
            fetch("lame", lame_in, lame)
            fetch("shear", shear_in, shear)
            fetch("jac", jac_in, jac)
    barrier = pltpu.get_barrier_semaphore()
    for o in greet:
        pl.semaphore_signal(barrier, inc=1, device_id=device(o), device_id_type=FLAT)
    fetch("sea_face", sea_face_in, sea_face)
    fetch("send", send_in, send)
    fetch("nbr", nbr_in, nbr)
    fetch("nrm", nrm_in, nrm)
    fetch("fscale", fscale_in, fscale)
    fetch("cluster", cluster_in, cluster)
    fetch("lift", lift_in, lift)
    fetch("sea_cell", sea_cell_in, sea_cell)
    grid_rows = slice(ROW0, ROW0 + 64)
    first = len(near)
    for t in range(4):
        lanes = slice(t * LANES, (t + 1) * LANES)
        for k, (src, dst) in enumerate(
            (
                (momentum.at[:, :, lanes], flow.at[0:2, t, grid_rows, :]),
                (depth.at[:, lanes], flow.at[2, t, grid_rows, :]),
                (height.at[:, lanes], level.at[t, grid_rows, :]),
            )
        ):
            pltpu.make_async_copy(src, dst, local_sem.at[first + k]).start()

    def wait_all(ref, sem):
        pltpu.make_async_copy(ref, ref, sem).wait()

    lane = lax.broadcasted_iota(jnp.int32, (8, LANES), 1)
    sub = lax.broadcasted_iota(jnp.int32, (8, LANES), 0)

    for name in ("deriv", "fproj"):
        near[name].wait()
    amat[...] = jnp.zeros_like(amat)
    for d in range(3):
        amat[d * BP : d * BP + B, 0:B] = deriv[d]
    for f in range(4):
        for c in range(10):
            row = fproj[c, f : f + 1, :]
            if c < 8:
                amat[72 + f * 16 + c : 73 + f * 16 + c, 0:B] = row
            else:
                k = 32 + f * 2 + c - 8
                amat[104 + k : 105 + k, 0:B] = row
                for r in range(4):
                    k = 80 + f * 16 + r * 2 + c - 8
                    amat[k : k + 1, 0:B] = row
    a_high, a_low = split(amat[...])
    a_all = a_high + pltpu.roll(a_high, BP, 1) + pltpu.roll(a_low, 2 * BP, 1)
    a_all = a_all.astype(BF16)[:, 0:80]
    for name in ("density", "lame", "shear", "jac"):
        near[name].wait()

    def predictor(i, _):
        chunks = []
        for h in range(GROUP):
            off = pl.multiple_of((i * GROUP + h) * CH, CH)
            chunks.append(Chunk(off))
        for k in range(1, 4):
            for c in chunks:
                c.advance(k)
        for c in chunks:
            c.finish()
        return 0

    class Chunk:
        def __init__(self, off):
            self.off = off
            self.cut = cut = pl.ds(off, CH)
            self.rho = 1.0 / density[:, cut]
            self.lam = lame[:, cut]
            self.mu = shear[:, cut]
            self.jc = [[jac[d, x : x + 1, cut] for x in range(3)] for d in range(3)]
            pad = jnp.zeros((BP - B, CH), F32)
            self.term = [
                STEP_SIZE * jnp.concatenate([x_ref[v, :, cut], pad], axis=0) for v in range(Q)
            ]
            self.integral = self.term

        def combine(self, g, scale):
            jc = [[x * scale for x in row] for row in self.jc] if scale != 1.0 else self.jc
            lam, mu, rho = self.lam, self.mu, self.rho

            def phys(x, v):
                return (
                    jc[0][x] * g[0:BP, v * CH : (v + 1) * CH]
                    + jc[1][x] * g[BP : 2 * BP, v * CH : (v + 1) * CH]
                    + jc[2][x] * g[2 * BP : 3 * BP, v * CH : (v + 1) * CH]
                )

            vg = [[phys(j, 6 + i) for j in range(3)] for i in range(3)]
            div = lam * (vg[0][0] + vg[1][1] + vg[2][2])
            res = [div + (mu + mu) * vg[i][i] for i in range(3)]
            res += [mu * (vg[i][j] + vg[j][i]) for i, j in STRESS_ORDER[3:]]
            for i in range(3):
                s = STRESS_PAIRS[i]
                res.append(rho * (phys(0, s[0]) + phys(1, s[1]) + phys(2, s[2])))
            return res

        def advance(self, k):
            right = stacked(jnp.concatenate(self.term, axis=1))
            g = jnp.dot(a_all[0:72], right, preferred_element_type=F32)
            self.term = self.combine(g, STEP_SIZE / (k + 1))
            self.integral = [s + w for s, w in zip(self.integral, self.term)]

        def finish(self):
            off, cut = self.off, self.cut
            right = stacked(jnp.concatenate(self.integral, axis=1))
            g = jnp.dot(a_all, right, preferred_element_type=F32)
            volume = self.combine(g, 1.0)
            for v in range(Q):
                cols = slice(v * CH, (v + 1) * CH)
                base[v, :, cut] = volume[v]
                for f in range(4):
                    here = pl.ds(pl.multiple_of(f * E + off, LANES), CH)
                    tab[v, :, here] = g[72 + f * 16 : 80 + f * 16, cols]
                    tab[Q + v, :, here] = g[80 + f * 16 : 88 + f * 16, cols]
                otail[v, :, cut] = g[136:144, cols]
            pair = lax.broadcasted_iota(jnp.int32, (8, CH), 0) // 2
            for f in range(4):
                here = pl.ds(pl.multiple_of(f * E + off, LANES), CH)
                for j in range(3):
                    packed = None
                    for v in range(4 * j, min(4 * j + 4, Q)):
                        val = g[80 + f * 16 : 88 + f * 16, v * CH : (v + 1) * CH]
                        packed = val if packed is None else jnp.where(pair == v % 4, val, packed)
                    tab2[j, :, here] = packed

    per = E // (CH * GROUP)
    for i in range(DOFS):
        near[f"dof{i}"].wait()
        lax.fori_loop(i * per // DOFS, (i + 1) * per // DOFS, predictor, 0)
    near["sea_face"].wait()

    shift = lax.rem(devices - me, devices)
    ups = [jnp.broadcast_to(tab[8, 0:1, t * LANES : (t + 1) * LANES], (8, LANES)) for t in range(4)]
    slots = []
    for r in range(8):
        idx = sea_face[r * 8 : r * 8 + 8, :]
        at, which = idx & (LANES - 1), idx >> 7
        val = jnp.zeros((8, LANES), F32)
        for t in range(4):
            val = jnp.where(which == t, jnp.take_along_axis(ups[t], at, axis=1), val)
        slots.append(val)
    handed = pltpu.roll(jnp.concatenate(slots, axis=0), shift, 1)
    zeros64 = jnp.zeros((64, LANES), F32)
    hand[...] = jnp.transpose(jnp.concatenate([handed, zeros64], axis=0))

    def gather(sources, idx, tiles):
        at, which = idx & (LANES - 1), idx >> 7
        res = [jnp.zeros((8, LANES), F32)] * len(sources)
        for t in tiles:
            mask = which == t
            for k, source in enumerate(sources):
                val = jnp.take_along_axis(source[:, t * LANES : (t + 1) * LANES], at, axis=1)
                res[k] = jnp.where(mask, val, res[k])
        return res

    direct = range(TILES)
    pair = sub // 2
    def index(f, cut):
        if f < 4:
            return jnp.broadcast_to(nbr[f : f + 1, cut], (8, LANES))
        return nbr8[:, cut]

    def local_gather(et, _):
        off = pl.multiple_of(et * LANES, LANES)
        cut = pl.ds(off, LANES)
        for f in range(5):
            here = pl.ds(pl.multiple_of(f * E + off, LANES), LANES)
            got = gather([tab.at[v + Q * (f // 4)] for v in range(Q)], index(f, cut), direct)
            for v in range(Q):
                acc[v, :, here] = got[v] - (tab[v, :, here] if f < 4 else otail[v, :, cut])
        return 0

    near["nbr"].wait()
    for f in range(4):
        nbr8[2 * f : 2 * f + 2, :] = jnp.broadcast_to(nbr[f : f + 1, :], (2, E))
    ahead = jnp.where(dom == 0, 4, jnp.where(dom == 1, 3, 0))
    lax.fori_loop(0, ahead, local_gather, 0)

    pl.semaphore_wait(barrier, len(greet))

    def push(src, dst, offset, group):
        pltpu.make_async_remote_copy(
            src_ref=src,
            dst_ref=dst,
            send_sem=send_sem.at[group],
            recv_sem=recv_sem.at[group],
            device_id=device(offset),
            device_id_type=FLAT,
        ).start()

    hand_offsets = (1, n_tile, devices // 2)
    for k, o in enumerate(hand_offsets):
        row = o // 8 * 8
        push(hand.at[row : row + 8, :], hand_in.at[k], o, 0)

    wait_all(flow.at[0:2, 0:4, grid_rows, :], local_sem.at[first])
    wait_all(flow.at[2, 0:4, grid_rows, :], local_sem.at[first + 1])
    wait_all(level.at[0:4, grid_rows, :], local_sem.at[first + 2])
    top, low = slice(ROW0, ROW0 + 8), slice(ROW0 + 56, ROW0 + 64)
    above, below = slice(ROW0 - 8, ROW0), slice(ROW0 + 64, ROW0 + 72)
    group = lane // 8

    def column(ring, t):
        res = None
        for r in range(8):
            val = ring[t, ROW0 + 8 * r : ROW0 + 8 * r + 8, :]
            turn = (8 * r + (8 if t else 0)) % LANES
            val = pltpu.roll(val, turn, 1) if turn else val
            res = val if res is None else jnp.where(group == r, val, res)
        return res

    corners = ((0, top), (3, top), (0, low), (3, low))
    for side, t in ((0, 0), (1, 3)):
        fx, fy, dp = (column(flow.at[k], t) for k in range(3))
        flow_side[side, 0] = jnp.where(lane < 64, fx, pltpu.roll(fy, 64, 1))
        flow_side[side, 1] = dp
    for k, (t, rows) in enumerate(corners):
        turns = (0, 8, 16) if t == 0 else (0, LANES - 8, LANES - 16)
        fx, fy, dp = (
            pltpu.roll(flow[i, t, rows, :], turns[i], 1) if i else flow[i, t, rows, :]
            for i in range(3)
        )
        spot = group if t == 0 else 15 - group
        flow_corner[k] = jnp.where(spot == 0, fx, jnp.where(spot == 1, fy, dp))
    corner_offsets = (-n_tile - 1, -n_tile + 1, n_tile - 1, n_tile + 1)
    cols = slice(0, 4)
    push(flow.at[:, cols, top, :], flow.at[:, cols, below, :], -n_tile, 2)
    push(flow.at[:, cols, low, :], flow.at[:, cols, above, :], n_tile, 2)
    push(flow_side.at[0], flow_side_in.at[0], -1, 2)
    push(flow_side.at[1], flow_side_in.at[1], 1, 2)
    for k, o in enumerate(corner_offsets):
        push(flow_corner.at[k], flow_corner_in.at[k], o, 2)

    near["send"].wait()
    sidx[...] = jnp.zeros_like(sidx)
    sidx[0:11, 0:SLOTS] = send[...]
    block = lane // SLOTS
    places = [(v // 4, v % 4) for v in range(Q)] + [(2, 1 + j) for j in range(3)]
    rows = []
    for p in range(RTILES):
        idx = jnp.zeros((8, LANES), jnp.int32)
        for n in range(4 * p, min(4 * p + 4, len(offsets))):
            row = jnp.broadcast_to(sidx[n : n + 1, :], (8, LANES))
            idx = jnp.where(block == n % 4, pltpu.roll(row, SLOTS * (n % 4), 1), idx)
        rows.append(idx)
    for p in reversed(range(RTILES)):
        members = [n for n in range(4 * p, 4 * p + 4) if n < len(offsets)]
        sources = [tab.at[v] for v in range(Q)] + [tab2.at[j] for j in range(3)]
        got = gather(sources, rows[p], direct)
        for n in members:
            for r in range(3):
                packed = None
                for k, (pr, pb) in enumerate(places):
                    if pr != r:
                        continue
                    turn = (SLOTS * (pb - n % 4)) % LANES
                    val = pltpu.roll(got[k], turn, 1) if turn else got[k]
                    packed = val if packed is None else jnp.where(block == pb, val, packed)
                msg[n, r * 8 : r * 8 + 8, :] = packed
        for n in members:
            push(msg.at[n], msg_in.at[n], offsets[n], 1)

    for name in ("nrm", "fscale", "cluster", "sea_cell", "lift"):
        near[name].wait()
    lmat[...] = jnp.zeros_like(lmat)
    for f in range(4):
        for c in range(10):
            k = f * 8 + c if c < 8 else 32 + f * 2 + c - 8
            lmat[k : k + 1, 0:B] = lift[c, f : f + 1, :]
    l_high, l_low = split(jnp.transpose(lmat[...]))
    l_high, l_low = l_high[0:BP], l_low[0:BP]
    l_all = l_high + pltpu.roll(l_high, 40, 1) + pltpu.roll(l_low, 80, 1)
    l_all = l_all.astype(BF16)[:, 0:120]
    inv_den = 1.0 / density[...]
    speed = jnp.sqrt((lame[...] + 2.0 * shear[...]) * inv_den)
    half = 0.5 * fscale[...]
    scaled = [half * nrm[j] for j in range(3)]
    coefs = (
        scaled
        + [shear[...] * s for s in scaled]
        + [inv_den * s for s in scaled]
        + [half * speed]
    )
    for k, c in enumerate(coefs):
        for f in range(4):
            coef[k, 2 * f : 2 * f + 2, :] = jnp.broadcast_to(c[f : f + 1, :], (2, E))
    wait_all(hand_in, recv_sem.at[0])
    back = (0, devices - 1, devices - n_tile, devices // 2)
    cells = pltpu.roll(sea_cell[...], shift, 1)
    cells_t = jnp.transpose(
        jnp.concatenate([cells, jnp.zeros((64, LANES), jnp.int32)], axis=0).astype(F32)
    ).astype(jnp.int32)
    values = [hand[0:1, :]]
    for k, o in enumerate(hand_offsets):
        values.append(hand_in[k, o % 8 : o % 8 + 1, :])
    row_ids = lax.broadcasted_iota(jnp.int32, (64, LANES), 0)
    highs, lows = [], []
    for k in range(0, 4, 2):
        pair_v = values[k] + pltpu.roll(values[k + 1], 64, 1)
        pair_c = cells_t[back[k] : back[k] + 1, :] + pltpu.roll(
            cells_t[back[k + 1] : back[k + 1] + 1, :], 64, 1
        )
        v_high, v_low = split(pair_v)
        here = row_ids == jnp.broadcast_to(pair_c >> 9, (64, LANES))
        highs.append(jnp.where(here, v_high, 0.0))
        lows.append(jnp.where(here, v_low, 0.0))
    left = jnp.concatenate(
        [jnp.concatenate(highs, axis=1), jnp.concatenate(lows, axis=1)], axis=0
    ).astype(BF16)
    col_ids = lax.broadcasted_iota(jnp.int32, (64, E), 1)
    picks = []
    for k in range(4):
        chosen = jnp.broadcast_to(cells[:, back[k] : back[k] + 1] & (E - 1), (64, E))
        picks.append(jnp.where(col_ids == chosen, 1.0, 0.0).astype(BF16))
    lifted = jnp.dot(left, jnp.concatenate(picks, axis=0), preferred_element_type=F32)
    for t in range(4):
        lanes = slice(t * LANES, (t + 1) * LANES)
        level[t, ROW0 : ROW0 + 64, :] += lifted[0:64, lanes] + lifted[64:128, lanes]
    for side, t in ((0, 0), (1, 3)):
        level_side[side] = column(level, t)
    push(level.at[cols, top, :], level.at[cols, below, :], -n_tile, 3)
    push(level.at[cols, low, :], level.at[cols, above, :], n_tile, 3)
    push(level_side.at[0], level_side_in.at[0], -1, 3)
    push(level_side.at[1], level_side_in.at[1], 1, 3)
    for k, (o, (t, rows)) in enumerate(zip(corner_offsets, corners)):
        push(level.at[t, rows, :], level_corner_in.at[k], o, 3)

    lax.fori_loop(ahead, E // LANES, local_gather, 0)

    halo_bytes = flow.at[0, 0:4, 0:64, :]
    wait_all(halo_bytes, recv_sem.at[2])
    wait_all(halo_bytes, send_sem.at[2])
    above_ok, below_ok, right_ok, left_ok = inside(n_dom, n_tile)

    def close(ring, side, corner, res, scale):
        for t in range(4):
            res[t, ROW0 - 8 : ROW0, :] = ring[t, ROW0 - 8 : ROW0, :] * (above_ok * scale)
            res[t, ROW0 + 64 : ROW0 + 72, :] = ring[t, ROW0 + 64 : ROW0 + 72, :] * (below_ok * scale)
            val = ring[t, grid_rows, :]
            res[t, grid_rows, :] = val * scale if scale != 1.0 else val
        side_ok = jnp.where(lane < 64, right_ok, left_ok) * scale
        for r in range(8):
            right, left = side(r)
            res[4, ROW0 + 8 * r : ROW0 + 8 * r + 8, :] = jnp.where(lane < 64, right, left) * side_ok
        res[4, below, :] = jnp.where(lane < 64, corner(0), corner(1)) * (side_ok * below_ok)
        res[4, above, :] = jnp.where(lane < 64, corner(2), corner(3)) * (side_ok * above_ok)
        for t in range(5):
            res[t, 0:8, :] = jnp.zeros((8, LANES), F32)
            res[t, ROWS - 8 : ROWS, :] = jnp.zeros((8, LANES), F32)

    def turned(val, turn):
        return pltpu.roll(val, turn % LANES, 1) if turn % LANES else val

    for k in range(3):
        start = 64 if k == 1 else 0
        from_right, from_left = flow_side_in[0, k // 2], flow_side_in[1, k // 2]

        def side(r):
            at = start + 8 * r
            return turned(from_right, -at), turned(from_left, LANES - 8 - at)

        def corner(j):
            return turned(flow_corner_in[j], (-8 if j % 2 == 0 else 8) * k)

        close(flow.at[k], side, corner, flow_out.at[k], 0.5 * WAVE_RATE if k == 2 else 1.0)
    for k, to in ((1, 1), (2, 3)):
        for r in range(10):
            rows = slice(ROW0 - 8 + 8 * r, ROW0 + 8 * r)
            spun = [pltpu.roll(flow_out[k, t, rows, :], 1, 1) for t in range(5)]
            for t in range(5):
                flow_out[to, t, rows, :] = jnp.where(lane == 0, spun[(t + 4) % 5], spun[t])
    wait_all(msg_in, recv_sem.at[1])
    for p in range(RTILES):
        members = [n for n in range(4 * p, 4 * p + 4) if n < len(offsets)]
        cols = slice((TILES + p) * LANES, (TILES + p + 1) * LANES)
        unpacked = []
        for k, (pr, pb) in enumerate(places):
            res = None
            for n in members:
                val = msg_in[n, pr * 8 : pr * 8 + 8, :]
                turn = (SLOTS * (n % 4 - pb)) % LANES
                val = pltpu.roll(val, turn, 1) if turn else val
                res = val if res is None else jnp.where(block == n % 4, val, res)
            unpacked.append(res)
        for j in range(3):
            tails[p * 3 + j] = unpacked[Q + j]
        for v in range(Q):
            r = 2 * (v % 4)
            first = jnp.broadcast_to(tails[p * 3 + v // 4, r : r + 1, :], (8, LANES))
            second = jnp.broadcast_to(tails[p * 3 + v // 4, r + 1 : r + 2, :], (8, LANES))
            tab[v, :, cols] = unpacked[v]
            tab[Q + v, :, cols] = jnp.where(sub % 2 == 0, first, second)
    def finish_one(off):
        cut = pl.ds(off, LANES)
        lam = lame[:, cut]
        remote = range(TILES, TILES + RTILES)
        parts = [[] for _ in range(Q)]
        for f in range(5):
            here = pl.ds(pl.multiple_of(f * E + off, LANES), LANES)
            if f < 4:
                c = [coef[k, 2 * f : 2 * f + 1, cut] for k in range(10)]
            else:
                c = [coef[k, :, cut] for k in range(10)]
            got = gather([tab.at[v + Q * (f // 4)] for v in range(Q)], index(f, cut), remote)
            jump = [acc[v, :, here] + got[v] for v in range(Q)]
            u = jump[6:9]
            n, mun, rhn, ws = c[0:3], c[3:6], c[6:9], c[9]
            flux = lam * (u[0] * n[0] + u[1] * n[1] + u[2] * n[2])
            res = []
            for i in range(3):
                push_i = u[i] * mun[i]
                res.append(flux + (push_i + push_i) + ws * jump[i])
            for k, (i, j) in enumerate(STRESS_ORDER[3:]):
                res.append(u[i] * mun[j] + u[j] * mun[i] + ws * jump[3 + k])
            for i in range(3):
                s = STRESS_PAIRS[i]
                res.append(
                    jump[s[0]] * rhn[0] + jump[s[1]] * rhn[1] + jump[s[2]] * rhn[2] + ws * u[i]
                )
            for v in range(Q):
                parts[v].append(res[v])
        right = jnp.concatenate([jnp.concatenate(x, axis=0) for x in parts], axis=1)
        high, low = split(right)
        right = jnp.concatenate([high, low, high], axis=0).astype(BF16)
        lifts = jnp.dot(l_all, right, preferred_element_type=F32)
        chosen = jnp.broadcast_to(cluster[:, cut], (B, LANES)) == 1
        for v in range(Q):
            x = x_ref[v, :, cut]
            new = x + (base[v, 0:B, cut] + lifts[0:B, v * LANES : (v + 1) * LANES])
            out[v, :, cut] = jnp.where(chosen, new, x)

    def finish(i, _):
        for et in range(SIDE):
            finish_one(pl.multiple_of((i * SIDE + et) * LANES, LANES))
        return 0

    lax.fori_loop(0, E // LANES // SIDE, finish, 0)
    halo_bytes = level.at[0:2, 0:56, :]
    wait_all(halo_bytes, recv_sem.at[3])
    wait_all(halo_bytes, send_sem.at[3])
    wait_all(hand_in, send_sem.at[0])
    wait_all(msg, send_sem.at[1])
    from_right, from_left = level_side_in[0], level_side_in[1]

    def level_sides(r):
        return turned(from_right, -8 * r), turned(from_left, LANES - 8 - 8 * r)

    close(level, level_sides, lambda j: level_corner_in[j], level_out, 1.0)


def inside(n_dom, n_tile):
    dom, tile = lax.axis_index("dom"), lax.axis_index("tile")
    return (
        jnp.where(dom > 0, 1.0, 0.0),
        jnp.where(dom < n_dom - 1, 1.0, 0.0),
        jnp.where(tile < n_tile - 1, 1.0, 0.0),
        jnp.where(tile > 0, 1.0, 0.0),
    )


def grid_kernel(n_dom, n_tile, dof, flow_in, level_in, dof_out, height_out, momentum_out, *rest):
    flow, level, flow_res, sem = rest
    dof_copy = pltpu.make_async_copy(dof, dof_out, sem.at[0])
    dof_copy.start()
    above_ok, below_ok, right_ok, left_ok = inside(n_dom, n_tile)
    c0 = 0.5 * WAVE_RATE
    lane = lax.broadcasted_iota(jnp.int32, (8, LANES), 1)
    side_ok = jnp.where(lane < 64, right_ok, left_ok)
    for ring in (flow.at[0], level):
        for t in range(5):
            ring[t, 0:8, :] = jnp.zeros((8, LANES), F32)
            ring[t, ROWS - 8 : ROWS, :] = jnp.zeros((8, LANES), F32)

    def turned(vals, turn):
        spun = [pltpu.roll(x, -turn % LANES, 1) for x in vals]
        edge = lane >= LANES - turn if turn > 0 else lane < -turn
        step = 1 if turn > 0 else 4
        return [jnp.where(edge, spun[(t + step) % 5], spun[t]) for t in range(5)]

    def block(r):
        at = ROW0 - 8 + 8 * r
        return at, slice(at, at + 8)

    def rise(r, flow_old, level_old):
        at, rows = block(r)
        row_ok = above_ok if r == 0 else below_ok if r == 9 else 1.0
        vals = [flow_old[1, t, rows, :] for t in range(5)]
        later = turned(vals, 2)
        for t in range(5):
            spread = flow_old[0, t, at + 1 : at + 9, :] - flow_old[0, t, at - 1 : at + 7, :]
            rate = c0 * row_ok * side_ok if t == 4 else c0 * row_ok
            level[t, rows, :] = level_old[t, rows, :] - rate * (spread + (later[t] - vals[t]))

    def push(r, flow_old, last=False):
        at, rows = block(r)
        to, spot = (flow_res, slice(8 * r - 8, 8 * r)) if last else (flow, rows)
        vals = [level[t, rows, :] for t in range(5)]
        before = turned(vals, -2)
        res = []
        for t in range(5):
            if t < 4 or not last:
                slope = level[t, at + 1 : at + 9, :] - level[t, at - 1 : at + 7, :]
                to[0, t, spot, :] = flow_old[0, t, rows, :] - flow_in[2, t, rows, :] * slope
            res.append(flow_old[1, t, rows, :] - flow_in[3, t, rows, :] * (vals[t] - before[t]))
        res = turned(res, 1)[0:4] if last else res
        for t, val in enumerate(res):
            to[1, t, spot, :] = val

    def wave(flow_old, level_old):
        for r in range(10):
            rise(r, flow_old, level_old)
        for r in range(10):
            push(r, flow_old)

    wave(flow_in, level_in)

    def again(_, carry):
        wave(flow, level)
        return carry

    lax.fori_loop(0, STEPS - 2, again, 0)
    for r in range(10):
        rise(r, flow, level)
    for t in range(4):
        lanes = slice(t * LANES, (t + 1) * LANES)
        pltpu.make_async_copy(
            level.at[t, ROW0 : ROW0 + 64, :], height_out.at[:, lanes], sem.at[1]
        ).start()
    for part in range(2):
        for r in range(4 * part, 4 * part + 4):
            push(r + 1, flow, last=True)
        rows = slice(32 * part, 32 * part + 32)
        for t in range(4):
            lanes = slice(t * LANES, (t + 1) * LANES)
            pltpu.make_async_copy(
                flow_res.at[:, t, rows, :], momentum_out.at[:, rows, lanes], sem.at[2]
            ).start()
    dof_copy.wait()
    whole = level.at[0:4, ROW0 : ROW0 + 64, :]
    pltpu.make_async_copy(whole, whole, sem.at[1]).wait()
    pltpu.make_async_copy(flow_res, flow_res, sem.at[2]).wait()


def shards(
    dof_values,
    density,
    lame_lambda,
    shear_modulus,
    jacobian,
    normals,
    face_scale,
    derivative,
    face_proj,
    lift_matrix,
    neighbour,
    send_face,
    cluster,
    sea_face,
    sea_cell,
    height,
    momentum,
    ocean_depth,
):
    n_dom, n_tile = lax.axis_size("dom"), lax.axis_size("tile")
    row = lambda x: x.reshape(1, x.shape[0])
    vmem = pl.BlockSpec(memory_space=pltpu.VMEM)
    far = pl.BlockSpec(memory_space=pltpu.HBM)
    table = (TILES + RTILES) * LANES
    args = (
        jnp.transpose(dof_values, (1, 0, 2)),
        row(density),
        row(lame_lambda),
        row(shear_modulus),
        jacobian,
        jnp.transpose(normals, (1, 0, 2)),
        face_scale,
        derivative,
        jnp.transpose(face_proj, (1, 0, 2)),
        jnp.transpose(lift_matrix, (2, 0, 1)),
        neighbour,
        send_face,
        row(cluster),
        jnp.transpose(sea_face),
        jnp.transpose(sea_cell),
        height,
        momentum,
        ocean_depth,
    )
    dof_new, flow, level = pl.pallas_call(
        functools.partial(kernel, n_dom, n_tile),
        out_shape=(
            pltpu.VMEM((Q, B, E), F32),
            pltpu.VMEM((4, 5, ROWS, LANES), F32),
            pltpu.VMEM((5, ROWS, LANES), F32),
        ),
        in_specs=[far] * 18,
        out_specs=(vmem,) * 3,
        scratch_shapes=[pltpu.VMEM(x.shape, x.dtype) for x in args[:15]]
        + [
            pltpu.VMEM((Q, BP, E), F32),
            pltpu.VMEM((2 * Q, 8, table), F32),
            pltpu.VMEM((3, 8, TILES * LANES), F32),
            pltpu.VMEM((Q, 8, E), F32),
            pltpu.VMEM((Q, 8, 5 * E), F32),
            pltpu.VMEM((144, LANES), F32),
            pltpu.VMEM((LANES, LANES), F32),
            pltpu.VMEM((16, LANES), jnp.int32),
            pltpu.VMEM((8, E), jnp.int32),
            pltpu.VMEM((10, 8, E), F32),
            pltpu.VMEM((11, 24, LANES), F32),
            pltpu.VMEM((11, 24, LANES), F32),
            pltpu.VMEM((9, 8, LANES), F32),
            pltpu.VMEM((LANES, LANES), F32),
            pltpu.VMEM((3, 8, LANES), F32),
            pltpu.VMEM((3, 5, ROWS, LANES), F32),
            pltpu.VMEM((5, ROWS, LANES), F32),
            pltpu.VMEM((2, 2, 8, LANES), F32),
            pltpu.VMEM((2, 2, 8, LANES), F32),
            pltpu.VMEM((4, 8, LANES), F32),
            pltpu.VMEM((4, 8, LANES), F32),
            pltpu.VMEM((2, 8, LANES), F32),
            pltpu.VMEM((2, 8, LANES), F32),
            pltpu.VMEM((4, 8, LANES), F32),
            pltpu.SemaphoreType.DMA((18,)),
            pltpu.SemaphoreType.DMA((4,)),
            pltpu.SemaphoreType.DMA((4,)),
        ],
        compiler_params=pltpu.CompilerParams(
            collective_id=0, has_side_effects=True, vmem_limit_bytes=VMEM
        ),
    )(*args)
    dof_out, height_out, momentum_out = pl.pallas_call(
        functools.partial(grid_kernel, n_dom, n_tile),
        out_shape=(
            jax.ShapeDtypeStruct((Q, B, E), F32),
            jax.ShapeDtypeStruct(height.shape, F32),
            jax.ShapeDtypeStruct(momentum.shape, F32),
        ),
        in_specs=[vmem] * 3,
        out_specs=(far,) * 3,
        scratch_shapes=[
            pltpu.VMEM((2, 5, ROWS, LANES), F32),
            pltpu.VMEM((5, ROWS, LANES), F32),
            pltpu.VMEM((2, 4, 64, LANES), F32),
            pltpu.SemaphoreType.DMA((3,)),
        ],
        compiler_params=pltpu.CompilerParams(vmem_limit_bytes=16 << 20),
    )(dof_new, flow, level)
    return jnp.transpose(dof_out, (1, 0, 2)), height_out, momentum_out


def solution(mesh):
    both = ("dom", "tile")
    return jax.shard_map(
        shards,
        mesh=mesh,
        in_specs=(
            P(None, None, both),
            P(both),
            P(both),
            P(both),
            P(None, None, both),
            P(None, None, both),
            P(None, both),
            P(),
            P(),
            P(),
            P(None, both),
            P(both, None),
            P(both),
            P(both, None),
            P(both, None),
            P("dom", "tile"),
            P(None, "dom", "tile"),
            P("dom", "tile"),
        ),
        out_specs=(P(None, None, both), P("dom", "tile"), P(None, "dom", "tile")),
        check_vma=False,
    )
```

```python
import functools

import jax
import jax.numpy as jnp
from jax import lax
from jax.experimental import pallas as pl
from jax.experimental.pallas import tpu as pltpu
from jax.sharding import PartitionSpec as P

STEPS = 4
STRESS_PAIRS = ((0, 3, 5), (3, 1, 4), (5, 4, 2))
STRESS_ORDER = ((0, 0), (1, 1), (2, 2), (0, 1), (1, 2), (0, 2))
STEP_SIZE = 0.3
WAVE_RATE = 0.45
FLAT = pl.DeviceIdType.LOGICAL
F32 = jnp.float32
BF16 = jnp.bfloat16

B = 20
BP = 24
Q = 9
E = 512
CH = 256
GROUP = 2
DOFS = 1
LANES = 128
VMEM = 58 << 20
SIDE = 4
TILES = 16
RTILES = 3
SLOTS = 32
ROW0 = 16
ROWS = 96


def partner_offsets(tile_count, device_count):
    t = tile_count
    return [1, -1, 2, -2, t, -t, t + 1, -(t + 1), 2 * t, -2 * t, device_count // 2]


def split(x):
    high = x.astype(BF16).astype(F32)
    return high, x - high


def stacked(x):
    high, low = split(x)
    pad = jnp.zeros((8,) + x.shape[1:], F32)
    parts = [high, low, high]
    if (3 * x.shape[0]) % 16:
        parts.append(pad)
    return jnp.concatenate(parts, axis=0).astype(BF16)


def kernel(n_dom, n_tile, *refs):
    (
        dof_in,
        density_in,
        lame_in,
        shear_in,
        jac_in,
        nrm_in,
        fscale_in,
        deriv_in,
        fproj_in,
        lift_in,
        nbr_in,
        send_in,
        cluster_in,
        sea_face_in,
        sea_cell_in,
        height,
        momentum,
        depth,
    ) = refs[:18]
    out, flow_out, level_out = refs[18:21]
    (
        x_ref,
        density,
        lame,
        shear,
        jac,
        nrm,
        fscale,
        deriv,
        fproj,
        lift,
        nbr,
        send,
        cluster,
        sea_face,
        sea_cell,
    ) = refs[21:36]
    (
        base,
        tab,
        tab2,
        otail,
        acc,
        amat,
        lmat,
        sidx,
        nbr8,
        coef,
        msg,
        msg_in,
        tails,
        hand,
        hand_in,
        cell_rows,
        cell_cols,
        flow,
        level,
        flow_side,
        flow_side_in,
        flow_corner,
        flow_corner_in,
        level_side,
        level_side_in,
        level_corner_in,
        local_sem,
        send_sem,
        recv_sem,
    ) = refs[36:]
    devices = n_dom * n_tile
    dom, tile = lax.axis_index("dom"), lax.axis_index("tile")
    me = dom * n_tile + tile
    offsets = partner_offsets(n_tile, devices)
    greet = offsets + [n_tile - 1, -(n_tile - 1)]

    def device(offset):
        target = me + offset % devices
        return jnp.where(target >= devices, target - devices, target)

    near = {}

    def fetch(name, src, dst):
        near[name] = pltpu.make_async_copy(src, dst, local_sem.at[len(near)])
        near[name].start()

    fetch("deriv", deriv_in, deriv)
    fetch("fproj", fproj_in, fproj)
    for i in range(DOFS):
        cut = slice(i * E // DOFS, (i + 1) * E // DOFS)
        fetch(f"dof{i}", dof_in.at[:, :, cut], x_ref.at[:, :, cut])
        if i == 0:
            fetch("density", density_in, density)
            fetch("lame", lame_in, lame)
            fetch("shear", shear_in, shear)
            fetch("jac", jac_in, jac)
    barrier = pltpu.get_barrier_semaphore()
    for o in greet:
        pl.semaphore_signal(barrier, inc=1, device_id=device(o), device_id_type=FLAT)
    fetch("sea_face", sea_face_in, sea_face)
    fetch("send", send_in, send)
    fetch("nbr", nbr_in, nbr)
    fetch("nrm", nrm_in, nrm)
    fetch("fscale", fscale_in, fscale)
    fetch("cluster", cluster_in, cluster)
    fetch("lift", lift_in, lift)
    fetch("sea_cell", sea_cell_in, sea_cell)
    grid_rows = slice(ROW0, ROW0 + 64)
    first = len(near)
    for t in range(4):
        lanes = slice(t * LANES, (t + 1) * LANES)
        for k, (src, dst) in enumerate(
            (
                (momentum.at[:, :, lanes], flow.at[0:2, t, grid_rows, :]),
                (depth.at[:, lanes], flow.at[2, t, grid_rows, :]),
                (height.at[:, lanes], level.at[t, grid_rows, :]),
            )
        ):
            pltpu.make_async_copy(src, dst, local_sem.at[first + k]).start()

    def wait_all(ref, sem):
        pltpu.make_async_copy(ref, ref, sem).wait()

    lane = lax.broadcasted_iota(jnp.int32, (8, LANES), 1)
    sub = lax.broadcasted_iota(jnp.int32, (8, LANES), 0)

    amat[...] = jnp.zeros_like(amat)
    for name in ("deriv", "fproj"):
        near[name].wait()
    for d in range(3):
        amat[d * BP : d * BP + B, 0:B] = deriv[d]
    for f in range(4):
        for c in range(10):
            row = fproj[c, f : f + 1, :]
            if c < 8:
                amat[72 + f * 16 + c : 73 + f * 16 + c, 0:B] = row
            else:
                k = 32 + f * 2 + c - 8
                amat[104 + k : 105 + k, 0:B] = row
                for r in range(4):
                    k = 80 + f * 16 + r * 2 + c - 8
                    amat[k : k + 1, 0:B] = row
    a_high, a_low = split(amat[...])
    a_all = a_high + pltpu.roll(a_high, BP, 1) + pltpu.roll(a_low, 2 * BP, 1)
    a_all = a_all.astype(BF16)[:, 0:80]
    for name in ("density", "lame", "shear", "jac"):
        near[name].wait()

    def predictor(i, _):
        chunks = []
        for h in range(GROUP):
            off = pl.multiple_of((i * GROUP + h) * CH, CH)
            chunks.append(Chunk(off))
        for k in range(1, 4):
            for c in chunks:
                c.advance(k)
        for c in chunks:
            c.finish()
        return 0

    class Chunk:
        def __init__(self, off):
            self.off = off
            self.cut = cut = pl.ds(off, CH)
            self.rho = 1.0 / density[:, cut]
            self.lam = lame[:, cut]
            self.mu = shear[:, cut]
            self.jc = [[jac[d, x : x + 1, cut] for x in range(3)] for d in range(3)]
            pad = jnp.zeros((BP - B, CH), F32)
            self.term = [
                STEP_SIZE * jnp.concatenate([x_ref[v, :, cut], pad], axis=0) for v in range(Q)
            ]
            self.integral = self.term

        def combine(self, g, scale):
            jc = [[x * scale for x in row] for row in self.jc] if scale != 1.0 else self.jc
            lam, mu, rho = self.lam, self.mu, self.rho

            def phys(x, v):
                return (
                    jc[0][x] * g[0:BP, v * CH : (v + 1) * CH]
                    + jc[1][x] * g[BP : 2 * BP, v * CH : (v + 1) * CH]
                    + jc[2][x] * g[2 * BP : 3 * BP, v * CH : (v + 1) * CH]
                )

            vg = [[phys(j, 6 + i) for j in range(3)] for i in range(3)]
            div = lam * (vg[0][0] + vg[1][1] + vg[2][2])
            res = [div + (mu + mu) * vg[i][i] for i in range(3)]
            res += [mu * (vg[i][j] + vg[j][i]) for i, j in STRESS_ORDER[3:]]
            for i in range(3):
                s = STRESS_PAIRS[i]
                res.append(rho * (phys(0, s[0]) + phys(1, s[1]) + phys(2, s[2])))
            return res

        def advance(self, k):
            right = stacked(jnp.concatenate(self.term, axis=1))
            g = jnp.dot(a_all[0:72], right, preferred_element_type=F32)
            self.term = self.combine(g, STEP_SIZE / (k + 1))
            self.integral = [s + w for s, w in zip(self.integral, self.term)]

        def finish(self):
            off, cut = self.off, self.cut
            right = stacked(jnp.concatenate(self.integral, axis=1))
            g = jnp.dot(a_all, right, preferred_element_type=F32)
            volume = self.combine(g, 1.0)
            for v in range(Q):
                cols = slice(v * CH, (v + 1) * CH)
                base[v, :, cut] = volume[v]
                for f in range(4):
                    here = pl.ds(pl.multiple_of(f * E + off, LANES), CH)
                    tab[v, :, here] = g[72 + f * 16 : 80 + f * 16, cols]
                    tab[Q + v, :, here] = g[80 + f * 16 : 88 + f * 16, cols]
                otail[v, :, cut] = g[136:144, cols]
            pair = lax.broadcasted_iota(jnp.int32, (8, CH), 0) // 2
            for f in range(4):
                here = pl.ds(pl.multiple_of(f * E + off, LANES), CH)
                for j in range(3):
                    packed = None
                    for v in range(4 * j, min(4 * j + 4, Q)):
                        val = g[80 + f * 16 : 88 + f * 16, v * CH : (v + 1) * CH]
                        packed = val if packed is None else jnp.where(pair == v % 4, val, packed)
                    tab2[j, :, here] = packed

    per = E // (CH * GROUP)
    for i in range(DOFS):
        near[f"dof{i}"].wait()
        lax.fori_loop(i * per // DOFS, (i + 1) * per // DOFS, predictor, 0)
    near["sea_face"].wait()

    shift = lax.rem(devices - me, devices)
    ups = [jnp.broadcast_to(tab[8, 0:1, t * LANES : (t + 1) * LANES], (8, LANES)) for t in range(4)]
    slots = []
    for r in range(8):
        idx = sea_face[r * 8 : r * 8 + 8, :]
        at, which = idx & (LANES - 1), idx >> 7
        val = jnp.zeros((8, LANES), F32)
        for t in range(4):
            val = jnp.where(which == t, jnp.take_along_axis(ups[t], at, axis=1), val)
        slots.append(val)
    handed = pltpu.roll(jnp.concatenate(slots, axis=0), shift, 1)
    zeros64 = jnp.zeros((64, LANES), F32)
    hand[...] = jnp.transpose(jnp.concatenate([handed, zeros64], axis=0))

    def gather(sources, idx, tiles):
        at, which = idx & (LANES - 1), idx >> 7
        res = [jnp.zeros((8, LANES), F32)] * len(sources)
        for t in tiles:
            mask = which == t
            for k, source in enumerate(sources):
                val = jnp.take_along_axis(source[:, t * LANES : (t + 1) * LANES], at, axis=1)
                res[k] = jnp.where(mask, val, res[k])
        return res

    direct = range(TILES)
    pair = sub // 2
    def index(f, cut):
        if f < 4:
            return jnp.broadcast_to(nbr[f : f + 1, cut], (8, LANES))
        return nbr8[:, cut]

    def local_gather(et, _):
        off = pl.multiple_of(et * LANES, LANES)
        cut = pl.ds(off, LANES)
        for f in range(5):
            here = pl.ds(pl.multiple_of(f * E + off, LANES), LANES)
            got = gather([tab.at[v + Q * (f // 4)] for v in range(Q)], index(f, cut), direct)
            for v in range(Q):
                acc[v, :, here] = got[v] - (tab[v, :, here] if f < 4 else otail[v, :, cut])
        return 0

    near["nbr"].wait()
    for f in range(4):
        nbr8[2 * f : 2 * f + 2, :] = jnp.broadcast_to(nbr[f : f + 1, :], (2, E))
    ahead = jnp.where(dom == 0, 4, jnp.where(dom == 1, 3, 0))
    lax.fori_loop(0, ahead, local_gather, 0)

    pl.semaphore_wait(barrier, len(greet))

    def push(src, dst, offset, group):
        pltpu.make_async_remote_copy(
            src_ref=src,
            dst_ref=dst,
            send_sem=send_sem.at[group],
            recv_sem=recv_sem.at[group],
            device_id=device(offset),
            device_id_type=FLAT,
        ).start()

    hand_offsets = (1, n_tile, devices // 2)
    for k, o in enumerate(hand_offsets):
        row = o // 8 * 8
        push(hand.at[row : row + 8, :], hand_in.at[k], o, 0)

    wait_all(flow.at[0:2, 0:4, grid_rows, :], local_sem.at[first])
    wait_all(flow.at[2, 0:4, grid_rows, :], local_sem.at[first + 1])
    wait_all(level.at[0:4, grid_rows, :], local_sem.at[first + 2])
    top, low = slice(ROW0, ROW0 + 8), slice(ROW0 + 56, ROW0 + 64)
    above, below = slice(ROW0 - 8, ROW0), slice(ROW0 + 64, ROW0 + 72)
    group = lane // 8

    def column(ring, t):
        res = None
        for r in range(8):
            val = ring[t, ROW0 + 8 * r : ROW0 + 8 * r + 8, :]
            turn = (8 * r + (8 if t else 0)) % LANES
            val = pltpu.roll(val, turn, 1) if turn else val
            res = val if res is None else jnp.where(group == r, val, res)
        return res

    corners = ((0, top), (3, top), (0, low), (3, low))
    for side, t in ((0, 0), (1, 3)):
        fx, fy, dp = (column(flow.at[k], t) for k in range(3))
        flow_side[side, 0] = jnp.where(lane < 64, fx, pltpu.roll(fy, 64, 1))
        flow_side[side, 1] = dp
    for k, (t, rows) in enumerate(corners):
        turns = (0, 8, 16) if t == 0 else (0, LANES - 8, LANES - 16)
        fx, fy, dp = (
            pltpu.roll(flow[i, t, rows, :], turns[i], 1) if i else flow[i, t, rows, :]
            for i in range(3)
        )
        spot = group if t == 0 else 15 - group
        flow_corner[k] = jnp.where(spot == 0, fx, jnp.where(spot == 1, fy, dp))
    corner_offsets = (-n_tile - 1, -n_tile + 1, n_tile - 1, n_tile + 1)
    cols = slice(0, 4)
    push(flow.at[:, cols, top, :], flow.at[:, cols, below, :], -n_tile, 2)
    push(flow.at[:, cols, low, :], flow.at[:, cols, above, :], n_tile, 2)
    push(flow_side.at[0], flow_side_in.at[0], -1, 2)
    push(flow_side.at[1], flow_side_in.at[1], 1, 2)
    for k, o in enumerate(corner_offsets):
        push(flow_corner.at[k], flow_corner_in.at[k], o, 2)

    near["send"].wait()
    sidx[...] = jnp.zeros_like(sidx)
    sidx[0:11, 0:SLOTS] = send[...]
    block = lane // SLOTS
    places = [(v // 4, v % 4) for v in range(Q)] + [(2, 1 + j) for j in range(3)]
    rows = []
    for p in range(RTILES):
        idx = jnp.zeros((8, LANES), jnp.int32)
        for n in range(4 * p, min(4 * p + 4, len(offsets))):
            row = jnp.broadcast_to(sidx[n : n + 1, :], (8, LANES))
            idx = jnp.where(block == n % 4, pltpu.roll(row, SLOTS * (n % 4), 1), idx)
        rows.append(idx)
    for p in reversed(range(RTILES)):
        members = [n for n in range(4 * p, 4 * p + 4) if n < len(offsets)]
        sources = [tab.at[v] for v in range(Q)] + [tab2.at[j] for j in range(3)]
        got = gather(sources, rows[p], direct)
        for n in members:
            for r in range(3):
                packed = None
                for k, (pr, pb) in enumerate(places):
                    if pr != r:
                        continue
                    turn = (SLOTS * (pb - n % 4)) % LANES
                    val = pltpu.roll(got[k], turn, 1) if turn else got[k]
                    packed = val if packed is None else jnp.where(block == pb, val, packed)
                msg[n, r * 8 : r * 8 + 8, :] = packed
        for n in members:
            push(msg.at[n], msg_in.at[n], offsets[n], 1)

    for name in ("nrm", "fscale", "cluster", "sea_cell", "lift"):
        near[name].wait()
    lmat[...] = jnp.zeros_like(lmat)
    for f in range(4):
        for c in range(10):
            k = f * 8 + c if c < 8 else 32 + f * 2 + c - 8
            lmat[k : k + 1, 0:B] = lift[c, f : f + 1, :]
    l_high, l_low = split(jnp.transpose(lmat[...]))
    l_high, l_low = l_high[0:BP], l_low[0:BP]
    l_all = l_high + pltpu.roll(l_high, 40, 1) + pltpu.roll(l_low, 80, 1)
    l_all = l_all.astype(BF16)[:, 0:120]
    inv_den = 1.0 / density[...]
    speed = jnp.sqrt((lame[...] + 2.0 * shear[...]) * inv_den)
    half = 0.5 * fscale[...]
    scaled = [half * nrm[j] for j in range(3)]
    coefs = (
        scaled
        + [shear[...] * s for s in scaled]
        + [inv_den * s for s in scaled]
        + [half * speed]
    )
    for k, c in enumerate(coefs):
        for f in range(4):
            coef[k, 2 * f : 2 * f + 2, :] = jnp.broadcast_to(c[f : f + 1, :], (2, E))
    back = (0, devices - 1, devices - n_tile, devices // 2)
    cells = pltpu.roll(sea_cell[...], shift, 1)
    cells_t = jnp.transpose(
        jnp.concatenate([cells, jnp.zeros((64, LANES), jnp.int32)], axis=0).astype(F32)
    ).astype(jnp.int32)
    row_ids = lax.broadcasted_iota(jnp.int32, (64, LANES), 0)
    col_ids = lax.broadcasted_iota(jnp.int32, (64, E), 1)
    for k in range(0, 4, 2):
        pair_c = cells_t[back[k] : back[k] + 1, :] + pltpu.roll(
            cells_t[back[k + 1] : back[k + 1] + 1, :], 64, 1
        )
        here = row_ids == jnp.broadcast_to(pair_c >> 9, (64, LANES))
        cell_rows[k // 2] = jnp.where(here, 1.0, 0.0)
    for k in range(4):
        chosen = jnp.broadcast_to(cells[:, back[k] : back[k] + 1] & (E - 1), (64, E))
        cell_cols[64 * k : 64 * k + 64, :] = jnp.where(col_ids == chosen, 1.0, 0.0).astype(BF16)
    wait_all(hand_in, recv_sem.at[0])
    values = [hand[0:1, :]]
    for k, o in enumerate(hand_offsets):
        values.append(hand_in[k, o % 8 : o % 8 + 1, :])
    highs, lows = [], []
    for k in range(0, 4, 2):
        v_high, v_low = split(values[k] + pltpu.roll(values[k + 1], 64, 1))
        highs.append(cell_rows[k // 2] * v_high)
        lows.append(cell_rows[k // 2] * v_low)
    left = jnp.concatenate(
        [jnp.concatenate(highs, axis=1), jnp.concatenate(lows, axis=1)], axis=0
    ).astype(BF16)
    lifted = jnp.dot(left, cell_cols[...], preferred_element_type=F32)
    for t in range(4):
        lanes = slice(t * LANES, (t + 1) * LANES)
        level[t, ROW0 : ROW0 + 64, :] += lifted[0:64, lanes] + lifted[64:128, lanes]
    for side, t in ((0, 0), (1, 3)):
        level_side[side] = column(level, t)
    push(level.at[cols, top, :], level.at[cols, below, :], -n_tile, 3)
    push(level.at[cols, low, :], level.at[cols, above, :], n_tile, 3)
    push(level_side.at[0], level_side_in.at[0], -1, 3)
    push(level_side.at[1], level_side_in.at[1], 1, 3)
    for k, (o, (t, rows)) in enumerate(zip(corner_offsets, corners)):
        push(level.at[t, rows, :], level_corner_in.at[k], o, 3)

    lax.fori_loop(ahead, E // LANES, local_gather, 0)

    halo_bytes = flow.at[0, 0:4, 0:64, :]
    wait_all(halo_bytes, recv_sem.at[2])
    wait_all(halo_bytes, send_sem.at[2])
    above_ok, below_ok, right_ok, left_ok = inside(n_dom, n_tile)

    def close(ring, side, corner, res, scale):
        for t in range(4):
            res[t, ROW0 - 8 : ROW0, :] = ring[t, ROW0 - 8 : ROW0, :] * (above_ok * scale)
            res[t, ROW0 + 64 : ROW0 + 72, :] = ring[t, ROW0 + 64 : ROW0 + 72, :] * (below_ok * scale)
            val = ring[t, grid_rows, :]
            res[t, grid_rows, :] = val * scale if scale != 1.0 else val
        side_ok = jnp.where(lane < 64, right_ok, left_ok) * scale
        for r in range(8):
            right, left = side(r)
            res[4, ROW0 + 8 * r : ROW0 + 8 * r + 8, :] = jnp.where(lane < 64, right, left) * side_ok
        res[4, below, :] = jnp.where(lane < 64, corner(0), corner(1)) * (side_ok * below_ok)
        res[4, above, :] = jnp.where(lane < 64, corner(2), corner(3)) * (side_ok * above_ok)
        for t in range(5):
            res[t, 0:8, :] = jnp.zeros((8, LANES), F32)
            res[t, ROWS - 8 : ROWS, :] = jnp.zeros((8, LANES), F32)

    def turned(val, turn):
        return pltpu.roll(val, turn % LANES, 1) if turn % LANES else val

    for k in range(3):
        start = 64 if k == 1 else 0
        from_right, from_left = flow_side_in[0, k // 2], flow_side_in[1, k // 2]

        def side(r):
            at = start + 8 * r
            return turned(from_right, -at), turned(from_left, LANES - 8 - at)

        def corner(j):
            return turned(flow_corner_in[j], (-8 if j % 2 == 0 else 8) * k)

        close(flow.at[k], side, corner, flow_out.at[k], 0.5 * WAVE_RATE if k == 2 else 1.0)
    for k, to in ((1, 1), (2, 3)):
        for r in range(10):
            rows = slice(ROW0 - 8 + 8 * r, ROW0 + 8 * r)
            spun = [pltpu.roll(flow_out[k, t, rows, :], 1, 1) for t in range(5)]
            for t in range(5):
                flow_out[to, t, rows, :] = jnp.where(lane == 0, spun[(t + 4) % 5], spun[t])
    wait_all(msg_in, recv_sem.at[1])
    for p in range(RTILES):
        members = [n for n in range(4 * p, 4 * p + 4) if n < len(offsets)]
        cols = slice((TILES + p) * LANES, (TILES + p + 1) * LANES)
        unpacked = []
        for k, (pr, pb) in enumerate(places):
            res = None
            for n in members:
                val = msg_in[n, pr * 8 : pr * 8 + 8, :]
                turn = (SLOTS * (n % 4 - pb)) % LANES
                val = pltpu.roll(val, turn, 1) if turn else val
                res = val if res is None else jnp.where(block == n % 4, val, res)
            unpacked.append(res)
        for j in range(3):
            tails[p * 3 + j] = unpacked[Q + j]
        for v in range(Q):
            r = 2 * (v % 4)
            first = jnp.broadcast_to(tails[p * 3 + v // 4, r : r + 1, :], (8, LANES))
            second = jnp.broadcast_to(tails[p * 3 + v // 4, r + 1 : r + 2, :], (8, LANES))
            tab[v, :, cols] = unpacked[v]
            tab[Q + v, :, cols] = jnp.where(sub % 2 == 0, first, second)
    def finish_one(off):
        cut = pl.ds(off, LANES)
        lam = lame[:, cut]
        remote = range(TILES, TILES + RTILES)
        parts = [[] for _ in range(Q)]
        for f in range(5):
            here = pl.ds(pl.multiple_of(f * E + off, LANES), LANES)
            if f < 4:
                c = [coef[k, 2 * f : 2 * f + 1, cut] for k in range(10)]
            else:
                c = [coef[k, :, cut] for k in range(10)]
            got = gather([tab.at[v + Q * (f // 4)] for v in range(Q)], index(f, cut), remote)
            jump = [acc[v, :, here] + got[v] for v in range(Q)]
            u = jump[6:9]
            n, mun, rhn, ws = c[0:3], c[3:6], c[6:9], c[9]
            flux = lam * (u[0] * n[0] + u[1] * n[1] + u[2] * n[2])
            res = []
            for i in range(3):
                push_i = u[i] * mun[i]
                res.append(flux + (push_i + push_i) + ws * jump[i])
            for k, (i, j) in enumerate(STRESS_ORDER[3:]):
                res.append(u[i] * mun[j] + u[j] * mun[i] + ws * jump[3 + k])
            for i in range(3):
                s = STRESS_PAIRS[i]
                res.append(
                    jump[s[0]] * rhn[0] + jump[s[1]] * rhn[1] + jump[s[2]] * rhn[2] + ws * u[i]
                )
            for v in range(Q):
                parts[v].append(res[v])
        right = jnp.concatenate([jnp.concatenate(x, axis=0) for x in parts], axis=1)
        high, low = split(right)
        right = jnp.concatenate([high, low, high], axis=0).astype(BF16)
        lifts = jnp.dot(l_all, right, preferred_element_type=F32)
        chosen = jnp.broadcast_to(cluster[:, cut], (B, LANES)) == 1
        for v in range(Q):
            x = x_ref[v, :, cut]
            new = x + (base[v, 0:B, cut] + lifts[0:B, v * LANES : (v + 1) * LANES])
            out[v, :, cut] = jnp.where(chosen, new, x)

    def finish(i, _):
        for et in range(SIDE):
            finish_one(pl.multiple_of((i * SIDE + et) * LANES, LANES))
        return 0

    lax.fori_loop(0, E // LANES // SIDE, finish, 0)
    halo_bytes = level.at[0:2, 0:56, :]
    wait_all(halo_bytes, recv_sem.at[3])
    wait_all(halo_bytes, send_sem.at[3])
    wait_all(hand_in, send_sem.at[0])
    wait_all(msg, send_sem.at[1])
    from_right, from_left = level_side_in[0], level_side_in[1]

    def level_sides(r):
        return turned(from_right, -8 * r), turned(from_left, LANES - 8 - 8 * r)

    close(level, level_sides, lambda j: level_corner_in[j], level_out, 1.0)


def inside(n_dom, n_tile):
    dom, tile = lax.axis_index("dom"), lax.axis_index("tile")
    return (
        jnp.where(dom > 0, 1.0, 0.0),
        jnp.where(dom < n_dom - 1, 1.0, 0.0),
        jnp.where(tile < n_tile - 1, 1.0, 0.0),
        jnp.where(tile > 0, 1.0, 0.0),
    )


def grid_kernel(n_dom, n_tile, dof, flow_in, level_in, dof_out, height_out, momentum_out, *rest):
    flow, level, flow_res, sem = rest
    dof_copy = pltpu.make_async_copy(dof, dof_out, sem.at[0])
    dof_copy.start()
    above_ok, below_ok, right_ok, left_ok = inside(n_dom, n_tile)
    c0 = 0.5 * WAVE_RATE
    lane = lax.broadcasted_iota(jnp.int32, (8, LANES), 1)
    side_ok = jnp.where(lane < 64, right_ok, left_ok)
    for ring in (flow.at[0], level):
        for t in range(5):
            ring[t, 0:8, :] = jnp.zeros((8, LANES), F32)
            ring[t, ROWS - 8 : ROWS, :] = jnp.zeros((8, LANES), F32)

    def turned(vals, turn):
        spun = [pltpu.roll(x, -turn % LANES, 1) for x in vals]
        edge = lane >= LANES - turn if turn > 0 else lane < -turn
        step = 1 if turn > 0 else 4
        return [jnp.where(edge, spun[(t + step) % 5], spun[t]) for t in range(5)]

    def block(r):
        at = ROW0 - 8 + 8 * r
        return at, slice(at, at + 8)

    def rise(r, flow_old, level_old):
        at, rows = block(r)
        row_ok = above_ok if r == 0 else below_ok if r == 9 else 1.0
        vals = [flow_old[1, t, rows, :] for t in range(5)]
        later = turned(vals, 2)
        for t in range(5):
            spread = flow_old[0, t, at + 1 : at + 9, :] - flow_old[0, t, at - 1 : at + 7, :]
            rate = c0 * row_ok * side_ok if t == 4 else c0 * row_ok
            level[t, rows, :] = level_old[t, rows, :] - rate * (spread + (later[t] - vals[t]))

    def push(r, flow_old, last=False):
        at, rows = block(r)
        to, spot = (flow_res, slice(8 * r - 8, 8 * r)) if last else (flow, rows)
        vals = [level[t, rows, :] for t in range(5)]
        before = turned(vals, -2)
        res = []
        for t in range(5):
            if t < 4 or not last:
                slope = level[t, at + 1 : at + 9, :] - level[t, at - 1 : at + 7, :]
                to[0, t, spot, :] = flow_old[0, t, rows, :] - flow_in[2, t, rows, :] * slope
            res.append(flow_old[1, t, rows, :] - flow_in[3, t, rows, :] * (vals[t] - before[t]))
        res = turned(res, 1)[0:4] if last else res
        for t, val in enumerate(res):
            to[1, t, spot, :] = val

    def wave(flow_old, level_old):
        for r in range(10):
            rise(r, flow_old, level_old)
        for r in range(10):
            push(r, flow_old)

    wave(flow_in, level_in)

    def again(_, carry):
        wave(flow, level)
        return carry

    lax.fori_loop(0, STEPS - 2, again, 0)
    for r in range(10):
        rise(r, flow, level)
    for t in range(4):
        lanes = slice(t * LANES, (t + 1) * LANES)
        pltpu.make_async_copy(
            level.at[t, ROW0 : ROW0 + 64, :], height_out.at[:, lanes], sem.at[1]
        ).start()
    for part in range(2):
        for r in range(4 * part, 4 * part + 4):
            push(r + 1, flow, last=True)
        rows = slice(32 * part, 32 * part + 32)
        for t in range(4):
            lanes = slice(t * LANES, (t + 1) * LANES)
            pltpu.make_async_copy(
                flow_res.at[:, t, rows, :], momentum_out.at[:, rows, lanes], sem.at[2]
            ).start()
    dof_copy.wait()
    whole = level.at[0:4, ROW0 : ROW0 + 64, :]
    pltpu.make_async_copy(whole, whole, sem.at[1]).wait()
    pltpu.make_async_copy(flow_res, flow_res, sem.at[2]).wait()


def shards(
    dof_values,
    density,
    lame_lambda,
    shear_modulus,
    jacobian,
    normals,
    face_scale,
    derivative,
    face_proj,
    lift_matrix,
    neighbour,
    send_face,
    cluster,
    sea_face,
    sea_cell,
    height,
    momentum,
    ocean_depth,
):
    n_dom, n_tile = lax.axis_size("dom"), lax.axis_size("tile")
    row = lambda x: x.reshape(1, x.shape[0])
    vmem = pl.BlockSpec(memory_space=pltpu.VMEM)
    far = pl.BlockSpec(memory_space=pltpu.HBM)
    table = (TILES + RTILES) * LANES
    args = (
        jnp.transpose(dof_values, (1, 0, 2)),
        row(density),
        row(lame_lambda),
        row(shear_modulus),
        jacobian,
        jnp.transpose(normals, (1, 0, 2)),
        face_scale,
        derivative,
        jnp.transpose(face_proj, (1, 0, 2)),
        jnp.transpose(lift_matrix, (2, 0, 1)),
        neighbour,
        send_face,
        row(cluster),
        jnp.transpose(sea_face),
        jnp.transpose(sea_cell),
        height,
        momentum,
        ocean_depth,
    )
    dof_new, flow, level = pl.pallas_call(
        functools.partial(kernel, n_dom, n_tile),
        out_shape=(
            pltpu.VMEM((Q, B, E), F32),
            pltpu.VMEM((4, 5, ROWS, LANES), F32),
            pltpu.VMEM((5, ROWS, LANES), F32),
        ),
        in_specs=[far] * 18,
        out_specs=(vmem,) * 3,
        scratch_shapes=[pltpu.VMEM(x.shape, x.dtype) for x in args[:15]]
        + [
            pltpu.VMEM((Q, BP, E), F32),
            pltpu.VMEM((2 * Q, 8, table), F32),
            pltpu.VMEM((3, 8, TILES * LANES), F32),
            pltpu.VMEM((Q, 8, E), F32),
            pltpu.VMEM((Q, 8, 5 * E), F32),
            pltpu.VMEM((144, LANES), F32),
            pltpu.VMEM((LANES, LANES), F32),
            pltpu.VMEM((16, LANES), jnp.int32),
            pltpu.VMEM((8, E), jnp.int32),
            pltpu.VMEM((10, 8, E), F32),
            pltpu.VMEM((11, 24, LANES), F32),
            pltpu.VMEM((11, 24, LANES), F32),
            pltpu.VMEM((9, 8, LANES), F32),
            pltpu.VMEM((LANES, LANES), F32),
            pltpu.VMEM((3, 8, LANES), F32),
            pltpu.VMEM((2, 64, LANES), F32),
            pltpu.VMEM((256, E), BF16),
            pltpu.VMEM((3, 5, ROWS, LANES), F32),
            pltpu.VMEM((5, ROWS, LANES), F32),
            pltpu.VMEM((2, 2, 8, LANES), F32),
            pltpu.VMEM((2, 2, 8, LANES), F32),
            pltpu.VMEM((4, 8, LANES), F32),
            pltpu.VMEM((4, 8, LANES), F32),
            pltpu.VMEM((2, 8, LANES), F32),
            pltpu.VMEM((2, 8, LANES), F32),
            pltpu.VMEM((4, 8, LANES), F32),
            pltpu.SemaphoreType.DMA((18,)),
            pltpu.SemaphoreType.DMA((4,)),
            pltpu.SemaphoreType.DMA((4,)),
        ],
        compiler_params=pltpu.CompilerParams(
            collective_id=0, has_side_effects=True, vmem_limit_bytes=VMEM
        ),
    )(*args)
    dof_out, height_out, momentum_out = pl.pallas_call(
        functools.partial(grid_kernel, n_dom, n_tile),
        out_shape=(
            jax.ShapeDtypeStruct((Q, B, E), F32),
            jax.ShapeDtypeStruct(height.shape, F32),
            jax.ShapeDtypeStruct(momentum.shape, F32),
        ),
        in_specs=[vmem] * 3,
        out_specs=(far,) * 3,
        scratch_shapes=[
            pltpu.VMEM((2, 5, ROWS, LANES), F32),
            pltpu.VMEM((5, ROWS, LANES), F32),
            pltpu.VMEM((2, 4, 64, LANES), F32),
            pltpu.SemaphoreType.DMA((3,)),
        ],
        compiler_params=pltpu.CompilerParams(vmem_limit_bytes=16 << 20),
    )(dof_new, flow, level)
    return jnp.transpose(dof_out, (1, 0, 2)), height_out, momentum_out


def solution(mesh):
    both = ("dom", "tile")
    return jax.shard_map(
        shards,
        mesh=mesh,
        in_specs=(
            P(None, None, both),
            P(both),
            P(both),
            P(both),
            P(None, None, both),
            P(None, None, both),
            P(None, both),
            P(),
            P(),
            P(),
            P(None, both),
            P(both, None),
            P(both),
            P(both, None),
            P(both, None),
            P("dom", "tile"),
            P(None, "dom", "tile"),
            P("dom", "tile"),
        ),
        out_specs=(P(None, None, both), P("dom", "tile"), P(None, "dom", "tile")),
        check_vma=False,
    )
```
